128 devices in a mesh: dp: 8 (over y_lo, z), tensor: 16 (over y_hi, x, core).
Axes of the slice: x: 4, y: 4 (y_hi: 2, y_lo: 2; y = y_hi * 2 + y_lo), z: 4, core: 2. Of those that a mesh axis runs over, the one named last changes fastest.
Arguments:
- tokens: bfloat16 [2048, 4096], P('dp', 'tensor'), may hold values from -0.25 to 0.25
- small_weights: bfloat16 [2, 3328, 8960], P(None, ('dp', 'tensor')), may hold values from -6 to 6
- ffn_growth: bfloat16 [11008, 8960], P('tensor'), may hold values from -0.0625 to 0.0625
- width_growth: bfloat16 [4096, 3328], P('dp'), may hold values from -0.109375 to 0.109375
Outputs:
- grown_weights: bfloat16 [2, 4096, 11008], P(None, 'dp', 'tensor')
- hidden: bfloat16 [2048, 11008], P('dp', 'tensor')
The draws below stay inside these ranges and needn't reach their ends.
All inputs are finite; a program needn't handle non-finite values.
Results may differ from the reference program's by a relative error of at most 0.0071.
Values may be sent and summed in bfloat16 or wider, within the bound.
A program may use at most 128 MiB of HBM per device.

```python
import jax
import jax.numpy as jnp
from jax import lax

DS = 3328
FS = 8960
DL = 4096
FL = 11008
TOKENS = 2048


def level_of(own_key, extent, cuts, smallest, largest):
    factor_of = 1.0
    for dim, shards_of in cuts:
        draws = jax.random.uniform(jax.random.fold_in(jax.random.fold_in(own_key, 6), dim), (shards_of,), jnp.float32, smallest / len(cuts), largest / len(cuts))
        factor_of = factor_of * jnp.repeat(jnp.exp(draws), extent[dim] // shards_of).reshape((-1,) + (1,) * (len(extent) - 1 - dim))
    return factor_of


def noise(rng, dims, width, most, shards=(), dtype=jnp.bfloat16):
    array = width * jax.random.normal(rng, dims, jnp.float32)
    if shards:
        array = array * level_of(rng, dims, shards, -0.22, 0.18)
    return jnp.clip(array, -most, most).astype(dtype)


def setup_inputs(seed: int = 0) -> dict:
    arg_keys = jax.random.split(jax.random.key(seed), 5)
    tokens = noise(arg_keys[0], (TOKENS, DL), (DL ** -0.5), 0.25, ((0, 8), (1, 16)))
    small_weights = noise(arg_keys[1], (2, DS, FS), 1.0, 6.0, ((1, 128),))
    ffn_growth = noise(arg_keys[2], (FL, FS), FS ** -0.5, 0.0625, ((0, 16),))
    width_growth = noise(arg_keys[3], (DL, DS), DS ** -0.5, 0.109375, ((0, 8),))
    return dict(tokens=tokens, small_weights=small_weights, ffn_growth=ffn_growth, width_growth=width_growth)


def reference(tokens, small_weights, ffn_growth, width_growth):
    def grow_one(single):
        panels = jnp.dot(single, ffn_growth.T, preferred_element_type=jnp.float32).astype(jnp.bfloat16)
        return jnp.dot(width_growth, panels, preferred_element_type=jnp.float32).astype(jnp.bfloat16)

    grown_weights = lax.map(grow_one, small_weights)
    pre_gate = jnp.dot(tokens, grown_weights[0], preferred_element_type=jnp.float32)
    pre_up = jnp.dot(tokens, grown_weights[1], preferred_element_type=jnp.float32)
    hidden = (jax.nn.silu(pre_gate) * pre_up).astype(jnp.bfloat16)
    return grown_weights, hidden
```

```python
import jax
import jax.numpy as jnp
from jax import lax
from jax.sharding import PartitionSpec as P


def on_device(tokens, small_weights, ffn_growth, width_growth):
    n_t = lax.axis_size("tensor")
    t = lax.axis_index("tensor")
    ds = width_growth.shape[1]
    xw = ds // n_t
    gathered = lax.all_gather(tokens, "tensor", axis=1, tiled=True)
    w_cols = lax.dynamic_slice_in_dim(width_growth, t * xw, xw, axis=1)
    w_cols = lax.all_gather(w_cols, "dp", axis=0, tiled=True)
    tw_part = jnp.dot(gathered, w_cols, preferred_element_type=jnp.float32)
    tw_t = lax.all_gather(tw_part.astype(jnp.bfloat16).T, "tensor", axis=0, tiled=True)
    panels = jnp.einsum(
        "msf,cf->msc",
        lax.all_gather(small_weights, "tensor", axis=1, tiled=True),
        ffn_growth,
        preferred_element_type=jnp.float32,
    ).astype(jnp.bfloat16)
    all_panels = lax.all_gather(panels, "dp", axis=1, tiled=True)
    summed = jnp.einsum(
        "rs,msc->mrc",
        width_growth,
        all_panels,
        preferred_element_type=jnp.float32,
    )
    grown_weights = summed.astype(jnp.bfloat16)
    pre_values = jnp.einsum(
        "st,msc->tmc",
        tw_t,
        all_panels,
        preferred_element_type=jnp.float32,
    )
    hidden = (jax.nn.silu(pre_values[:, 0, :]) * pre_values[:, 1, :]).astype(jnp.bfloat16)
    return (grown_weights, hidden)


def solution(mesh):
    placed = (P("dp", "tensor"), P(None, ("dp", "tensor"), None), P("tensor", None), P("dp", None))
    return jax.shard_map(
        on_device,
        mesh=mesh,
        in_specs=placed,
        out_specs=(P(None, "dp", "tensor"), P("dp", "tensor")),
        check_vma=False,
    )
```

```python
import functools

import jax
import jax.numpy as jnp
from jax import lax
from jax.experimental import pallas as pl
from jax.experimental.pallas import tpu as pltpu
from jax.sharding import PartitionSpec as P

MESH = pl.DeviceIdType.MESH


def _ring_pos(d):
    h = d // 4
    return h * 7 + (1 - 2 * h) * (d % 4)


def _ring_dev(p):
    h = p // 4
    return h * 4 + h * 3 + (1 - 2 * h) * (p % 4)


def _dp_ring_kernel(n, p_ref, w3_ref, grown_ref, pall_ref, recv, acc, ssem, rsem, lsem, osem):
    t = lax.axis_index("tensor")
    d = lax.axis_index("dp")
    pos = _ring_pos(d)
    right = _ring_dev((pos + 1) % n)
    left = _ring_dev((pos + n - 1) % n)

    barrier = pltpu.get_barrier_semaphore()
    for nb in (left, right):
        pl.semaphore_signal(barrier, inc=1, device_id=(nb, t), device_id_type=MESH)
    pl.semaphore_wait(barrier, 2)

    own = []
    for m in range(2):
        c = pltpu.make_async_copy(p_ref.at[m], recv.at[m, d], osem.at[m])
        c.start()
        own.append(c)
    for c in own:
        c.wait()
    for m in range(2):
        pltpu.make_async_copy(recv.at[m, d], pall_ref.at[m, d], lsem.at[m, d]).start()

    def step(k, carry):
        o0 = _ring_dev((pos - k + n) % n)
        o1 = _ring_dev((pos + k) % n)
        c0 = pltpu.make_async_remote_copy(
            src_ref=recv.at[0, o0], dst_ref=recv.at[0, o0],
            send_sem=ssem.at[0, k], recv_sem=rsem.at[0, k],
            device_id=(right, t), device_id_type=MESH)
        c1 = pltpu.make_async_remote_copy(
            src_ref=recv.at[1, o1], dst_ref=recv.at[1, o1],
            send_sem=ssem.at[1, k], recv_sem=rsem.at[1, k],
            device_id=(left, t), device_id_type=MESH)
        c0.start()
        c1.start()
        g0 = jnp.dot(w3_ref[o0], recv[0, o0], preferred_element_type=jnp.float32)
        g1 = jnp.dot(w3_ref[o1], recv[1, o1], preferred_element_type=jnp.float32)

        @pl.when(k == 0)
        def _():
            acc[0] = g0
            acc[1] = g1

        @pl.when(k > 0)
        def _():
            acc[0] += g0
            acc[1] += g1

        c0.wait()
        c1.wait()
        n0 = _ring_dev((pos - k - 1 + n) % n)
        n1 = _ring_dev((pos + k + 1) % n)
        pltpu.make_async_copy(recv.at[0, n0], pall_ref.at[0, n0], lsem.at[0, n0]).start()
        pltpu.make_async_copy(recv.at[1, n1], pall_ref.at[1, n1], lsem.at[1, n1]).start()
        return carry

    lax.fori_loop(0, n - 1, step, 0)
    o0 = _ring_dev((pos - (n - 1) + n) % n)
    o1 = _ring_dev((pos + n - 1) % n)
    acc[0] += jnp.dot(w3_ref[o0], recv[0, o0], preferred_element_type=jnp.float32)
    acc[1] += jnp.dot(w3_ref[o1], recv[1, o1], preferred_element_type=jnp.float32)
    grown_ref[...] = acc[...].astype(grown_ref.dtype)
    for m in range(2):
        for o in range(n):
            pltpu.make_async_copy(recv.at[m, o], pall_ref.at[m, o], lsem.at[m, o]).wait()


def _dp_ring(panels, w3):
    n, rows, blk = w3.shape
    _, _, cols = panels.shape
    flops = 2 * 2 * rows * blk * cols * n
    return pl.pallas_call(
        functools.partial(_dp_ring_kernel, n),
        out_shape=(
            jax.ShapeDtypeStruct((2, rows, cols), jnp.bfloat16),
            jax.ShapeDtypeStruct((2, n, blk, cols), jnp.bfloat16),
        ),
        in_specs=[pl.BlockSpec(memory_space=pltpu.VMEM)] * 2,
        out_specs=(pl.BlockSpec(memory_space=pltpu.VMEM), pl.BlockSpec(memory_space=pl.ANY)),
        scratch_shapes=[
            pltpu.VMEM((2, n, blk, cols), jnp.bfloat16),
            pltpu.VMEM((2, rows, cols), jnp.float32),
            pltpu.SemaphoreType.DMA((2, n - 1)),
            pltpu.SemaphoreType.DMA((2, n - 1)),
            pltpu.SemaphoreType.DMA((2, n)),
            pltpu.SemaphoreType.DMA((2,)),
        ],
        compiler_params=pltpu.CompilerParams(
            collective_id=0, has_side_effects=True, vmem_limit_bytes=56 * 1024 * 1024),
        cost_estimate=pl.CostEstimate(
            flops=flops, transcendentals=0, bytes_accessed=2 * 2 * n * blk * cols * 2),
    )(panels, w3)


def on_device(tokens, small_weights, ffn_growth, width_growth):
    n_t = lax.axis_size("tensor")
    n_d = lax.axis_size("dp")
    t = lax.axis_index("tensor")
    rows, ds = width_growth.shape
    xw = ds // n_t
    blk = ds // n_d
    gathered = lax.all_gather(tokens, "tensor", axis=1, tiled=True)
    w_cols = lax.dynamic_slice_in_dim(width_growth, t * xw, xw, axis=1)
    w_cols = lax.all_gather(w_cols, "dp", axis=0, tiled=True)
    tw_part = jnp.dot(gathered, w_cols, preferred_element_type=jnp.float32)
    tw_t = lax.all_gather(tw_part.astype(jnp.bfloat16).T, "tensor", axis=0, tiled=True)
    panels = jnp.einsum(
        "msf,cf->msc",
        lax.all_gather(small_weights, "tensor", axis=1, tiled=True),
        ffn_growth,
        preferred_element_type=jnp.float32,
    ).astype(jnp.bfloat16)
    w3 = width_growth.reshape(rows, n_d, blk).transpose(1, 0, 2)
    grown_weights, pall = _dp_ring(panels, w3)
    all_panels = pall.reshape(2, ds, panels.shape[2])
    pre_values = jnp.einsum(
        "st,msc->tmc",
        tw_t,
        all_panels,
        preferred_element_type=jnp.float32,
    )
    hidden = (jax.nn.silu(pre_values[:, 0, :]) * pre_values[:, 1, :]).astype(jnp.bfloat16)
    return (grown_weights, hidden)


def solution(mesh):
    placed = (P("dp", "tensor"), P(None, ("dp", "tensor"), None), P("tensor", None), P("dp", None))
    return jax.shard_map(
        on_device,
        mesh=mesh,
        in_specs=placed,
        out_specs=(P(None, "dp", "tensor"), P("dp", "tensor")),
        check_vma=False,
    )
```

```python
import functools

import jax
import jax.numpy as jnp
from jax import lax
from jax.experimental import pallas as pl
from jax.experimental.pallas import tpu as pltpu
from jax.sharding import PartitionSpec as P

MESH = pl.DeviceIdType.MESH


def _ring_pos(d):
    h = d // 4
    return h * 7 + (1 - 2 * h) * (d % 4)


def _ring_dev(p):
    h = p // 4
    return h * 4 + h * 3 + (1 - 2 * h) * (p % 4)


def _dp_ring_kernel(n, p_ref, w3_ref, grown_ref, pall_ref, recv, acc, ssem, rsem, lsem, osem):
    t = lax.axis_index("tensor")
    d = lax.axis_index("dp")
    pos = _ring_pos(d)
    right = _ring_dev((pos + 1) % n)
    left = _ring_dev((pos + n - 1) % n)

    barrier = pltpu.get_barrier_semaphore()
    for nb in (left, right):
        pl.semaphore_signal(barrier, inc=1, device_id=(nb, t), device_id_type=MESH)
    pl.semaphore_wait(barrier, 2)

    own = []
    for m in range(2):
        c = pltpu.make_async_copy(p_ref.at[m], recv.at[m, d], osem.at[m])
        c.start()
        own.append(c)
    for c in own:
        c.wait()
    for m in range(2):
        pltpu.make_async_copy(recv.at[m, d], pall_ref.at[m, d], lsem.at[m, d]).start()

    def step(k, carry):
        o0 = _ring_dev((pos - k + n) % n)
        o1 = _ring_dev((pos + k) % n)
        c0 = pltpu.make_async_remote_copy(
            src_ref=recv.at[0, o0], dst_ref=recv.at[0, o0],
            send_sem=ssem.at[0, k], recv_sem=rsem.at[0, k],
            device_id=(right, t), device_id_type=MESH)
        c1 = pltpu.make_async_remote_copy(
            src_ref=recv.at[1, o1], dst_ref=recv.at[1, o1],
            send_sem=ssem.at[1, k], recv_sem=rsem.at[1, k],
            device_id=(left, t), device_id_type=MESH)
        c0.start()
        c1.start()
        g0 = jnp.dot(w3_ref[o0], recv[0, o0], preferred_element_type=jnp.float32)
        g1 = jnp.dot(w3_ref[o1], recv[1, o1], preferred_element_type=jnp.float32)

        @pl.when(k == 0)
        def _():
            acc[0] = g0
            acc[1] = g1

        @pl.when(k > 0)
        def _():
            acc[0] += g0
            acc[1] += g1

        c0.wait()
        c1.wait()
        n0 = _ring_dev((pos - k - 1 + n) % n)
        n1 = _ring_dev((pos + k + 1) % n)
        pltpu.make_async_copy(recv.at[0, n0], pall_ref.at[0, n0], lsem.at[0, n0]).start()
        pltpu.make_async_copy(recv.at[1, n1], pall_ref.at[1, n1], lsem.at[1, n1]).start()
        return carry

    lax.fori_loop(0, n - 1, step, 0)
    o0 = _ring_dev((pos - (n - 1) + n) % n)
    o1 = _ring_dev((pos + n - 1) % n)
    acc[0] += jnp.dot(w3_ref[o0], recv[0, o0], preferred_element_type=jnp.float32)
    acc[1] += jnp.dot(w3_ref[o1], recv[1, o1], preferred_element_type=jnp.float32)
    grown_ref[...] = acc[...].astype(grown_ref.dtype)
    for m in range(2):
        for o in range(n):
            pltpu.make_async_copy(recv.at[m, o], pall_ref.at[m, o], lsem.at[m, o]).wait()


def _dp_ring(panels, w3):
    n, rows, blk = w3.shape
    _, _, cols = panels.shape
    flops = 2 * 2 * rows * blk * cols * n
    return pl.pallas_call(
        functools.partial(_dp_ring_kernel, n),
        out_shape=(
            jax.ShapeDtypeStruct((2, rows, cols), jnp.bfloat16),
            jax.ShapeDtypeStruct((2, n, blk, cols), jnp.bfloat16),
        ),
        in_specs=[pl.BlockSpec(memory_space=pltpu.VMEM)] * 2,
        out_specs=(pl.BlockSpec(memory_space=pltpu.VMEM), pl.BlockSpec(memory_space=pl.ANY)),
        scratch_shapes=[
            pltpu.VMEM((2, n, blk, cols), jnp.bfloat16),
            pltpu.VMEM((2, rows, cols), jnp.float32),
            pltpu.SemaphoreType.DMA((2, n - 1)),
            pltpu.SemaphoreType.DMA((2, n - 1)),
            pltpu.SemaphoreType.DMA((2, n)),
            pltpu.SemaphoreType.DMA((2,)),
        ],
        compiler_params=pltpu.CompilerParams(
            collective_id=0, has_side_effects=True, vmem_limit_bytes=56 * 1024 * 1024),
        cost_estimate=pl.CostEstimate(
            flops=flops, transcendentals=0, bytes_accessed=2 * 2 * n * blk * cols * 2),
    )(panels, w3)


def _tw_kernel(nt, nd, tok_ref, wcol_ref, out_ref, tbuf, wbuf, xbuf,
               ts_sem, tr_sem, ws_sem, wr_sem, xs_sem, xr_sem, l_sem):
    t = lax.axis_index("tensor")
    d = lax.axis_index("dp")
    rb = tok_ref.shape[1]

    barrier = pltpu.get_barrier_semaphore()

    def greet_t(j, c):
        pl.semaphore_signal(barrier, inc=1, device_id=(d, (t + j) % nt), device_id_type=MESH)
        return c

    def greet_d(j, c):
        pl.semaphore_signal(barrier, inc=1, device_id=((d + j) % nd, t), device_id_type=MESH)
        return c

    lax.fori_loop(1, nt, greet_t, 0)
    lax.fori_loop(1, nd, greet_d, 0)
    pl.semaphore_wait(barrier, nt - 1 + nd - 1)

    c0 = pltpu.make_async_copy(tok_ref, tbuf.at[t], l_sem.at[0])
    c1 = pltpu.make_async_copy(wcol_ref, wbuf.at[d], l_sem.at[1])
    c0.start()
    c1.start()

    def t_copy(p):
        return pltpu.make_async_remote_copy(
            src_ref=tok_ref, dst_ref=tbuf.at[t], send_sem=ts_sem.at[p], recv_sem=tr_sem.at[t],
            device_id=(d, p), device_id_type=MESH)

    def t_recv(p):
        return pltpu.make_async_remote_copy(
            src_ref=tok_ref, dst_ref=tbuf.at[p], send_sem=ts_sem.at[p], recv_sem=tr_sem.at[p],
            device_id=(d, p), device_id_type=MESH)

    def w_copy(p):
        return pltpu.make_async_remote_copy(
            src_ref=wcol_ref, dst_ref=wbuf.at[d], send_sem=ws_sem.at[p], recv_sem=wr_sem.at[d],
            device_id=(p, t), device_id_type=MESH)

    def w_recv(p):
        return pltpu.make_async_remote_copy(
            src_ref=wcol_ref, dst_ref=wbuf.at[p], send_sem=ws_sem.at[p], recv_sem=wr_sem.at[p],
            device_id=(p, t), device_id_type=MESH)

    def send_t(j, c):
        t_copy((t + j) % nt).start()
        return c

    def send_d(j, c):
        w_copy((d + j) % nd).start()
        return c

    lax.fori_loop(1, nt, send_t, 0)
    lax.fori_loop(1, nd, send_d, 0)

    def wait_t(j, c):
        p = (t + j) % nt
        t_copy(p).wait_send()
        t_recv(p).wait_recv()
        return c

    def wait_d(j, c):
        p = (d + j) % nd
        w_copy(p).wait_send()
        w_recv(p).wait_recv()
        return c

    lax.fori_loop(1, nt, wait_t, 0)
    lax.fori_loop(1, nd, wait_d, 0)
    c0.wait()
    c1.wait()

    per = nt // nd
    acc = None
    for q in range(nt):
        part = jnp.dot(tbuf[q], wbuf[q // per, pl.ds((q % per) * rb, rb), :],
                       preferred_element_type=jnp.float32)
        acc = part if acc is None else acc + part
    xbuf[t] = acc.astype(xbuf.dtype)

    def x_copy(p):
        return pltpu.make_async_remote_copy(
            src_ref=xbuf.at[t], dst_ref=xbuf.at[t], send_sem=xs_sem.at[p], recv_sem=xr_sem.at[t],
            device_id=(d, p), device_id_type=MESH)

    def x_recv(p):
        return pltpu.make_async_remote_copy(
            src_ref=xbuf.at[p], dst_ref=xbuf.at[p], send_sem=xs_sem.at[p], recv_sem=xr_sem.at[p],
            device_id=(d, p), device_id_type=MESH)

    def send_x(j, c):
        x_copy((t + j) % nt).start()
        return c

    def wait_x(j, c):
        p = (t + j) % nt
        x_copy(p).wait_send()
        x_recv(p).wait_recv()
        return c

    lax.fori_loop(1, nt, send_x, 0)
    lax.fori_loop(1, nt, wait_x, 0)
    out_ref[...] = xbuf[...]


def _tw(tokens, wcol, nt, nd):
    tok, rb = tokens.shape
    rows, xw = wcol.shape
    return pl.pallas_call(
        functools.partial(_tw_kernel, nt, nd),
        out_shape=jax.ShapeDtypeStruct((nt, tok, xw), jnp.bfloat16),
        in_specs=[pl.BlockSpec(memory_space=pltpu.VMEM)] * 2,
        out_specs=pl.BlockSpec(memory_space=pltpu.VMEM),
        scratch_shapes=[
            pltpu.VMEM((nt, tok, rb), jnp.bfloat16),
            pltpu.VMEM((nd, rows, xw), jnp.bfloat16),
            pltpu.VMEM((nt, tok, xw), jnp.bfloat16),
            pltpu.SemaphoreType.DMA((nt,)),
            pltpu.SemaphoreType.DMA((nt,)),
            pltpu.SemaphoreType.DMA((nd,)),
            pltpu.SemaphoreType.DMA((nd,)),
            pltpu.SemaphoreType.DMA((nt,)),
            pltpu.SemaphoreType.DMA((nt,)),
            pltpu.SemaphoreType.DMA((2,)),
        ],
        compiler_params=pltpu.CompilerParams(
            collective_id=1, has_side_effects=True, vmem_limit_bytes=32 * 1024 * 1024),
        cost_estimate=pl.CostEstimate(
            flops=2 * tok * rb * nt * xw, transcendentals=0,
            bytes_accessed=(nt * tok * rb + nd * rows * xw + 2 * nt * tok * xw) * 2),
    )(tokens, wcol)


def on_device(tokens, small_weights, ffn_growth, width_growth):
    n_t = lax.axis_size("tensor")
    n_d = lax.axis_size("dp")
    t = lax.axis_index("tensor")
    rows, ds = width_growth.shape
    xw = ds // n_t
    blk = ds // n_d
    w_cols = lax.dynamic_slice_in_dim(width_growth, t * xw, xw, axis=1)
    tw_blocks = _tw(tokens, w_cols, n_t, n_d)
    panels = jnp.einsum(
        "msf,cf->msc",
        lax.all_gather(small_weights, "tensor", axis=1, tiled=True),
        ffn_growth,
        preferred_element_type=jnp.float32,
    ).astype(jnp.bfloat16)
    w3 = width_growth.reshape(rows, n_d, blk).transpose(1, 0, 2)
    grown_weights, pall = _dp_ring(panels, w3)
    all_panels = pall.reshape(2, n_t, xw, panels.shape[2])
    pre_values = jnp.einsum(
        "kts,mksc->tmc",
        tw_blocks,
        all_panels,
        preferred_element_type=jnp.float32,
    )
    hidden = (jax.nn.silu(pre_values[:, 0, :]) * pre_values[:, 1, :]).astype(jnp.bfloat16)
    return (grown_weights, hidden)


def solution(mesh):
    placed = (P("dp", "tensor"), P(None, ("dp", "tensor"), None), P("tensor", None), P("dp", None))
    return jax.shard_map(
        on_device,
        mesh=mesh,
        in_specs=placed,
        out_specs=(P(None, "dp", "tensor"), P("dp", "tensor")),
        check_vma=False,
    )
```

```python
import functools

import jax
import jax.numpy as jnp
from jax import lax
from jax.experimental import pallas as pl
from jax.experimental.pallas import tpu as pltpu
from jax.sharding import PartitionSpec as P

MESH = pl.DeviceIdType.MESH


def _ring_pos(d):
    h = d // 4
    return h * 7 + (1 - 2 * h) * (d % 4)


def _ring_dev(p):
    h = p // 4
    return h * 4 + h * 3 + (1 - 2 * h) * (p % 4)


def _layer_kernel(n, nt, p_ref, w3_ref, tok_ref, wcol_ref, grown_ref, hid_ref,
                  recv, acc, tbuf, wbuf, xbuf, ssem, rsem,
                  ts_sem, tr_sem, ws_sem, wr_sem, xs_sem, xr_sem, osem):
    t = lax.axis_index("tensor")
    d = lax.axis_index("dp")
    pos = _ring_pos(d)
    right = _ring_dev((pos + 1) % n)
    left = _ring_dev((pos + n - 1) % n)
    rb = tok_ref.shape[1]
    xw = wcol_ref.shape[1]
    blk = p_ref.shape[1]

    barrier = pltpu.get_barrier_semaphore()

    def greet_t(j, c):
        pl.semaphore_signal(barrier, inc=1, device_id=(d, (t + j) % nt), device_id_type=MESH)
        return c

    def greet_d(j, c):
        pl.semaphore_signal(barrier, inc=1, device_id=((d + j) % n, t), device_id_type=MESH)
        return c

    lax.fori_loop(1, nt, greet_t, 0)
    lax.fori_loop(1, n, greet_d, 0)
    pl.semaphore_wait(barrier, nt - 1 + n - 1)

    own = [
        pltpu.make_async_copy(p_ref.at[0], recv.at[0, d], osem.at[0]),
        pltpu.make_async_copy(p_ref.at[1], recv.at[1, d], osem.at[1]),
        pltpu.make_async_copy(tok_ref, tbuf.at[t], osem.at[2]),
        pltpu.make_async_copy(wcol_ref, wbuf.at[d], osem.at[3]),
    ]
    for c in own:
        c.start()

    def t_copy(p):
        return pltpu.make_async_remote_copy(
            src_ref=tok_ref, dst_ref=tbuf.at[t], send_sem=ts_sem.at[p], recv_sem=tr_sem.at[t],
            device_id=(d, p), device_id_type=MESH)

    def t_recv(p):
        return pltpu.make_async_remote_copy(
            src_ref=tok_ref, dst_ref=tbuf.at[p], send_sem=ts_sem.at[p], recv_sem=tr_sem.at[p],
            device_id=(d, p), device_id_type=MESH)

    def w_copy(p):
        return pltpu.make_async_remote_copy(
            src_ref=wcol_ref, dst_ref=wbuf.at[d], send_sem=ws_sem.at[p], recv_sem=wr_sem.at[d],
            device_id=(p, t), device_id_type=MESH)

    def w_recv(p):
        return pltpu.make_async_remote_copy(
            src_ref=wcol_ref, dst_ref=wbuf.at[p], send_sem=ws_sem.at[p], recv_sem=wr_sem.at[p],
            device_id=(p, t), device_id_type=MESH)

    def x_copy(p):
        return pltpu.make_async_remote_copy(
            src_ref=xbuf.at[t], dst_ref=xbuf.at[t], send_sem=xs_sem.at[p], recv_sem=xr_sem.at[t],
            device_id=(d, p), device_id_type=MESH)

    def x_recv(p):
        return pltpu.make_async_remote_copy(
            src_ref=xbuf.at[p], dst_ref=xbuf.at[p], send_sem=xs_sem.at[p], recv_sem=xr_sem.at[p],
            device_id=(d, p), device_id_type=MESH)

    def send_t(j, c):
        t_copy((t + j) % nt).start()
        return c

    def send_d(j, c):
        w_copy((d + j) % n).start()
        return c

    lax.fori_loop(1, nt, send_t, 0)
    lax.fori_loop(1, n, send_d, 0)
    for c in own:
        c.wait()

    def step(k, carry):
        o0 = _ring_dev((pos - k + n) % n)
        o1 = _ring_dev((pos + k) % n)
        c0 = pltpu.make_async_remote_copy(
            src_ref=recv.at[0, o0], dst_ref=recv.at[0, o0],
            send_sem=ssem.at[0, k], recv_sem=rsem.at[0, k],
            device_id=(right, t), device_id_type=MESH)
        c1 = pltpu.make_async_remote_copy(
            src_ref=recv.at[1, o1], dst_ref=recv.at[1, o1],
            send_sem=ssem.at[1, k], recv_sem=rsem.at[1, k],
            device_id=(left, t), device_id_type=MESH)
        c0.start()
        c1.start()
        g0 = jnp.dot(w3_ref[o0], recv[0, o0], preferred_element_type=jnp.float32)
        g1 = jnp.dot(w3_ref[o1], recv[1, o1], preferred_element_type=jnp.float32)

        @pl.when(k == 0)
        def _():
            acc[0] = g0
            acc[1] = g1

        @pl.when(k > 0)
        def _():
            acc[0] += g0
            acc[1] += g1

        c0.wait()
        c1.wait()
        return carry

    lax.fori_loop(0, 1, step, 0)

    def wait_t(j, c):
        p = (t + j) % nt
        t_copy(p).wait_send()
        t_recv(p).wait_recv()
        return c

    def wait_d(j, c):
        p = (d + j) % n
        w_copy(p).wait_send()
        w_recv(p).wait_recv()
        return c

    lax.fori_loop(1, nt, wait_t, 0)
    lax.fori_loop(1, n, wait_d, 0)
    per = nt // n
    tw = None
    for q in range(nt):
        part = jnp.dot(tbuf[q], wbuf[q // per, pl.ds((q % per) * rb, rb), :],
                       preferred_element_type=jnp.float32)
        tw = part if tw is None else tw + part
    xbuf[t] = tw.astype(xbuf.dtype)

    def send_x(j, c):
        x_copy((t + j) % nt).start()
        return c

    lax.fori_loop(1, nt, send_x, 0)
    lax.fori_loop(1, n - 1, step, 0)
    o0 = _ring_dev((pos - (n - 1) + n) % n)
    o1 = _ring_dev((pos + n - 1) % n)
    acc[0] += jnp.dot(w3_ref[o0], recv[0, o0], preferred_element_type=jnp.float32)
    acc[1] += jnp.dot(w3_ref[o1], recv[1, o1], preferred_element_type=jnp.float32)
    grown_ref[...] = acc[...].astype(grown_ref.dtype)

    def wait_x(j, c):
        p = (t + j) % nt
        x_copy(p).wait_send()
        x_recv(p).wait_recv()
        return c

    lax.fori_loop(1, nt, wait_x, 0)
    half = blk // xw
    pre = []
    for m in range(2):
        s = None
        for q in range(nt):
            part = jnp.dot(xbuf[q], recv[m, q // half, pl.ds((q % half) * xw, xw), :],
                           preferred_element_type=jnp.float32)
            s = part if s is None else s + part
        pre.append(s)
    gate = pre[0]
    hid_ref[...] = (gate / (1.0 + jnp.exp(-gate)) * pre[1]).astype(hid_ref.dtype)


def _layer(panels, w3, tokens, wcol, nt):
    n, rows, blk = w3.shape
    _, _, cols = panels.shape
    tok, rb = tokens.shape
    xw = wcol.shape[1]
    flops = 2 * 2 * rows * blk * cols * n + 2 * tok * rb * nt * xw + 2 * 2 * tok * xw * nt * cols
    return pl.pallas_call(
        functools.partial(_layer_kernel, n, nt),
        out_shape=(
            jax.ShapeDtypeStruct((2, rows, cols), jnp.bfloat16),
            jax.ShapeDtypeStruct((tok, cols), jnp.bfloat16),
        ),
        in_specs=[pl.BlockSpec(memory_space=pltpu.VMEM)] * 4,
        out_specs=(pl.BlockSpec(memory_space=pltpu.VMEM), pl.BlockSpec(memory_space=pltpu.VMEM)),
        scratch_shapes=[
            pltpu.VMEM((2, n, blk, cols), jnp.bfloat16),
            pltpu.VMEM((2, rows, cols), jnp.float32),
            pltpu.VMEM((nt, tok, rb), jnp.bfloat16),
            pltpu.VMEM((n, rows, xw), jnp.bfloat16),
            pltpu.VMEM((nt, tok, xw), jnp.bfloat16),
            pltpu.SemaphoreType.DMA((2, n - 1)),
            pltpu.SemaphoreType.DMA((2, n - 1)),
            pltpu.SemaphoreType.DMA((nt,)),
            pltpu.SemaphoreType.DMA((nt,)),
            pltpu.SemaphoreType.DMA((n,)),
            pltpu.SemaphoreType.DMA((n,)),
            pltpu.SemaphoreType.DMA((nt,)),
            pltpu.SemaphoreType.DMA((nt,)),
            pltpu.SemaphoreType.DMA((4,)),
        ],
        compiler_params=pltpu.CompilerParams(
            collective_id=0, has_side_effects=True, vmem_limit_bytes=60 * 1024 * 1024),
        cost_estimate=pl.CostEstimate(
            flops=flops, transcendentals=tok * cols,
            bytes_accessed=2 * 2 * n * blk * cols * 2),
    )(panels, w3, tokens, wcol)


def on_device(tokens, small_weights, ffn_growth, width_growth):
    n_t = lax.axis_size("tensor")
    n_d = lax.axis_size("dp")
    t = lax.axis_index("tensor")
    rows, ds = width_growth.shape
    xw = ds // n_t
    blk = ds // n_d
    w_cols = lax.dynamic_slice_in_dim(width_growth, t * xw, xw, axis=1)
    panels = jnp.einsum(
        "msf,cf->msc",
        lax.all_gather(small_weights, "tensor", axis=1, tiled=True),
        ffn_growth,
        preferred_element_type=jnp.float32,
    ).astype(jnp.bfloat16)
    w3 = width_growth.reshape(rows, n_d, blk).transpose(1, 0, 2)
    grown_weights, hidden = _layer(panels, w3, tokens, w_cols, n_t)
    return (grown_weights, hidden)


def solution(mesh):
    placed = (P("dp", "tensor"), P(None, ("dp", "tensor"), None), P("tensor", None), P("dp", None))
    return jax.shard_map(
        on_device,
        mesh=mesh,
        in_specs=placed,
        out_specs=(P(None, "dp", "tensor"), P("dp", "tensor")),
        check_vma=False,
    )
```

```python
import functools

import jax
import jax.numpy as jnp
from jax import lax
from jax.experimental import pallas as pl
from jax.experimental.pallas import tpu as pltpu
from jax.sharding import PartitionSpec as P

MESH = pl.DeviceIdType.MESH


def _ring_pos(d):
    h = d // 4
    return h * 7 + (1 - 2 * h) * (d % 4)


def _ring_dev(p):
    h = p // 4
    return h * 4 + h * 3 + (1 - 2 * h) * (p % 4)


def _dp_ring_kernel(n, p_ref, w3_ref, grown_ref, pall_ref, recv, acc, ssem, rsem, lsem, osem):
    t = lax.axis_index("tensor")
    d = lax.axis_index("dp")
    pos = _ring_pos(d)
    right = _ring_dev((pos + 1) % n)
    left = _ring_dev((pos + n - 1) % n)

    barrier = pltpu.get_barrier_semaphore()
    for nb in (left, right):
        pl.semaphore_signal(barrier, inc=1, device_id=(nb, t), device_id_type=MESH)
    pl.semaphore_wait(barrier, 2)

    own = []
    for m in range(2):
        c = pltpu.make_async_copy(p_ref.at[m], recv.at[m, d], osem.at[m])
        c.start()
        own.append(c)
    for c in own:
        c.wait()
    for m in range(2):
        pltpu.make_async_copy(recv.at[m, d], pall_ref.at[d, m], lsem.at[m, d]).start()

    def step(k, carry):
        o0 = _ring_dev((pos - k + n) % n)
        o1 = _ring_dev((pos + k) % n)
        c0 = pltpu.make_async_remote_copy(
            src_ref=recv.at[0, o0], dst_ref=recv.at[0, o0],
            send_sem=ssem.at[0, k], recv_sem=rsem.at[0, k],
            device_id=(right, t), device_id_type=MESH)
        c1 = pltpu.make_async_remote_copy(
            src_ref=recv.at[1, o1], dst_ref=recv.at[1, o1],
            send_sem=ssem.at[1, k], recv_sem=rsem.at[1, k],
            device_id=(left, t), device_id_type=MESH)
        c0.start()
        c1.start()
        g0 = jnp.dot(w3_ref[o0, 0], recv[0, o0], preferred_element_type=jnp.float32)
        g1 = jnp.dot(w3_ref[o1, 1], recv[1, o1], preferred_element_type=jnp.float32)

        @pl.when(k == 0)
        def _():
            acc[...] = g0 + g1

        @pl.when(k > 0)
        def _():
            acc[...] += g0 + g1

        c0.wait()
        c1.wait()
        n0 = _ring_dev((pos - k - 1 + n) % n)
        n1 = _ring_dev((pos + k + 1) % n)
        pltpu.make_async_copy(recv.at[0, n0], pall_ref.at[n0, 0], lsem.at[0, n0]).start()
        pltpu.make_async_copy(recv.at[1, n1], pall_ref.at[n1, 1], lsem.at[1, n1]).start()
        return carry

    lax.fori_loop(0, n - 1, step, 0)
    o0 = _ring_dev((pos - (n - 1) + n) % n)
    o1 = _ring_dev((pos + n - 1) % n)
    acc[...] += (jnp.dot(w3_ref[o0, 0], recv[0, o0], preferred_element_type=jnp.float32)
                 + jnp.dot(w3_ref[o1, 1], recv[1, o1], preferred_element_type=jnp.float32))
    grown_ref[...] = acc[...].astype(grown_ref.dtype)
    for m in range(2):
        for o in range(n):
            pltpu.make_async_copy(recv.at[m, o], pall_ref.at[o, m], lsem.at[m, o]).wait()


def _dp_ring(panels, w3h, cid):
    n, _, rows, hb = w3h.shape
    _, _, cols = panels.shape
    flops = 2 * 2 * rows * hb * cols * n
    return pl.pallas_call(
        functools.partial(_dp_ring_kernel, n),
        out_shape=(
            jax.ShapeDtypeStruct((rows, cols), jnp.bfloat16),
            jax.ShapeDtypeStruct((n, 2, hb, cols), jnp.bfloat16),
        ),
        in_specs=[pl.BlockSpec(memory_space=pltpu.VMEM)] * 2,
        out_specs=(pl.BlockSpec(memory_space=pltpu.VMEM), pl.BlockSpec(memory_space=pl.ANY)),
        scratch_shapes=[
            pltpu.VMEM((2, n, hb, cols), jnp.bfloat16),
            pltpu.VMEM((rows, cols), jnp.float32),
            pltpu.SemaphoreType.DMA((2, n - 1)),
            pltpu.SemaphoreType.DMA((2, n - 1)),
            pltpu.SemaphoreType.DMA((2, n)),
            pltpu.SemaphoreType.DMA((2,)),
        ],
        compiler_params=pltpu.CompilerParams(
            collective_id=cid, has_side_effects=True, vmem_limit_bytes=48 * 1024 * 1024),
        cost_estimate=pl.CostEstimate(
            flops=flops, transcendentals=0, bytes_accessed=2 * n * 2 * hb * cols * 2),
    )(panels, w3h)


def _tw_kernel(nt, nd, tok_ref, wcol_ref, out_ref, tbuf, wbuf, xbuf,
               ts_sem, tr_sem, ws_sem, wr_sem, xs_sem, xr_sem, l_sem):
    t = lax.axis_index("tensor")
    d = lax.axis_index("dp")
    rb = tok_ref.shape[1]

    barrier = pltpu.get_barrier_semaphore()

    def greet_t(j, c):
        pl.semaphore_signal(barrier, inc=1, device_id=(d, (t + j) % nt), device_id_type=MESH)
        return c

    def greet_d(j, c):
        pl.semaphore_signal(barrier, inc=1, device_id=((d + j) % nd, t), device_id_type=MESH)
        return c

    lax.fori_loop(1, nt, greet_t, 0)
    lax.fori_loop(1, nd, greet_d, 0)
    pl.semaphore_wait(barrier, nt - 1 + nd - 1)

    c0 = pltpu.make_async_copy(tok_ref, tbuf.at[t], l_sem.at[0])
    c1 = pltpu.make_async_copy(wcol_ref, wbuf.at[d], l_sem.at[1])
    c0.start()
    c1.start()

    def t_copy(p):
        return pltpu.make_async_remote_copy(
            src_ref=tok_ref, dst_ref=tbuf.at[t], send_sem=ts_sem.at[p], recv_sem=tr_sem.at[t],
            device_id=(d, p), device_id_type=MESH)

    def t_recv(p):
        return pltpu.make_async_remote_copy(
            src_ref=tok_ref, dst_ref=tbuf.at[p], send_sem=ts_sem.at[p], recv_sem=tr_sem.at[p],
            device_id=(d, p), device_id_type=MESH)

    def w_copy(p):
        return pltpu.make_async_remote_copy(
            src_ref=wcol_ref, dst_ref=wbuf.at[d], send_sem=ws_sem.at[p], recv_sem=wr_sem.at[d],
            device_id=(p, t), device_id_type=MESH)

    def w_recv(p):
        return pltpu.make_async_remote_copy(
            src_ref=wcol_ref, dst_ref=wbuf.at[p], send_sem=ws_sem.at[p], recv_sem=wr_sem.at[p],
            device_id=(p, t), device_id_type=MESH)

    def send_t(j, c):
        t_copy((t + j) % nt).start()
        return c

    def send_d(j, c):
        w_copy((d + j) % nd).start()
        return c

    lax.fori_loop(1, nt, send_t, 0)
    lax.fori_loop(1, nd, send_d, 0)

    def wait_t(j, c):
        p = (t + j) % nt
        t_copy(p).wait_send()
        t_recv(p).wait_recv()
        return c

    def wait_d(j, c):
        p = (d + j) % nd
        w_copy(p).wait_send()
        w_recv(p).wait_recv()
        return c

    lax.fori_loop(1, nt, wait_t, 0)
    lax.fori_loop(1, nd, wait_d, 0)
    c0.wait()
    c1.wait()

    per = nt // nd
    acc = None
    for q in range(nt):
        part = jnp.dot(tbuf[q], wbuf[q // per, pl.ds((q % per) * rb, rb), :],
                       preferred_element_type=jnp.float32)
        acc = part if acc is None else acc + part
    xbuf[t] = acc.astype(xbuf.dtype)

    def x_copy(p):
        return pltpu.make_async_remote_copy(
            src_ref=xbuf.at[t], dst_ref=xbuf.at[t], send_sem=xs_sem.at[p], recv_sem=xr_sem.at[t],
            device_id=(d, p), device_id_type=MESH)

    def x_recv(p):
        return pltpu.make_async_remote_copy(
            src_ref=xbuf.at[p], dst_ref=xbuf.at[p], send_sem=xs_sem.at[p], recv_sem=xr_sem.at[p],
            device_id=(d, p), device_id_type=MESH)

    def send_x(j, c):
        x_copy((t + j) % nt).start()
        return c

    def wait_x(j, c):
        p = (t + j) % nt
        x_copy(p).wait_send()
        x_recv(p).wait_recv()
        return c

    lax.fori_loop(1, nt, send_x, 0)
    lax.fori_loop(1, nt, wait_x, 0)
    out_ref[...] = xbuf[...]


def _tw(tokens, wcol, nt, nd):
    tok, rb = tokens.shape
    rows, xw = wcol.shape
    return pl.pallas_call(
        functools.partial(_tw_kernel, nt, nd),
        out_shape=jax.ShapeDtypeStruct((nt, tok, xw), jnp.bfloat16),
        in_specs=[pl.BlockSpec(memory_space=pltpu.VMEM)] * 2,
        out_specs=pl.BlockSpec(memory_space=pltpu.VMEM),
        scratch_shapes=[
            pltpu.VMEM((nt, tok, rb), jnp.bfloat16),
            pltpu.VMEM((nd, rows, xw), jnp.bfloat16),
            pltpu.VMEM((nt, tok, xw), jnp.bfloat16),
            pltpu.SemaphoreType.DMA((nt,)),
            pltpu.SemaphoreType.DMA((nt,)),
            pltpu.SemaphoreType.DMA((nd,)),
            pltpu.SemaphoreType.DMA((nd,)),
            pltpu.SemaphoreType.DMA((nt,)),
            pltpu.SemaphoreType.DMA((nt,)),
            pltpu.SemaphoreType.DMA((2,)),
        ],
        compiler_params=pltpu.CompilerParams(
            collective_id=2, has_side_effects=True, vmem_limit_bytes=32 * 1024 * 1024),
        cost_estimate=pl.CostEstimate(
            flops=2 * tok * rb * nt * xw, transcendentals=0,
            bytes_accessed=(nt * tok * rb + nd * rows * xw + 2 * nt * tok * xw) * 2 * 64),
    )(tokens, wcol)


def on_device(tokens, small_weights, ffn_growth, width_growth):
    n_t = lax.axis_size("tensor")
    n_d = lax.axis_size("dp")
    t = lax.axis_index("tensor")
    rows, ds = width_growth.shape
    xw = ds // n_t
    blk = ds // n_d
    w_cols = lax.dynamic_slice_in_dim(width_growth, t * xw, xw, axis=1)
    tw_blocks = _tw(tokens, w_cols, n_t, n_d)
    hb = blk // 2
    w3h = width_growth.reshape(rows, n_d, 2, hb).transpose(1, 2, 0, 3)
    grown = []
    parts = []
    panels = tw_blocks
    for m in range(2):
        panels, sw = lax.optimization_barrier((panels, small_weights[m]))
        if not m:
            tw_blocks = panels
        s_rows = lax.all_gather(sw, "tensor", axis=0, tiled=True)
        panels = jnp.dot(s_rows, ffn_growth.T, preferred_element_type=jnp.float32).astype(jnp.bfloat16)
        g, pall = _dp_ring(panels.reshape(2, hb, panels.shape[1]), w3h, m)
        grown.append(g)
        parts.append(pall.reshape(n_t, xw, panels.shape[1]))
    grown_weights = jnp.stack(grown)
    all_panels = jnp.stack(parts)
    pre_values = jnp.einsum(
        "kts,mksc->tmc",
        tw_blocks,
        all_panels,
        preferred_element_type=jnp.float32,
    )
    hidden = (jax.nn.silu(pre_values[:, 0, :]) * pre_values[:, 1, :]).astype(jnp.bfloat16)
    return (grown_weights, hidden)


def solution(mesh):
    placed = (P("dp", "tensor"), P(None, ("dp", "tensor"), None), P("tensor", None), P("dp", None))
    return jax.shard_map(
        on_device,
        mesh=mesh,
        in_specs=placed,
        out_specs=(P(None, "dp", "tensor"), P("dp", "tensor")),
        check_vma=False,
    )
```

```python
import functools

import jax
import jax.numpy as jnp
from jax import lax
from jax.experimental import pallas as pl
from jax.experimental.pallas import tpu as pltpu
from jax.sharding import PartitionSpec as P

MESH = pl.DeviceIdType.MESH


def _ring_pos(d):
    h = d // 4
    return h * 7 + (1 - 2 * h) * (d % 4)


def _ring_dev(p):
    h = p // 4
    return h * 4 + h * 3 + (1 - 2 * h) * (p % 4)


def _dp_ring_kernel(n, p_ref, w3_ref, tw_ref, grown_ref, hid_ref, recv, acc, pre, ssem, rsem, osem):
    t = lax.axis_index("tensor")
    d = lax.axis_index("dp")
    pos = _ring_pos(d)
    right = _ring_dev((pos + 1) % n)
    left = _ring_dev((pos + n - 1) % n)
    blk = p_ref.shape[1]
    xw = tw_ref.shape[2]
    per = blk // xw

    barrier = pltpu.get_barrier_semaphore()
    for nb in (left, right):
        pl.semaphore_signal(barrier, inc=1, device_id=(nb, t), device_id_type=MESH)
    pl.semaphore_wait(barrier, 2)

    own = []
    for m in range(2):
        c = pltpu.make_async_copy(p_ref.at[m], recv.at[m, d], osem.at[m])
        c.start()
        own.append(c)
    for c in own:
        c.wait()

    def contrib(m, o):
        g = jnp.dot(w3_ref[o], recv[m, o], preferred_element_type=jnp.float32)
        h = None
        for q in range(per):
            part = jnp.dot(tw_ref[per * o + q], recv[m, o, pl.ds(q * xw, xw), :],
                           preferred_element_type=jnp.float32)
            h = part if h is None else h + part
        return g, h

    def step(k, carry):
        o0 = _ring_dev((pos - k + n) % n)
        o1 = _ring_dev((pos + k) % n)
        c0 = pltpu.make_async_remote_copy(
            src_ref=recv.at[0, o0], dst_ref=recv.at[0, o0],
            send_sem=ssem.at[0, k], recv_sem=rsem.at[0, k],
            device_id=(right, t), device_id_type=MESH)
        c1 = pltpu.make_async_remote_copy(
            src_ref=recv.at[1, o1], dst_ref=recv.at[1, o1],
            send_sem=ssem.at[1, k], recv_sem=rsem.at[1, k],
            device_id=(left, t), device_id_type=MESH)
        c0.start()
        c1.start()
        g0, h0 = contrib(0, o0)
        g1, h1 = contrib(1, o1)

        @pl.when(k == 0)
        def _():
            acc[0] = g0
            acc[1] = g1
            pre[0] = h0
            pre[1] = h1

        @pl.when(k > 0)
        def _():
            acc[0] += g0
            acc[1] += g1
            pre[0] += h0
            pre[1] += h1

        c0.wait()
        c1.wait()
        return carry

    lax.fori_loop(0, n - 1, step, 0)
    o0 = _ring_dev((pos - (n - 1) + n) % n)
    o1 = _ring_dev((pos + n - 1) % n)
    g0, h0 = contrib(0, o0)
    g1, h1 = contrib(1, o1)
    acc[0] += g0
    acc[1] += g1
    grown_ref[...] = acc[...].astype(grown_ref.dtype)
    gate = pre[0] + h0
    up = pre[1] + h1
    hid_ref[...] = (gate / (1.0 + jnp.exp(-gate)) * up).astype(hid_ref.dtype)


def _dp_ring(panels, w3, tw_blocks):
    n, rows, blk = w3.shape
    _, _, cols = panels.shape
    nt, tok, xw = tw_blocks.shape
    flops = 2 * 2 * rows * blk * cols * n + 2 * 2 * tok * xw * nt * cols
    return pl.pallas_call(
        functools.partial(_dp_ring_kernel, n),
        out_shape=(
            jax.ShapeDtypeStruct((2, rows, cols), jnp.bfloat16),
            jax.ShapeDtypeStruct((tok, cols), jnp.bfloat16),
        ),
        in_specs=[pl.BlockSpec(memory_space=pltpu.VMEM)] * 3,
        out_specs=(pl.BlockSpec(memory_space=pltpu.VMEM), pl.BlockSpec(memory_space=pltpu.VMEM)),
        scratch_shapes=[
            pltpu.VMEM((2, n, blk, cols), jnp.bfloat16),
            pltpu.VMEM((2, rows, cols), jnp.float32),
            pltpu.VMEM((2, tok, cols), jnp.float32),
            pltpu.SemaphoreType.DMA((2, n - 1)),
            pltpu.SemaphoreType.DMA((2, n - 1)),
            pltpu.SemaphoreType.DMA((2,)),
        ],
        compiler_params=pltpu.CompilerParams(
            collective_id=0, has_side_effects=True, vmem_limit_bytes=56 * 1024 * 1024),
        cost_estimate=pl.CostEstimate(
            flops=flops, transcendentals=tok * cols, bytes_accessed=2 * 2 * n * blk * cols * 2),
    )(panels, w3, tw_blocks)


def _tw_kernel(nt, nd, tok_ref, wcol_ref, out_ref, tbuf, wbuf, xbuf,
               ts_sem, tr_sem, ws_sem, wr_sem, xs_sem, xr_sem, l_sem):
    t = lax.axis_index("tensor")
    d = lax.axis_index("dp")
    rb = tok_ref.shape[1]

    barrier = pltpu.get_barrier_semaphore()

    def greet_t(j, c):
        pl.semaphore_signal(barrier, inc=1, device_id=(d, (t + j) % nt), device_id_type=MESH)
        return c

    def greet_d(j, c):
        pl.semaphore_signal(barrier, inc=1, device_id=((d + j) % nd, t), device_id_type=MESH)
        return c

    lax.fori_loop(1, nt, greet_t, 0)
    lax.fori_loop(1, nd, greet_d, 0)
    pl.semaphore_wait(barrier, nt - 1 + nd - 1)

    c0 = pltpu.make_async_copy(tok_ref, tbuf.at[t], l_sem.at[0])
    c1 = pltpu.make_async_copy(wcol_ref, wbuf.at[d], l_sem.at[1])
    c0.start()
    c1.start()

    def t_copy(p):
        return pltpu.make_async_remote_copy(
            src_ref=tok_ref, dst_ref=tbuf.at[t], send_sem=ts_sem.at[p], recv_sem=tr_sem.at[t],
            device_id=(d, p), device_id_type=MESH)

    def t_recv(p):
        return pltpu.make_async_remote_copy(
            src_ref=tok_ref, dst_ref=tbuf.at[p], send_sem=ts_sem.at[p], recv_sem=tr_sem.at[p],
            device_id=(d, p), device_id_type=MESH)

    def w_copy(p):
        return pltpu.make_async_remote_copy(
            src_ref=wcol_ref, dst_ref=wbuf.at[d], send_sem=ws_sem.at[p], recv_sem=wr_sem.at[d],
            device_id=(p, t), device_id_type=MESH)

    def w_recv(p):
        return pltpu.make_async_remote_copy(
            src_ref=wcol_ref, dst_ref=wbuf.at[p], send_sem=ws_sem.at[p], recv_sem=wr_sem.at[p],
            device_id=(p, t), device_id_type=MESH)

    def send_t(j, c):
        t_copy((t + j) % nt).start()
        return c

    def send_d(j, c):
        w_copy((d + j) % nd).start()
        return c

    lax.fori_loop(1, nt, send_t, 0)
    lax.fori_loop(1, nd, send_d, 0)

    def wait_t(j, c):
        p = (t + j) % nt
        t_copy(p).wait_send()
        t_recv(p).wait_recv()
        return c

    def wait_d(j, c):
        p = (d + j) % nd
        w_copy(p).wait_send()
        w_recv(p).wait_recv()
        return c

    lax.fori_loop(1, nt, wait_t, 0)
    lax.fori_loop(1, nd, wait_d, 0)
    c0.wait()
    c1.wait()

    per = nt // nd
    acc = None
    for q in range(nt):
        part = jnp.dot(tbuf[q], wbuf[q // per, pl.ds((q % per) * rb, rb), :],
                       preferred_element_type=jnp.float32)
        acc = part if acc is None else acc + part
    xbuf[t] = acc.astype(xbuf.dtype)

    def x_copy(p):
        return pltpu.make_async_remote_copy(
            src_ref=xbuf.at[t], dst_ref=xbuf.at[t], send_sem=xs_sem.at[p], recv_sem=xr_sem.at[t],
            device_id=(d, p), device_id_type=MESH)

    def x_recv(p):
        return pltpu.make_async_remote_copy(
            src_ref=xbuf.at[p], dst_ref=xbuf.at[p], send_sem=xs_sem.at[p], recv_sem=xr_sem.at[p],
            device_id=(d, p), device_id_type=MESH)

    def send_x(j, c):
        x_copy((t + j) % nt).start()
        return c

    def wait_x(j, c):
        p = (t + j) % nt
        x_copy(p).wait_send()
        x_recv(p).wait_recv()
        return c

    lax.fori_loop(1, nt, send_x, 0)
    lax.fori_loop(1, nt, wait_x, 0)
    out_ref[...] = xbuf[...]


def _tw(tokens, wcol, nt, nd):
    tok, rb = tokens.shape
    rows, xw = wcol.shape
    return pl.pallas_call(
        functools.partial(_tw_kernel, nt, nd),
        out_shape=jax.ShapeDtypeStruct((nt, tok, xw), jnp.bfloat16),
        in_specs=[pl.BlockSpec(memory_space=pltpu.VMEM)] * 2,
        out_specs=pl.BlockSpec(memory_space=pltpu.VMEM),
        scratch_shapes=[
            pltpu.VMEM((nt, tok, rb), jnp.bfloat16),
            pltpu.VMEM((nd, rows, xw), jnp.bfloat16),
            pltpu.VMEM((nt, tok, xw), jnp.bfloat16),
            pltpu.SemaphoreType.DMA((nt,)),
            pltpu.SemaphoreType.DMA((nt,)),
            pltpu.SemaphoreType.DMA((nd,)),
            pltpu.SemaphoreType.DMA((nd,)),
            pltpu.SemaphoreType.DMA((nt,)),
            pltpu.SemaphoreType.DMA((nt,)),
            pltpu.SemaphoreType.DMA((2,)),
        ],
        compiler_params=pltpu.CompilerParams(
            collective_id=1, has_side_effects=True, vmem_limit_bytes=32 * 1024 * 1024),
        cost_estimate=pl.CostEstimate(
            flops=2 * tok * rb * nt * xw, transcendentals=0,
            bytes_accessed=(nt * tok * rb + nd * rows * xw + 2 * nt * tok * xw) * 2),
    )(tokens, wcol)


def on_device(tokens, small_weights, ffn_growth, width_growth):
    n_t = lax.axis_size("tensor")
    n_d = lax.axis_size("dp")
    t = lax.axis_index("tensor")
    rows, ds = width_growth.shape
    xw = ds // n_t
    blk = ds // n_d
    w_cols = lax.dynamic_slice_in_dim(width_growth, t * xw, xw, axis=1)
    tw_blocks = _tw(tokens, w_cols, n_t, n_d)
    panels = jnp.einsum(
        "msf,cf->msc",
        lax.all_gather(small_weights, "tensor", axis=1, tiled=True),
        ffn_growth,
        preferred_element_type=jnp.float32,
    ).astype(jnp.bfloat16)
    w3 = width_growth.reshape(rows, n_d, blk).transpose(1, 0, 2)
    grown_weights, hidden = _dp_ring(panels, w3, tw_blocks)
    return (grown_weights, hidden)


def solution(mesh):
    placed = (P("dp", "tensor"), P(None, ("dp", "tensor"), None), P("tensor", None), P("dp", None))
    return jax.shard_map(
        on_device,
        mesh=mesh,
        in_specs=placed,
        out_specs=(P(None, "dp", "tensor"), P("dp", "tensor")),
        check_vma=False,
    )
```

```python
import functools

import jax
import jax.numpy as jnp
from jax import lax
from jax.experimental import pallas as pl
from jax.experimental.pallas import tpu as pltpu
from jax.sharding import Mesh, PartitionSpec as P

MESH = pl.DeviceIdType.MESH


def _tidx():
    return lax.axis_index("tp") * 2 + lax.axis_index("core")


def _dev(d, t):
    return (d, t // 2, t % 2)


def _ring_pos(d):
    h = d // 4
    return h * 7 + (1 - 2 * h) * (d % 4)


def _ring_dev(p):
    h = p // 4
    return h * 4 + h * 3 + (1 - 2 * h) * (p % 4)


def _dp_ring_kernel(n, p_ref, w3_ref, tw_ref, grown_ref, hid_ref, recv, acc, pre, ssem, rsem, osem):
    t = _tidx()
    d = lax.axis_index("dp")
    pos = _ring_pos(d)
    right = _ring_dev((pos + 1) % n)
    left = _ring_dev((pos + n - 1) % n)
    blk = p_ref.shape[1]
    xw = tw_ref.shape[2]
    per = blk // xw

    barrier = pltpu.get_barrier_semaphore()
    for nb in (left, right):
        pl.semaphore_signal(barrier, inc=1, device_id=_dev(nb, t), device_id_type=MESH)
    pl.semaphore_wait(barrier, 2)

    own = []
    for m in range(2):
        c = pltpu.make_async_copy(p_ref.at[m], recv.at[m, d], osem.at[m])
        c.start()
        own.append(c)
    for c in own:
        c.wait()

    def contrib(m, o):
        g = jnp.dot(w3_ref[o], recv[m, o], preferred_element_type=jnp.float32)
        h = None
        for q in range(per):
            part = jnp.dot(tw_ref[per * o + q], recv[m, o, pl.ds(q * xw, xw), :],
                           preferred_element_type=jnp.float32)
            h = part if h is None else h + part
        return g, h

    def step(k, carry):
        o0 = _ring_dev((pos - k + n) % n)
        o1 = _ring_dev((pos + k) % n)
        c0 = pltpu.make_async_remote_copy(
            src_ref=recv.at[0, o0], dst_ref=recv.at[0, o0],
            send_sem=ssem.at[0, k], recv_sem=rsem.at[0, k],
            device_id=_dev(right, t), device_id_type=MESH)
        c1 = pltpu.make_async_remote_copy(
            src_ref=recv.at[1, o1], dst_ref=recv.at[1, o1],
            send_sem=ssem.at[1, k], recv_sem=rsem.at[1, k],
            device_id=_dev(left, t), device_id_type=MESH)
        c0.start()
        c1.start()
        g0, h0 = contrib(0, o0)
        g1, h1 = contrib(1, o1)

        @pl.when(k == 0)
        def _():
            acc[0] = g0
            acc[1] = g1
            pre[0] = h0
            pre[1] = h1

        @pl.when(k > 0)
        def _():
            acc[0] += g0
            acc[1] += g1
            pre[0] += h0
            pre[1] += h1

        c0.wait()
        c1.wait()
        return carry

    lax.fori_loop(0, n - 1, step, 0)
    o0 = _ring_dev((pos - (n - 1) + n) % n)
    o1 = _ring_dev((pos + n - 1) % n)
    g0, h0 = contrib(0, o0)
    g1, h1 = contrib(1, o1)
    acc[0] += g0
    acc[1] += g1
    grown_ref[...] = acc[...].astype(grown_ref.dtype)
    gate = pre[0] + h0
    up = pre[1] + h1
    hid_ref[...] = (gate / (1.0 + jnp.exp(-gate)) * up).astype(hid_ref.dtype)


def _dp_ring(panels, w3, tw_blocks):
    n, rows, blk = w3.shape
    _, _, cols = panels.shape
    nt, tok, xw = tw_blocks.shape
    flops = 2 * 2 * rows * blk * cols * n + 2 * 2 * tok * xw * nt * cols
    return pl.pallas_call(
        functools.partial(_dp_ring_kernel, n),
        out_shape=(
            jax.ShapeDtypeStruct((2, rows, cols), jnp.bfloat16),
            jax.ShapeDtypeStruct((tok, cols), jnp.bfloat16),
        ),
        in_specs=[pl.BlockSpec(memory_space=pltpu.VMEM)] * 3,
        out_specs=(pl.BlockSpec(memory_space=pltpu.VMEM), pl.BlockSpec(memory_space=pltpu.VMEM)),
        scratch_shapes=[
            pltpu.VMEM((2, n, blk, cols), jnp.bfloat16),
            pltpu.VMEM((2, rows, cols), jnp.float32),
            pltpu.VMEM((2, tok, cols), jnp.float32),
            pltpu.SemaphoreType.DMA((2, n - 1)),
            pltpu.SemaphoreType.DMA((2, n - 1)),
            pltpu.SemaphoreType.DMA((2,)),
        ],
        compiler_params=pltpu.CompilerParams(
            collective_id=0, has_side_effects=True, vmem_limit_bytes=56 * 1024 * 1024),
        cost_estimate=pl.CostEstimate(
            flops=flops, transcendentals=tok * cols, bytes_accessed=2 * 2 * n * blk * cols * 2),
    )(panels, w3, tw_blocks)


def _tw_kernel(nt, nd, tok_ref, wcol_ref, out_ref, tbuf, wbuf, xbuf,
               ts_sem, tr_sem, ws_sem, wr_sem, xs_sem, xr_sem, l_sem):
    t = _tidx()
    d = lax.axis_index("dp")
    rb = tok_ref.shape[1]

    barrier = pltpu.get_barrier_semaphore()

    def greet_t(j, c):
        pl.semaphore_signal(barrier, inc=1, device_id=_dev(d, (t + j) % nt), device_id_type=MESH)
        return c

    def greet_d(j, c):
        pl.semaphore_signal(barrier, inc=1, device_id=_dev((d + j) % nd, t), device_id_type=MESH)
        return c

    lax.fori_loop(1, nt, greet_t, 0)
    lax.fori_loop(1, nd, greet_d, 0)
    pl.semaphore_wait(barrier, nt - 1 + nd - 1)

    c0 = pltpu.make_async_copy(tok_ref, tbuf.at[t], l_sem.at[0])
    c1 = pltpu.make_async_copy(wcol_ref, wbuf.at[d], l_sem.at[1])
    c0.start()
    c1.start()

    def t_copy(p):
        return pltpu.make_async_remote_copy(
            src_ref=tok_ref, dst_ref=tbuf.at[t], send_sem=ts_sem.at[p], recv_sem=tr_sem.at[t],
            device_id=_dev(d, p), device_id_type=MESH)

    def t_recv(p):
        return pltpu.make_async_remote_copy(
            src_ref=tok_ref, dst_ref=tbuf.at[p], send_sem=ts_sem.at[p], recv_sem=tr_sem.at[p],
            device_id=_dev(d, p), device_id_type=MESH)

    def w_copy(p):
        return pltpu.make_async_remote_copy(
            src_ref=wcol_ref, dst_ref=wbuf.at[d], send_sem=ws_sem.at[p], recv_sem=wr_sem.at[d],
            device_id=_dev(p, t), device_id_type=MESH)

    def w_recv(p):
        return pltpu.make_async_remote_copy(
            src_ref=wcol_ref, dst_ref=wbuf.at[p], send_sem=ws_sem.at[p], recv_sem=wr_sem.at[p],
            device_id=_dev(p, t), device_id_type=MESH)

    def send_t(j, c):
        t_copy((t + j) % nt).start()
        return c

    def send_d(j, c):
        w_copy((d + j) % nd).start()
        return c

    lax.fori_loop(1, nt, send_t, 0)
    lax.fori_loop(1, nd, send_d, 0)

    def wait_t(j, c):
        p = (t + j) % nt
        t_copy(p).wait_send()
        t_recv(p).wait_recv()
        return c

    def wait_d(j, c):
        p = (d + j) % nd
        w_copy(p).wait_send()
        w_recv(p).wait_recv()
        return c

    lax.fori_loop(1, nt, wait_t, 0)
    lax.fori_loop(1, nd, wait_d, 0)
    c0.wait()
    c1.wait()

    per = nt // nd
    acc = None
    for q in range(nt):
        part = jnp.dot(tbuf[q], wbuf[q // per, pl.ds((q % per) * rb, rb), :],
                       preferred_element_type=jnp.float32)
        acc = part if acc is None else acc + part
    xbuf[t] = acc.astype(xbuf.dtype)

    def x_copy(p):
        return pltpu.make_async_remote_copy(
            src_ref=xbuf.at[t], dst_ref=xbuf.at[t], send_sem=xs_sem.at[p], recv_sem=xr_sem.at[t],
            device_id=_dev(d, p), device_id_type=MESH)

    def x_recv(p):
        return pltpu.make_async_remote_copy(
            src_ref=xbuf.at[p], dst_ref=xbuf.at[p], send_sem=xs_sem.at[p], recv_sem=xr_sem.at[p],
            device_id=_dev(d, p), device_id_type=MESH)

    def send_x(j, c):
        x_copy((t + j) % nt).start()
        return c

    def wait_x(j, c):
        p = (t + j) % nt
        x_copy(p).wait_send()
        x_recv(p).wait_recv()
        return c

    lax.fori_loop(1, nt, send_x, 0)
    lax.fori_loop(1, nt, wait_x, 0)
    out_ref[...] = xbuf[...]


def _tw(tokens, wcol, nt, nd):
    tok, rb = tokens.shape
    rows, xw = wcol.shape
    return pl.pallas_call(
        functools.partial(_tw_kernel, nt, nd),
        out_shape=jax.ShapeDtypeStruct((nt, tok, xw), jnp.bfloat16),
        in_specs=[pl.BlockSpec(memory_space=pltpu.VMEM)] * 2,
        out_specs=pl.BlockSpec(memory_space=pltpu.VMEM),
        scratch_shapes=[
            pltpu.VMEM((nt, tok, rb), jnp.bfloat16),
            pltpu.VMEM((nd, rows, xw), jnp.bfloat16),
            pltpu.VMEM((nt, tok, xw), jnp.bfloat16),
            pltpu.SemaphoreType.DMA((nt,)),
            pltpu.SemaphoreType.DMA((nt,)),
            pltpu.SemaphoreType.DMA((nd,)),
            pltpu.SemaphoreType.DMA((nd,)),
            pltpu.SemaphoreType.DMA((nt,)),
            pltpu.SemaphoreType.DMA((nt,)),
            pltpu.SemaphoreType.DMA((2,)),
        ],
        compiler_params=pltpu.CompilerParams(
            collective_id=1, has_side_effects=True, vmem_limit_bytes=32 * 1024 * 1024),
        cost_estimate=pl.CostEstimate(
            flops=2 * tok * rb * nt * xw, transcendentals=0,
            bytes_accessed=(nt * tok * rb + nd * rows * xw + 2 * nt * tok * xw) * 2),
    )(tokens, wcol)


def on_device(tokens, small_weights, ffn_growth, width_growth):
    n_c = lax.axis_size("core")
    n_t = lax.axis_size("tp") * n_c
    n_d = lax.axis_size("dp")
    t = _tidx()
    rows, ds = width_growth.shape
    xw = ds // n_t
    blk = ds // n_d
    w_cols = lax.dynamic_slice_in_dim(width_growth, t * xw, xw, axis=1)
    tw_blocks = _tw(tokens, w_cols, n_t, n_d)
    mine = lax.all_gather(small_weights, "tp", axis=1, tiled=True)
    tw_blocks, sent = lax.optimization_barrier((tw_blocks, mine))
    other = lax.ppermute(sent, "core", perm=[(0, 1), (1, 0)])
    ffn_t = ffn_growth.T
    p_mine = jnp.dot(mine, ffn_t, preferred_element_type=jnp.float32).astype(jnp.bfloat16)
    p_other = jnp.dot(other, ffn_t, preferred_element_type=jnp.float32).astype(jnp.bfloat16)
    first = lax.axis_index("core") == 0
    cols = p_mine.shape[2]
    per_dev = small_weights.shape[1]
    halves = [jnp.where(first, p_mine, p_other), jnp.where(first, p_other, p_mine)]
    halves = [h.reshape(2, n_t // n_c, per_dev, cols) for h in halves]
    panels = jnp.stack(halves, axis=2).reshape(2, blk, cols)
    w3 = width_growth.reshape(rows, n_d, blk).transpose(1, 0, 2)
    grown_weights, hidden = _dp_ring(panels, w3, tw_blocks)
    return (grown_weights, hidden)


def solution(mesh):
    n_d = mesh.shape["dp"]
    sub = Mesh(mesh.devices.reshape(n_d, -1, 2), ("dp", "tp", "core"))
    tn = ("tp", "core")
    placed = (P("dp", tn), P(None, ("dp",) + tn, None), P(tn, None), P("dp", None))
    return jax.shard_map(
        on_device,
        mesh=sub,
        in_specs=placed,
        out_specs=(P(None, "dp", tn), P("dp", tn)),
        check_vma=False,
    )
```

```python
import functools

import jax
import jax.numpy as jnp
from jax import lax
from jax.experimental import pallas as pl
from jax.experimental.pallas import tpu as pltpu
from jax.sharding import PartitionSpec as P

MESH = pl.DeviceIdType.MESH


def _ring_pos(d):
    h = d // 4
    return h * 7 + (1 - 2 * h) * (d % 4)


def _ring_dev(p):
    h = p // 4
    return h * 4 + h * 3 + (1 - 2 * h) * (p % 4)


def _dp_ring_kernel(n, nt, p_ref, w3_ref, tf_ref, wg_ref, grown_ref, hid_ref,
                    recv, acc, xbuf, ssem, rsem, xs_sem, xr_sem, osem):
    t = lax.axis_index("tensor")
    d = lax.axis_index("dp")
    pos = _ring_pos(d)
    right = _ring_dev((pos + 1) % n)
    left = _ring_dev((pos + n - 1) % n)
    blk = p_ref.shape[1]
    rb = tf_ref.shape[2]
    xw = wg_ref.shape[2]
    per_w = wg_ref.shape[1] // rb
    per = blk // xw

    barrier = pltpu.get_barrier_semaphore()
    for nb in (left, right):
        pl.semaphore_signal(barrier, inc=1, device_id=(nb, t), device_id_type=MESH)

    def greet_t(j, c):
        pl.semaphore_signal(barrier, inc=1, device_id=(d, (t + j) % nt), device_id_type=MESH)
        return c

    lax.fori_loop(1, nt, greet_t, 0)
    pl.semaphore_wait(barrier, 2 + nt - 1)

    own = []
    for m in range(2):
        c = pltpu.make_async_copy(p_ref.at[m], recv.at[m, d], osem.at[m])
        c.start()
        own.append(c)

    tw = None
    for q in range(nt):
        part = jnp.dot(tf_ref[q], wg_ref[q // per_w, pl.ds((q % per_w) * rb, rb), :],
                       preferred_element_type=jnp.float32)
        tw = part if tw is None else tw + part
    xbuf[t] = tw.astype(xbuf.dtype)

    def x_copy(p):
        return pltpu.make_async_remote_copy(
            src_ref=xbuf.at[t], dst_ref=xbuf.at[t], send_sem=xs_sem.at[p], recv_sem=xr_sem.at[t],
            device_id=(d, p), device_id_type=MESH)

    def x_recv(p):
        return pltpu.make_async_remote_copy(
            src_ref=xbuf.at[p], dst_ref=xbuf.at[p], send_sem=xs_sem.at[p], recv_sem=xr_sem.at[p],
            device_id=(d, p), device_id_type=MESH)

    def send_x(j, c):
        x_copy((t + j) % nt).start()
        return c

    lax.fori_loop(1, nt, send_x, 0)
    for c in own:
        c.wait()

    def step(k, carry):
        o0 = _ring_dev((pos - k + n) % n)
        o1 = _ring_dev((pos + k) % n)
        c0 = pltpu.make_async_remote_copy(
            src_ref=recv.at[0, o0], dst_ref=recv.at[0, o0],
            send_sem=ssem.at[0, k], recv_sem=rsem.at[0, k],
            device_id=(right, t), device_id_type=MESH)
        c1 = pltpu.make_async_remote_copy(
            src_ref=recv.at[1, o1], dst_ref=recv.at[1, o1],
            send_sem=ssem.at[1, k], recv_sem=rsem.at[1, k],
            device_id=(left, t), device_id_type=MESH)
        c0.start()
        c1.start()
        g0 = jnp.dot(w3_ref[o0], recv[0, o0], preferred_element_type=jnp.float32)
        g1 = jnp.dot(w3_ref[o1], recv[1, o1], preferred_element_type=jnp.float32)

        @pl.when(k == 0)
        def _():
            acc[0] = g0
            acc[1] = g1

        @pl.when(k > 0)
        def _():
            acc[0] += g0
            acc[1] += g1

        c0.wait()
        c1.wait()
        return carry

    lax.fori_loop(0, n - 1, step, 0)
    o0 = _ring_dev((pos - (n - 1) + n) % n)
    o1 = _ring_dev((pos + n - 1) % n)
    acc[0] += jnp.dot(w3_ref[o0], recv[0, o0], preferred_element_type=jnp.float32)
    acc[1] += jnp.dot(w3_ref[o1], recv[1, o1], preferred_element_type=jnp.float32)
    grown_ref[...] = acc[...].astype(grown_ref.dtype)

    def wait_x(j, c):
        p = (t + j) % nt
        x_copy(p).wait_send()
        x_recv(p).wait_recv()
        return c

    lax.fori_loop(1, nt, wait_x, 0)
    pre = []
    for m in range(2):
        s = None
        for q in range(nt):
            part = jnp.dot(xbuf[q], recv[m, q // per, pl.ds((q % per) * xw, xw), :],
                           preferred_element_type=jnp.float32)
            s = part if s is None else s + part
        pre.append(s)
    gate = pre[0]
    hid_ref[...] = (gate / (1.0 + jnp.exp(-gate)) * pre[1]).astype(hid_ref.dtype)


def _dp_ring(panels, w3, t_full, w_gath):
    n, rows, blk = w3.shape
    _, _, cols = panels.shape
    nt, tok, rb = t_full.shape
    xw = w_gath.shape[2]
    flops = 2 * 2 * rows * blk * cols * n + 2 * 2 * tok * xw * nt * cols + 2 * tok * rb * nt * xw
    return pl.pallas_call(
        functools.partial(_dp_ring_kernel, n, nt),
        out_shape=(
            jax.ShapeDtypeStruct((2, rows, cols), jnp.bfloat16),
            jax.ShapeDtypeStruct((tok, cols), jnp.bfloat16),
        ),
        in_specs=[pl.BlockSpec(memory_space=pltpu.VMEM)] * 4,
        out_specs=(pl.BlockSpec(memory_space=pltpu.VMEM), pl.BlockSpec(memory_space=pltpu.VMEM)),
        scratch_shapes=[
            pltpu.VMEM((2, n, blk, cols), jnp.bfloat16),
            pltpu.VMEM((2, rows, cols), jnp.float32),
            pltpu.VMEM((nt, tok, xw), jnp.bfloat16),
            pltpu.SemaphoreType.DMA((2, n - 1)),
            pltpu.SemaphoreType.DMA((2, n - 1)),
            pltpu.SemaphoreType.DMA((nt,)),
            pltpu.SemaphoreType.DMA((nt,)),
            pltpu.SemaphoreType.DMA((2,)),
        ],
        compiler_params=pltpu.CompilerParams(
            collective_id=0, has_side_effects=True, vmem_limit_bytes=60 * 1024 * 1024),
        cost_estimate=pl.CostEstimate(
            flops=flops, transcendentals=tok * cols, bytes_accessed=2 * 2 * n * blk * cols * 2),
    )(panels, w3, t_full, w_gath)


def _wg_kernel(nd, wcol_ref, out_ref, wbuf, ws_sem, wr_sem, l_sem):
    t = lax.axis_index("tensor")
    d = lax.axis_index("dp")
    barrier = pltpu.get_barrier_semaphore()

    def greet_d(j, c):
        pl.semaphore_signal(barrier, inc=1, device_id=((d + j) % nd, t), device_id_type=MESH)
        return c

    lax.fori_loop(1, nd, greet_d, 0)
    pl.semaphore_wait(barrier, nd - 1)
    c1 = pltpu.make_async_copy(wcol_ref, wbuf.at[d], l_sem.at[0])
    c1.start()

    def w_copy(p):
        return pltpu.make_async_remote_copy(
            src_ref=wcol_ref, dst_ref=wbuf.at[d], send_sem=ws_sem.at[p], recv_sem=wr_sem.at[d],
            device_id=(p, t), device_id_type=MESH)

    def w_recv(p):
        return pltpu.make_async_remote_copy(
            src_ref=wcol_ref, dst_ref=wbuf.at[p], send_sem=ws_sem.at[p], recv_sem=wr_sem.at[p],
            device_id=(p, t), device_id_type=MESH)

    def send_d(j, c):
        w_copy((d + j) % nd).start()
        return c

    def wait_d(j, c):
        p = (d + j) % nd
        w_copy(p).wait_send()
        w_recv(p).wait_recv()
        return c

    lax.fori_loop(1, nd, send_d, 0)
    lax.fori_loop(1, nd, wait_d, 0)
    c1.wait()
    out_ref[...] = wbuf[...]


def _wg(wcol, nd):
    rows, xw = wcol.shape
    return pl.pallas_call(
        functools.partial(_wg_kernel, nd),
        out_shape=jax.ShapeDtypeStruct((nd, rows, xw), jnp.bfloat16),
        in_specs=[pl.BlockSpec(memory_space=pltpu.VMEM)],
        out_specs=pl.BlockSpec(memory_space=pltpu.VMEM),
        scratch_shapes=[
            pltpu.VMEM((nd, rows, xw), jnp.bfloat16),
            pltpu.SemaphoreType.DMA((nd,)),
            pltpu.SemaphoreType.DMA((nd,)),
            pltpu.SemaphoreType.DMA((1,)),
        ],
        compiler_params=pltpu.CompilerParams(
            collective_id=1, has_side_effects=True, vmem_limit_bytes=32 * 1024 * 1024),
        cost_estimate=pl.CostEstimate(
            flops=0, transcendentals=0, bytes_accessed=nd * rows * xw * 2 * 64),
    )(wcol)


def on_device(tokens, small_weights, ffn_growth, width_growth):
    n_t = lax.axis_size("tensor")
    n_d = lax.axis_size("dp")
    t = lax.axis_index("tensor")
    rows, ds = width_growth.shape
    xw = ds // n_t
    blk = ds // n_d
    w_cols = lax.dynamic_slice_in_dim(width_growth, t * xw, xw, axis=1)
    w_gath = _wg(w_cols, n_d)
    m, per_dev, fs = small_weights.shape
    tok, rb = tokens.shape
    t_rows = -(-tok * rb // fs)
    t_pad = jnp.pad(tokens.reshape(-1), (0, t_rows * fs - tok * rb)).reshape(t_rows, fs)
    ext = jnp.concatenate([small_weights.reshape(m * per_dev, fs), t_pad], axis=0)
    g = lax.all_gather(ext, "tensor", axis=0, tiled=False)
    s_part = g[:, : m * per_dev, :]
    t_full = g[:, m * per_dev:, :].reshape(n_t, t_rows * fs)[:, : tok * rb].reshape(n_t, tok, rb)
    p_dev = jnp.einsum(
        "kjf,cf->kjc", s_part, ffn_growth, preferred_element_type=jnp.float32
    ).astype(jnp.bfloat16)
    cols = p_dev.shape[2]
    panels = p_dev.reshape(n_t, m, per_dev, cols).transpose(1, 0, 2, 3).reshape(m, blk, cols)
    w3 = width_growth.reshape(rows, n_d, blk).transpose(1, 0, 2)
    grown_weights, hidden = _dp_ring(panels, w3, t_full, w_gath)
    return (grown_weights, hidden)


def solution(mesh):
    placed = (P("dp", "tensor"), P(None, ("dp", "tensor"), None), P("tensor", None), P("dp", None))
    return jax.shard_map(
        on_device,
        mesh=mesh,
        in_specs=placed,
        out_specs=(P(None, "dp", "tensor"), P("dp", "tensor")),
        check_vma=False,
    )
```

```python
import functools

import jax
import jax.numpy as jnp
from jax import lax
from jax.experimental import pallas as pl
from jax.experimental.pallas import tpu as pltpu
from jax.sharding import PartitionSpec as P

MESH = pl.DeviceIdType.MESH


def _ring_pos(d):
    h = d // 4
    return h * 7 + (1 - 2 * h) * (d % 4)


def _ring_dev(p):
    h = p // 4
    return h * 4 + h * 3 + (1 - 2 * h) * (p % 4)


def _cross_pos(d):
    z = d % 4
    return 2 * z + (d // 4 + z) % 2


def _cross_dev(p):
    i = p // 2
    return ((i + p % 2) % 2) * 4 + i


def _flip_z(d, c):
    z = d % 4
    return d + c * (1 - 2 * (z % 2))


def _flip_y(d, c):
    y = d // 4
    return d + c * (1 - 2 * y) * 4


def _dp_ring_kernel(n, p_ref, w3_ref, tw_ref, grown_ref, hid_ref, recv, acc, pre, ssem, rsem, osem):
    t = lax.axis_index("tensor")
    d = lax.axis_index("dp")
    c = t % 2
    pos_a = _ring_pos(_flip_z(d, c))
    pos_b = _cross_pos(_flip_y(d, c))

    def dev_a(p):
        return _flip_z(_ring_dev(p % n), c)

    def dev_b(p):
        return _flip_y(_cross_dev(p % n), c)

    flows = [
        (dev_a, pos_a, 1),
        (dev_a, pos_a, -1),
        (dev_b, pos_b, 1),
        (dev_b, pos_b, -1),
    ]
    xw = tw_ref.shape[2]

    barrier = pltpu.get_barrier_semaphore()
    for dev, pos, sgn in flows:
        pl.semaphore_signal(barrier, inc=1, device_id=(dev(pos + sgn + n), t), device_id_type=MESH)
    pl.semaphore_wait(barrier, 4)

    own = []
    for q in range(4):
        cp = pltpu.make_async_copy(p_ref.at[q], recv.at[q, d], osem.at[q])
        cp.start()
        own.append(cp)
    for cp in own:
        cp.wait()

    def origin(q, k):
        dev, pos, sgn = flows[q]
        return dev(pos - sgn * k + n)

    def contrib(q, o):
        g = jnp.dot(w3_ref[o, q % 2], recv[q, o], preferred_element_type=jnp.float32)
        h = jnp.dot(tw_ref[2 * o + q % 2], recv[q, o], preferred_element_type=jnp.float32)
        return g, h

    def step(k, carry):
        copies = []
        origins = []
        for q in range(4):
            dev, pos, sgn = flows[q]
            o = origin(q, k)
            cp = pltpu.make_async_remote_copy(
                src_ref=recv.at[q, o], dst_ref=recv.at[q, o],
                send_sem=ssem.at[q, k], recv_sem=rsem.at[q, k],
                device_id=(dev(pos + sgn + n), t), device_id_type=MESH)
            cp.start()
            copies.append(cp)
            origins.append(o)
        parts = [contrib(q, origins[q]) for q in range(4)]
        g0 = parts[0][0] + parts[1][0]
        g1 = parts[2][0] + parts[3][0]
        h0 = parts[0][1] + parts[1][1]
        h1 = parts[2][1] + parts[3][1]

        @pl.when(k == 0)
        def _():
            acc[0] = g0
            acc[1] = g1
            pre[0] = h0
            pre[1] = h1

        @pl.when(k > 0)
        def _():
            acc[0] += g0
            acc[1] += g1
            pre[0] += h0
            pre[1] += h1

        for cp in copies:
            cp.wait()
        return carry

    lax.fori_loop(0, n - 1, step, 0)
    parts = [contrib(q, origin(q, n - 1)) for q in range(4)]
    acc[0] += parts[0][0] + parts[1][0]
    acc[1] += parts[2][0] + parts[3][0]
    grown_ref[...] = acc[...].astype(grown_ref.dtype)
    gate = pre[0] + parts[0][1] + parts[1][1]
    up = pre[1] + parts[2][1] + parts[3][1]
    hid_ref[...] = (gate / (1.0 + jnp.exp(-gate)) * up).astype(hid_ref.dtype)


def _dp_ring(quarters, w3h, tw_blocks):
    n, _, rows, hb = w3h.shape
    _, _, cols = quarters.shape
    nt, tok, xw = tw_blocks.shape
    flops = 2 * 2 * rows * hb * 2 * cols * n + 2 * 2 * tok * xw * nt * cols
    return pl.pallas_call(
        functools.partial(_dp_ring_kernel, n),
        out_shape=(
            jax.ShapeDtypeStruct((2, rows, cols), jnp.bfloat16),
            jax.ShapeDtypeStruct((tok, cols), jnp.bfloat16),
        ),
        in_specs=[pl.BlockSpec(memory_space=pltpu.VMEM)] * 3,
        out_specs=(pl.BlockSpec(memory_space=pltpu.VMEM), pl.BlockSpec(memory_space=pltpu.VMEM)),
        scratch_shapes=[
            pltpu.VMEM((4, n, hb, cols), jnp.bfloat16),
            pltpu.VMEM((2, rows, cols), jnp.float32),
            pltpu.VMEM((2, tok, cols), jnp.float32),
            pltpu.SemaphoreType.DMA((4, n - 1)),
            pltpu.SemaphoreType.DMA((4, n - 1)),
            pltpu.SemaphoreType.DMA((4,)),
        ],
        compiler_params=pltpu.CompilerParams(
            collective_id=0, has_side_effects=True, vmem_limit_bytes=56 * 1024 * 1024),
        cost_estimate=pl.CostEstimate(
            flops=flops, transcendentals=tok * cols, bytes_accessed=4 * n * hb * cols * 2),
    )(quarters, w3h, tw_blocks)


def _tw_kernel(nt, nd, tok_ref, wcol_ref, out_ref, tbuf, wbuf, xbuf,
               ts_sem, tr_sem, ws_sem, wr_sem, xs_sem, xr_sem, l_sem):
    t = lax.axis_index("tensor")
    d = lax.axis_index("dp")
    rb = tok_ref.shape[1]

    barrier = pltpu.get_barrier_semaphore()

    def greet_t(j, c):
        pl.semaphore_signal(barrier, inc=1, device_id=(d, (t + j) % nt), device_id_type=MESH)
        return c

    def greet_d(j, c):
        pl.semaphore_signal(barrier, inc=1, device_id=((d + j) % nd, t), device_id_type=MESH)
        return c

    lax.fori_loop(1, nt, greet_t, 0)
    lax.fori_loop(1, nd, greet_d, 0)
    pl.semaphore_wait(barrier, nt - 1 + nd - 1)

    c0 = pltpu.make_async_copy(tok_ref, tbuf.at[t], l_sem.at[0])
    c1 = pltpu.make_async_copy(wcol_ref, wbuf.at[d], l_sem.at[1])
    c0.start()
    c1.start()

    def t_copy(p):
        return pltpu.make_async_remote_copy(
            src_ref=tok_ref, dst_ref=tbuf.at[t], send_sem=ts_sem.at[p], recv_sem=tr_sem.at[t],
            device_id=(d, p), device_id_type=MESH)

    def t_recv(p):
        return pltpu.make_async_remote_copy(
            src_ref=tok_ref, dst_ref=tbuf.at[p], send_sem=ts_sem.at[p], recv_sem=tr_sem.at[p],
            device_id=(d, p), device_id_type=MESH)

    def w_copy(p):
        return pltpu.make_async_remote_copy(
            src_ref=wcol_ref, dst_ref=wbuf.at[d], send_sem=ws_sem.at[p], recv_sem=wr_sem.at[d],
            device_id=(p, t), device_id_type=MESH)

    def w_recv(p):
        return pltpu.make_async_remote_copy(
            src_ref=wcol_ref, dst_ref=wbuf.at[p], send_sem=ws_sem.at[p], recv_sem=wr_sem.at[p],
            device_id=(p, t), device_id_type=MESH)

    def send_t(j, c):
        t_copy((t + j) % nt).start()
        return c

    def send_d(j, c):
        w_copy((d + j) % nd).start()
        return c

    lax.fori_loop(1, nt, send_t, 0)
    lax.fori_loop(1, nd, send_d, 0)

    def wait_t(j, c):
        p = (t + j) % nt
        t_copy(p).wait_send()
        t_recv(p).wait_recv()
        return c

    def wait_d(j, c):
        p = (d + j) % nd
        w_copy(p).wait_send()
        w_recv(p).wait_recv()
        return c

    lax.fori_loop(1, nt, wait_t, 0)
    lax.fori_loop(1, nd, wait_d, 0)
    c0.wait()
    c1.wait()

    per = nt // nd
    acc = None
    for q in range(nt):
        part = jnp.dot(tbuf[q], wbuf[q // per, pl.ds((q % per) * rb, rb), :],
                       preferred_element_type=jnp.float32)
        acc = part if acc is None else acc + part
    xbuf[t] = acc.astype(xbuf.dtype)

    def x_copy(p):
        return pltpu.make_async_remote_copy(
            src_ref=xbuf.at[t], dst_ref=xbuf.at[t], send_sem=xs_sem.at[p], recv_sem=xr_sem.at[t],
            device_id=(d, p), device_id_type=MESH)

    def x_recv(p):
        return pltpu.make_async_remote_copy(
            src_ref=xbuf.at[p], dst_ref=xbuf.at[p], send_sem=xs_sem.at[p], recv_sem=xr_sem.at[p],
            device_id=(d, p), device_id_type=MESH)

    def send_x(j, c):
        x_copy((t + j) % nt).start()
        return c

    def wait_x(j, c):
        p = (t + j) % nt
        x_copy(p).wait_send()
        x_recv(p).wait_recv()
        return c

    lax.fori_loop(1, nt, send_x, 0)
    lax.fori_loop(1, nt, wait_x, 0)
    out_ref[...] = xbuf[...]


def _tw(tokens, wcol, nt, nd):
    tok, rb = tokens.shape
    rows, xw = wcol.shape
    return pl.pallas_call(
        functools.partial(_tw_kernel, nt, nd),
        out_shape=jax.ShapeDtypeStruct((nt, tok, xw), jnp.bfloat16),
        in_specs=[pl.BlockSpec(memory_space=pltpu.VMEM)] * 2,
        out_specs=pl.BlockSpec(memory_space=pltpu.VMEM),
        scratch_shapes=[
            pltpu.VMEM((nt, tok, rb), jnp.bfloat16),
            pltpu.VMEM((nd, rows, xw), jnp.bfloat16),
            pltpu.VMEM((nt, tok, xw), jnp.bfloat16),
            pltpu.SemaphoreType.DMA((nt,)),
            pltpu.SemaphoreType.DMA((nt,)),
            pltpu.SemaphoreType.DMA((nd,)),
            pltpu.SemaphoreType.DMA((nd,)),
            pltpu.SemaphoreType.DMA((nt,)),
            pltpu.SemaphoreType.DMA((nt,)),
            pltpu.SemaphoreType.DMA((2,)),
        ],
        compiler_params=pltpu.CompilerParams(
            collective_id=1, has_side_effects=True, vmem_limit_bytes=32 * 1024 * 1024),
        cost_estimate=pl.CostEstimate(
            flops=2 * tok * rb * nt * xw, transcendentals=0,
            bytes_accessed=(nt * tok * rb + nd * rows * xw + 2 * nt * tok * xw) * 2),
    )(tokens, wcol)


def on_device(tokens, small_weights, ffn_growth, width_growth):
    n_t = lax.axis_size("tensor")
    n_d = lax.axis_size("dp")
    t = lax.axis_index("tensor")
    rows, ds = width_growth.shape
    xw = ds // n_t
    blk = ds // n_d
    w_cols = lax.dynamic_slice_in_dim(width_growth, t * xw, xw, axis=1)
    tw_blocks = _tw(tokens, w_cols, n_t, n_d)
    panels = jnp.einsum(
        "msf,cf->msc",
        lax.all_gather(small_weights, "tensor", axis=1, tiled=True),
        ffn_growth,
        preferred_element_type=jnp.float32,
    ).astype(jnp.bfloat16)
    hb = blk // 2
    w3h = width_growth.reshape(rows, n_d, 2, hb).transpose(1, 2, 0, 3)
    quarters = panels.reshape(4, hb, panels.shape[2])
    grown_weights, hidden = _dp_ring(quarters, w3h, tw_blocks)
    return (grown_weights, hidden)


def solution(mesh):
    placed = (P("dp", "tensor"), P(None, ("dp", "tensor"), None), P("tensor", None), P("dp", None))
    return jax.shard_map(
        on_device,
        mesh=mesh,
        in_specs=placed,
        out_specs=(P(None, "dp", "tensor"), P("dp", "tensor")),
        check_vma=False,
    )
```

```python
import functools

import jax
import jax.numpy as jnp
from jax import lax
from jax.experimental import pallas as pl
from jax.experimental.pallas import tpu as pltpu
from jax.sharding import PartitionSpec as P

MESH = pl.DeviceIdType.MESH


def _ring_pos(d):
    h = d // 4
    return h * 7 + (1 - 2 * h) * (d % 4)


def _ring_dev(p):
    h = p // 4
    return h * 4 + h * 3 + (1 - 2 * h) * (p % 4)


def _cross_pos(d):
    z = d % 4
    return 2 * z + (d // 4 + z) % 2


def _cross_dev(p):
    i = p // 2
    return ((i + p % 2) % 2) * 4 + i


def _flip_z(d, c):
    z = d % 4
    return d + c * (1 - 2 * (z % 2))


def _flip_y(d, c):
    y = d // 4
    return d + c * (1 - 2 * y) * 4


def _dp_ring_kernel(n, p_ref, w3_ref, grown_ref, pall_ref, recv, acc, ssem, rsem, lsem, osem):
    t = lax.axis_index("tensor")
    d = lax.axis_index("dp")
    c = t % 2
    pos_a = _ring_pos(_flip_z(d, c))
    pos_b = _cross_pos(_flip_y(d, c))

    def dev_a(p):
        return _flip_z(_ring_dev(p % n), c)

    def dev_b(p):
        return _flip_y(_cross_dev(p % n), c)

    flows = [
        (dev_a, pos_a, 1),
        (dev_a, pos_a, -1),
        (dev_b, pos_b, 1),
        (dev_b, pos_b, -1),
    ]

    barrier = pltpu.get_barrier_semaphore()
    for dev, pos, sgn in flows:
        pl.semaphore_signal(barrier, inc=1, device_id=(dev(pos + sgn + n), t), device_id_type=MESH)
    pl.semaphore_wait(barrier, 4)

    own = []
    for q in range(4):
        cp = pltpu.make_async_copy(p_ref.at[q], recv.at[q, d], osem.at[q])
        cp.start()
        own.append(cp)
    for cp in own:
        cp.wait()
    for q in range(4):
        pltpu.make_async_copy(recv.at[q, d], pall_ref.at[q // 2, d, q % 2], lsem.at[q, d]).start()

    def origin(q, k):
        dev, pos, sgn = flows[q]
        return dev(pos - sgn * k + n)

    def contrib(q, o):
        return jnp.dot(w3_ref[o, q % 2], recv[q, o], preferred_element_type=jnp.float32)

    def step(k, carry):
        copies = []
        origins = []
        for q in range(4):
            dev, pos, sgn = flows[q]
            o = origin(q, k)
            cp = pltpu.make_async_remote_copy(
                src_ref=recv.at[q, o], dst_ref=recv.at[q, o],
                send_sem=ssem.at[q, k], recv_sem=rsem.at[q, k],
                device_id=(dev(pos + sgn + n), t), device_id_type=MESH)
            cp.start()
            copies.append(cp)
            origins.append(o)
        parts = [contrib(q, origins[q]) for q in range(4)]
        g0 = parts[0] + parts[1]
        g1 = parts[2] + parts[3]

        @pl.when(k == 0)
        def _():
            acc[0] = g0
            acc[1] = g1

        @pl.when(k > 0)
        def _():
            acc[0] += g0
            acc[1] += g1

        for q in range(4):
            copies[q].wait()
            nxt = origin(q, k + 1)
            pltpu.make_async_copy(recv.at[q, nxt], pall_ref.at[q // 2, nxt, q % 2], lsem.at[q, nxt]).start()
        return carry

    lax.fori_loop(0, n - 1, step, 0)
    parts = [contrib(q, origin(q, n - 1)) for q in range(4)]
    acc[0] += parts[0] + parts[1]
    acc[1] += parts[2] + parts[3]
    grown_ref[...] = acc[...].astype(grown_ref.dtype)
    for q in range(4):
        for o in range(n):
            pltpu.make_async_copy(recv.at[q, o], pall_ref.at[q // 2, o, q % 2], lsem.at[q, o]).wait()


def _dp_ring(quarters, w3h):
    n, _, rows, hb = w3h.shape
    _, _, cols = quarters.shape
    flops = 2 * 2 * rows * hb * 2 * cols * n
    return pl.pallas_call(
        functools.partial(_dp_ring_kernel, n),
        out_shape=(
            jax.ShapeDtypeStruct((2, rows, cols), jnp.bfloat16),
            jax.ShapeDtypeStruct((2, n, 2, hb, cols), jnp.bfloat16),
        ),
        in_specs=[pl.BlockSpec(memory_space=pltpu.VMEM)] * 2,
        out_specs=(pl.BlockSpec(memory_space=pltpu.VMEM), pl.BlockSpec(memory_space=pl.ANY)),
        scratch_shapes=[
            pltpu.VMEM((4, n, hb, cols), jnp.bfloat16),
            pltpu.VMEM((2, rows, cols), jnp.float32),
            pltpu.SemaphoreType.DMA((4, n - 1)),
            pltpu.SemaphoreType.DMA((4, n - 1)),
            pltpu.SemaphoreType.DMA((4, n)),
            pltpu.SemaphoreType.DMA((4,)),
        ],
        compiler_params=pltpu.CompilerParams(
            collective_id=0, has_side_effects=True, vmem_limit_bytes=56 * 1024 * 1024),
        cost_estimate=pl.CostEstimate(
            flops=flops, transcendentals=0, bytes_accessed=4 * n * hb * cols * 2),
    )(quarters, w3h)


def _wg_kernel(nd, wcol_ref, out_ref, wbuf, ws_sem, wr_sem, l_sem):
    t = lax.axis_index("tensor")
    d = lax.axis_index("dp")
    barrier = pltpu.get_barrier_semaphore()

    def greet_d(j, c):
        pl.semaphore_signal(barrier, inc=1, device_id=((d + j) % nd, t), device_id_type=MESH)
        return c

    lax.fori_loop(1, nd, greet_d, 0)
    pl.semaphore_wait(barrier, nd - 1)
    c1 = pltpu.make_async_copy(wcol_ref, wbuf.at[d], l_sem.at[0])
    c1.start()

    def w_copy(p):
        return pltpu.make_async_remote_copy(
            src_ref=wcol_ref, dst_ref=wbuf.at[d], send_sem=ws_sem.at[p], recv_sem=wr_sem.at[d],
            device_id=(p, t), device_id_type=MESH)

    def w_recv(p):
        return pltpu.make_async_remote_copy(
            src_ref=wcol_ref, dst_ref=wbuf.at[p], send_sem=ws_sem.at[p], recv_sem=wr_sem.at[p],
            device_id=(p, t), device_id_type=MESH)

    def send_d(j, c):
        w_copy((d + j) % nd).start()
        return c

    def wait_d(j, c):
        p = (d + j) % nd
        w_copy(p).wait_send()
        w_recv(p).wait_recv()
        return c

    lax.fori_loop(1, nd, send_d, 0)
    lax.fori_loop(1, nd, wait_d, 0)
    c1.wait()
    out_ref[...] = wbuf[...]


def _wg(wcol, nd):
    rows, xw = wcol.shape
    return pl.pallas_call(
        functools.partial(_wg_kernel, nd),
        out_shape=jax.ShapeDtypeStruct((nd, rows, xw), jnp.bfloat16),
        in_specs=[pl.BlockSpec(memory_space=pltpu.VMEM)],
        out_specs=pl.BlockSpec(memory_space=pltpu.VMEM),
        scratch_shapes=[
            pltpu.VMEM((nd, rows, xw), jnp.bfloat16),
            pltpu.SemaphoreType.DMA((nd,)),
            pltpu.SemaphoreType.DMA((nd,)),
            pltpu.SemaphoreType.DMA((1,)),
        ],
        compiler_params=pltpu.CompilerParams(
            collective_id=1, has_side_effects=True, vmem_limit_bytes=32 * 1024 * 1024),
        cost_estimate=pl.CostEstimate(
            flops=0, transcendentals=0, bytes_accessed=nd * rows * xw * 2 * 64),
    )(wcol)


def on_device(tokens, small_weights, ffn_growth, width_growth):
    n_t = lax.axis_size("tensor")
    n_d = lax.axis_size("dp")
    t = lax.axis_index("tensor")
    rows, ds = width_growth.shape
    xw = ds // n_t
    blk = ds // n_d
    w_cols = lax.dynamic_slice_in_dim(width_growth, t * xw, xw, axis=1)
    w_gath = _wg(w_cols, n_d)
    m, per_dev, fs = small_weights.shape
    tok, rb = tokens.shape
    t_rows = -(-tok * rb // fs)
    t_pad = jnp.pad(tokens.reshape(-1), (0, t_rows * fs - tok * rb)).reshape(t_rows, fs)
    ext = jnp.concatenate([small_weights.reshape(m * per_dev, fs), t_pad], axis=0)
    g = lax.all_gather(ext, "tensor", axis=0, tiled=False)
    s_part = g[:, : m * per_dev, :]
    t_full = g[:, m * per_dev:, :].reshape(n_t, t_rows * fs)[:, : tok * rb].reshape(n_t, tok, rb)
    t_row = t_full.transpose(1, 0, 2).reshape(tok, n_t * rb)
    tw_part = jnp.dot(t_row, w_gath.reshape(n_d * rows, xw), preferred_element_type=jnp.float32)
    tw_t = lax.all_gather(tw_part.astype(jnp.bfloat16).T, "tensor", axis=0, tiled=True)
    p_dev = jnp.einsum(
        "kjf,cf->kjc", s_part, ffn_growth, preferred_element_type=jnp.float32
    ).astype(jnp.bfloat16)
    cols = p_dev.shape[2]
    panels = p_dev.reshape(n_t, m, per_dev, cols).transpose(1, 0, 2, 3).reshape(m, blk, cols)
    hb = blk // 2
    w3h = width_growth.reshape(rows, n_d, 2, hb).transpose(1, 2, 0, 3)
    quarters = panels.reshape(4, hb, cols)
    grown_weights, pall = _dp_ring(quarters, w3h)
    all_panels = pall.reshape(m, ds, cols)
    pre_values = jnp.einsum(
        "st,msc->tmc", tw_t, all_panels, preferred_element_type=jnp.float32
    )
    hidden = (jax.nn.silu(pre_values[:, 0, :]) * pre_values[:, 1, :]).astype(jnp.bfloat16)
    return (grown_weights, hidden)


def solution(mesh):
    placed = (P("dp", "tensor"), P(None, ("dp", "tensor"), None), P("tensor", None), P("dp", None))
    return jax.shard_map(
        on_device,
        mesh=mesh,
        in_specs=placed,
        out_specs=(P(None, "dp", "tensor"), P("dp", "tensor")),
        check_vma=False,
    )
```

```python
import functools

import jax
import jax.numpy as jnp
from jax import lax
from jax.experimental import pallas as pl
from jax.experimental.pallas import tpu as pltpu
from jax.sharding import PartitionSpec as P

MESH = pl.DeviceIdType.MESH


def _ring_pos(d):
    h = d // 4
    return h * 7 + (1 - 2 * h) * (d % 4)


def _ring_dev(p):
    h = p // 4
    return h * 4 + h * 3 + (1 - 2 * h) * (p % 4)


def _cross_pos(d):
    z = d % 4
    return 2 * z + (d // 4 + z) % 2


def _cross_dev(p):
    i = p // 2
    return ((i + p % 2) % 2) * 4 + i


def _flip_z(d, c):
    z = d % 4
    return d + c * (1 - 2 * (z % 2))


def _flip_y(d, c):
    y = d // 4
    return d + c * (1 - 2 * y) * 4


def _dp_ring_kernel(n, p_ref, w3_ref, tw_ref, grown_ref, hid_ref, recv, acc, pre, ssem, rsem, osem):
    t = lax.axis_index("tensor")
    d = lax.axis_index("dp")
    c = t % 2
    pos_a = _ring_pos(_flip_z(d, c))
    pos_b = _cross_pos(_flip_y(d, c))

    def dev_a(p):
        return _flip_z(_ring_dev(p % n), c)

    def dev_b(p):
        return _flip_y(_cross_dev(p % n), c)

    flows = [
        (dev_a, pos_a, 1),
        (dev_a, pos_a, -1),
        (dev_b, pos_b, 1),
        (dev_b, pos_b, -1),
    ]
    xw = tw_ref.shape[2]

    barrier = pltpu.get_barrier_semaphore()
    for dev, pos, sgn in flows:
        pl.semaphore_signal(barrier, inc=1, device_id=(dev(pos + sgn + n), t), device_id_type=MESH)
    pl.semaphore_wait(barrier, 4)

    own = []
    for q in range(4):
        cp = pltpu.make_async_copy(p_ref.at[q], recv.at[q, d], osem.at[q])
        cp.start()
        own.append(cp)

    def origin(q, k):
        dev, pos, sgn = flows[q]
        return dev(pos - sgn * k + n)

    def contrib(q, o):
        g = jnp.dot(w3_ref[o, q % 2], recv[q, o], preferred_element_type=jnp.float32)
        h = jnp.dot(tw_ref[2 * o + q % 2], recv[q, o], preferred_element_type=jnp.float32)
        return g, h

    def step(k, carry, first=False):
        copies = []
        origins = []
        for q in range(4):
            dev, pos, sgn = flows[q]
            o = origin(q, k)
            cp = pltpu.make_async_remote_copy(
                src_ref=p_ref.at[q] if first else recv.at[q, o], dst_ref=recv.at[q, o],
                send_sem=ssem.at[q, k], recv_sem=rsem.at[q, k],
                device_id=(dev(pos + sgn + n), t), device_id_type=MESH)
            cp.start()
            copies.append(cp)
            origins.append(o)
        if first:
            for cp in own:
                cp.wait()
        parts = [contrib(q, origins[q]) for q in range(4)]
        g0 = parts[0][0] + parts[1][0]
        g1 = parts[2][0] + parts[3][0]
        h0 = parts[0][1] + parts[1][1]
        h1 = parts[2][1] + parts[3][1]

        @pl.when(k == 0)
        def _():
            acc[0] = g0
            acc[1] = g1
            pre[0] = h0
            pre[1] = h1

        @pl.when(k > 0)
        def _():
            acc[0] += g0
            acc[1] += g1
            pre[0] += h0
            pre[1] += h1

        for cp in copies:
            cp.wait()
        return carry

    step(0, 0, first=True)
    lax.fori_loop(1, n - 1, step, 0)
    parts = [contrib(q, origin(q, n - 1)) for q in range(4)]
    acc[0] += parts[0][0] + parts[1][0]
    acc[1] += parts[2][0] + parts[3][0]
    grown_ref[...] = acc[...].astype(grown_ref.dtype)
    gate = pre[0] + parts[0][1] + parts[1][1]
    up = pre[1] + parts[2][1] + parts[3][1]
    hid_ref[...] = (gate / (1.0 + jnp.exp(-gate)) * up).astype(hid_ref.dtype)


def _dp_ring(quarters, w3h, tw_blocks):
    n, _, rows, hb = w3h.shape
    _, _, cols = quarters.shape
    nt, tok, xw = tw_blocks.shape
    flops = 2 * 2 * rows * hb * 2 * cols * n + 2 * 2 * tok * xw * nt * cols
    return pl.pallas_call(
        functools.partial(_dp_ring_kernel, n),
        out_shape=(
            jax.ShapeDtypeStruct((2, rows, cols), jnp.bfloat16),
            jax.ShapeDtypeStruct((tok, cols), jnp.bfloat16),
        ),
        in_specs=[pl.BlockSpec(memory_space=pltpu.VMEM)] * 3,
        out_specs=(pl.BlockSpec(memory_space=pltpu.VMEM), pl.BlockSpec(memory_space=pltpu.VMEM)),
        scratch_shapes=[
            pltpu.VMEM((4, n, hb, cols), jnp.bfloat16),
            pltpu.VMEM((2, rows, cols), jnp.float32),
            pltpu.VMEM((2, tok, cols), jnp.float32),
            pltpu.SemaphoreType.DMA((4, n - 1)),
            pltpu.SemaphoreType.DMA((4, n - 1)),
            pltpu.SemaphoreType.DMA((4,)),
        ],
        compiler_params=pltpu.CompilerParams(
            collective_id=0, has_side_effects=True, vmem_limit_bytes=56 * 1024 * 1024),
        cost_estimate=pl.CostEstimate(
            flops=flops, transcendentals=tok * cols, bytes_accessed=4 * n * hb * cols * 2),
    )(quarters, w3h, tw_blocks)


def _tw_kernel(nt, nd, tok_ref, wcol_ref, out_ref, tbuf, wbuf, xbuf,
               ts_sem, tr_sem, ws_sem, wr_sem, xs_sem, xr_sem, l_sem):
    t = lax.axis_index("tensor")
    d = lax.axis_index("dp")
    rb = tok_ref.shape[1]

    barrier = pltpu.get_barrier_semaphore()

    def greet_t(j, c):
        pl.semaphore_signal(barrier, inc=1, device_id=(d, (t + j) % nt), device_id_type=MESH)
        return c

    def greet_d(j, c):
        pl.semaphore_signal(barrier, inc=1, device_id=((d + j) % nd, t), device_id_type=MESH)
        return c

    lax.fori_loop(1, nt, greet_t, 0)
    lax.fori_loop(1, nd, greet_d, 0)
    pl.semaphore_wait(barrier, nt - 1 + nd - 1)

    c0 = pltpu.make_async_copy(tok_ref, tbuf.at[t], l_sem.at[0])
    c1 = pltpu.make_async_copy(wcol_ref, wbuf.at[d], l_sem.at[1])
    c0.start()
    c1.start()

    def t_copy(p):
        return pltpu.make_async_remote_copy(
            src_ref=tok_ref, dst_ref=tbuf.at[t], send_sem=ts_sem.at[p], recv_sem=tr_sem.at[t],
            device_id=(d, p), device_id_type=MESH)

    def t_recv(p):
        return pltpu.make_async_remote_copy(
            src_ref=tok_ref, dst_ref=tbuf.at[p], send_sem=ts_sem.at[p], recv_sem=tr_sem.at[p],
            device_id=(d, p), device_id_type=MESH)

    def w_copy(p):
        return pltpu.make_async_remote_copy(
            src_ref=wcol_ref, dst_ref=wbuf.at[d], send_sem=ws_sem.at[p], recv_sem=wr_sem.at[d],
            device_id=(p, t), device_id_type=MESH)

    def w_recv(p):
        return pltpu.make_async_remote_copy(
            src_ref=wcol_ref, dst_ref=wbuf.at[p], send_sem=ws_sem.at[p], recv_sem=wr_sem.at[p],
            device_id=(p, t), device_id_type=MESH)

    def send_t(j, c):
        t_copy((t + j) % nt).start()
        return c

    def send_d(j, c):
        w_copy((d + j) % nd).start()
        return c

    lax.fori_loop(1, nt, send_t, 0)
    lax.fori_loop(1, nd, send_d, 0)

    def wait_t(j, c):
        p = (t + j) % nt
        t_copy(p).wait_send()
        t_recv(p).wait_recv()
        return c

    def wait_d(j, c):
        p = (d + j) % nd
        w_copy(p).wait_send()
        w_recv(p).wait_recv()
        return c

    lax.fori_loop(1, nt, wait_t, 0)
    lax.fori_loop(1, nd, wait_d, 0)
    c0.wait()
    c1.wait()

    per = nt // nd
    acc = None
    for q in range(nt):
        part = jnp.dot(tbuf[q], wbuf[q // per, pl.ds((q % per) * rb, rb), :],
                       preferred_element_type=jnp.float32)
        acc = part if acc is None else acc + part
    xbuf[t] = acc.astype(xbuf.dtype)

    def x_copy(p):
        return pltpu.make_async_remote_copy(
            src_ref=xbuf.at[t], dst_ref=xbuf.at[t], send_sem=xs_sem.at[p], recv_sem=xr_sem.at[t],
            device_id=(d, p), device_id_type=MESH)

    def x_recv(p):
        return pltpu.make_async_remote_copy(
            src_ref=xbuf.at[p], dst_ref=xbuf.at[p], send_sem=xs_sem.at[p], recv_sem=xr_sem.at[p],
            device_id=(d, p), device_id_type=MESH)

    def send_x(j, c):
        x_copy((t + j) % nt).start()
        return c

    def wait_x(j, c):
        p = (t + j) % nt
        x_copy(p).wait_send()
        x_recv(p).wait_recv()
        return c

    lax.fori_loop(1, nt, send_x, 0)
    lax.fori_loop(1, nt, wait_x, 0)
    out_ref[...] = xbuf[...]


def _tw(tokens, wcol, nt, nd):
    tok, rb = tokens.shape
    rows, xw = wcol.shape
    return pl.pallas_call(
        functools.partial(_tw_kernel, nt, nd),
        out_shape=jax.ShapeDtypeStruct((nt, tok, xw), jnp.bfloat16),
        in_specs=[pl.BlockSpec(memory_space=pltpu.VMEM)] * 2,
        out_specs=pl.BlockSpec(memory_space=pltpu.VMEM),
        scratch_shapes=[
            pltpu.VMEM((nt, tok, rb), jnp.bfloat16),
            pltpu.VMEM((nd, rows, xw), jnp.bfloat16),
            pltpu.VMEM((nt, tok, xw), jnp.bfloat16),
            pltpu.SemaphoreType.DMA((nt,)),
            pltpu.SemaphoreType.DMA((nt,)),
            pltpu.SemaphoreType.DMA((nd,)),
            pltpu.SemaphoreType.DMA((nd,)),
            pltpu.SemaphoreType.DMA((nt,)),
            pltpu.SemaphoreType.DMA((nt,)),
            pltpu.SemaphoreType.DMA((2,)),
        ],
        compiler_params=pltpu.CompilerParams(
            collective_id=1, has_side_effects=True, vmem_limit_bytes=32 * 1024 * 1024),
        cost_estimate=pl.CostEstimate(
            flops=2 * tok * rb * nt * xw, transcendentals=0,
            bytes_accessed=(nt * tok * rb + nd * rows * xw + 2 * nt * tok * xw) * 2),
    )(tokens, wcol)


def on_device(tokens, small_weights, ffn_growth, width_growth):
    n_t = lax.axis_size("tensor")
    n_d = lax.axis_size("dp")
    t = lax.axis_index("tensor")
    rows, ds = width_growth.shape
    xw = ds // n_t
    blk = ds // n_d
    w_cols = lax.dynamic_slice_in_dim(width_growth, t * xw, xw, axis=1)
    tw_blocks = _tw(tokens, w_cols, n_t, n_d)
    panels = jnp.einsum(
        "msf,cf->msc",
        lax.all_gather(small_weights, "tensor", axis=1, tiled=True),
        ffn_growth,
        preferred_element_type=jnp.float32,
    ).astype(jnp.bfloat16)
    hb = blk // 2
    w3h = width_growth.reshape(rows, n_d, 2, hb).transpose(1, 2, 0, 3)
    quarters = panels.reshape(4, hb, panels.shape[2])
    grown_weights, hidden = _dp_ring(quarters, w3h, tw_blocks)
    return (grown_weights, hidden)


def solution(mesh):
    placed = (P("dp", "tensor"), P(None, ("dp", "tensor"), None), P("tensor", None), P("dp", None))
    return jax.shard_map(
        on_device,
        mesh=mesh,
        in_specs=placed,
        out_specs=(P(None, "dp", "tensor"), P("dp", "tensor")),
        check_vma=False,
    )
```

```python
import functools

import jax
import jax.numpy as jnp
from jax import lax
from jax.experimental import pallas as pl
from jax.experimental.pallas import tpu as pltpu
from jax.sharding import PartitionSpec as P

MESH = pl.DeviceIdType.MESH


def _ring_pos(d):
    h = d // 4
    return h * 7 + (1 - 2 * h) * (d % 4)


def _ring_dev(p):
    h = p // 4
    return h * 4 + h * 3 + (1 - 2 * h) * (p % 4)


def _cross_pos(d):
    z = d % 4
    return 2 * z + (d // 4 + z) % 2


def _cross_dev(p):
    i = p // 2
    return ((i + p % 2) % 2) * 4 + i


def _flip_z(d, c):
    z = d % 4
    return d + c * (1 - 2 * (z % 2))


def _flip_y(d, c):
    y = d // 4
    return d + c * (1 - 2 * y) * 4


def _dp_ring_kernel(n, p_ref, w3_ref, tw_ref, grown_ref, hid_ref, recv, acc, pre, ssem, rsem, osem):
    t = lax.axis_index("tensor")
    d = lax.axis_index("dp")
    c = t % 2
    pos_a = _ring_pos(_flip_z(d, c))
    pos_b = _cross_pos(_flip_y(d, c))

    def dev_a(p):
        return _flip_z(_ring_dev(p % n), c)

    def dev_b(p):
        return _flip_y(_cross_dev(p % n), c)

    flows = [
        (dev_a, pos_a, 1),
        (dev_a, pos_a, -1),
        (dev_b, pos_b, 1),
        (dev_b, pos_b, -1),
    ]
    xw = tw_ref.shape[2]

    barrier = pltpu.get_barrier_semaphore()
    for dev, pos, sgn in flows:
        pl.semaphore_signal(barrier, inc=1, device_id=(dev(pos + sgn + n), t), device_id_type=MESH)
    pl.semaphore_wait(barrier, 4)

    own = []
    for q in range(4):
        cp = pltpu.make_async_copy(p_ref.at[q], recv.at[q, d], osem.at[q])
        cp.start()
        own.append(cp)
    for cp in own:
        cp.wait()

    def origin(q, k):
        dev, pos, sgn = flows[q]
        return dev(pos - sgn * k + n)

    def contrib(q, o):
        g = jnp.dot(w3_ref[o, q % 2], recv[q, o], preferred_element_type=jnp.float32)
        h = jnp.dot(tw_ref[(t - 2 * o - q % 2 + 2 * n) % tw_ref.shape[0]], recv[q, o],
                    preferred_element_type=jnp.float32)
        return g, h

    def step(k, carry):
        copies = []
        origins = []
        for q in range(4):
            dev, pos, sgn = flows[q]
            o = origin(q, k)
            cp = pltpu.make_async_remote_copy(
                src_ref=recv.at[q, o], dst_ref=recv.at[q, o],
                send_sem=ssem.at[q, k], recv_sem=rsem.at[q, k],
                device_id=(dev(pos + sgn + n), t), device_id_type=MESH)
            cp.start()
            copies.append(cp)
            origins.append(o)
        parts = [contrib(q, origins[q]) for q in range(4)]
        g0 = parts[0][0] + parts[1][0]
        g1 = parts[2][0] + parts[3][0]
        h0 = parts[0][1] + parts[1][1]
        h1 = parts[2][1] + parts[3][1]

        @pl.when(k == 0)
        def _():
            acc[0] = g0
            acc[1] = g1
            pre[0] = h0
            pre[1] = h1

        @pl.when(k > 0)
        def _():
            acc[0] += g0
            acc[1] += g1
            pre[0] += h0
            pre[1] += h1

        for cp in copies:
            cp.wait()
        return carry

    lax.fori_loop(0, n - 1, step, 0)
    parts = [contrib(q, origin(q, n - 1)) for q in range(4)]
    acc[0] += parts[0][0] + parts[1][0]
    acc[1] += parts[2][0] + parts[3][0]
    grown_ref[...] = acc[...].astype(grown_ref.dtype)
    gate = pre[0] + parts[0][1] + parts[1][1]
    up = pre[1] + parts[2][1] + parts[3][1]
    hid_ref[...] = (gate / (1.0 + jnp.exp(-gate)) * up).astype(hid_ref.dtype)


def _dp_ring(quarters, w3h, tw_blocks):
    n, _, rows, hb = w3h.shape
    _, _, cols = quarters.shape
    nt, tok, xw = tw_blocks.shape
    flops = 2 * 2 * rows * hb * 2 * cols * n + 2 * 2 * tok * xw * nt * cols
    return pl.pallas_call(
        functools.partial(_dp_ring_kernel, n),
        out_shape=(
            jax.ShapeDtypeStruct((2, rows, cols), jnp.bfloat16),
            jax.ShapeDtypeStruct((tok, cols), jnp.bfloat16),
        ),
        in_specs=[pl.BlockSpec(memory_space=pltpu.VMEM)] * 3,
        out_specs=(pl.BlockSpec(memory_space=pltpu.VMEM), pl.BlockSpec(memory_space=pltpu.VMEM)),
        scratch_shapes=[
            pltpu.VMEM((4, n, hb, cols), jnp.bfloat16),
            pltpu.VMEM((2, rows, cols), jnp.float32),
            pltpu.VMEM((2, tok, cols), jnp.float32),
            pltpu.SemaphoreType.DMA((4, n - 1)),
            pltpu.SemaphoreType.DMA((4, n - 1)),
            pltpu.SemaphoreType.DMA((4,)),
        ],
        compiler_params=pltpu.CompilerParams(
            collective_id=0, has_side_effects=True, vmem_limit_bytes=56 * 1024 * 1024),
        cost_estimate=pl.CostEstimate(
            flops=flops, transcendentals=tok * cols, bytes_accessed=4 * n * hb * cols * 2),
    )(quarters, w3h, tw_blocks)


def _wg_kernel(nd, wcol_ref, out_ref, wbuf, ws_sem, wr_sem, l_sem):
    t = lax.axis_index("tensor")
    d = lax.axis_index("dp")
    barrier = pltpu.get_barrier_semaphore()

    def greet_d(j, c):
        pl.semaphore_signal(barrier, inc=1, device_id=((d + j) % nd, t), device_id_type=MESH)
        return c

    lax.fori_loop(1, nd, greet_d, 0)
    pl.semaphore_wait(barrier, nd - 1)
    c1 = pltpu.make_async_copy(wcol_ref, wbuf.at[d], l_sem.at[0])
    c1.start()

    def w_copy(p):
        return pltpu.make_async_remote_copy(
            src_ref=wcol_ref, dst_ref=wbuf.at[d], send_sem=ws_sem.at[p], recv_sem=wr_sem.at[d],
            device_id=(p, t), device_id_type=MESH)

    def w_recv(p):
        return pltpu.make_async_remote_copy(
            src_ref=wcol_ref, dst_ref=wbuf.at[p], send_sem=ws_sem.at[p], recv_sem=wr_sem.at[p],
            device_id=(p, t), device_id_type=MESH)

    def send_d(j, c):
        w_copy((d + j) % nd).start()
        return c

    def wait_d(j, c):
        p = (d + j) % nd
        w_copy(p).wait_send()
        w_recv(p).wait_recv()
        return c

    lax.fori_loop(1, nd, send_d, 0)
    lax.fori_loop(1, nd, wait_d, 0)
    c1.wait()
    out_ref[...] = wbuf[...]


def _wg(wcol, nd):
    rows, xw = wcol.shape
    return pl.pallas_call(
        functools.partial(_wg_kernel, nd),
        out_shape=jax.ShapeDtypeStruct((nd, rows, xw), jnp.bfloat16),
        in_specs=[pl.BlockSpec(memory_space=pltpu.VMEM)],
        out_specs=pl.BlockSpec(memory_space=pltpu.VMEM),
        scratch_shapes=[
            pltpu.VMEM((nd, rows, xw), jnp.bfloat16),
            pltpu.SemaphoreType.DMA((nd,)),
            pltpu.SemaphoreType.DMA((nd,)),
            pltpu.SemaphoreType.DMA((1,)),
        ],
        compiler_params=pltpu.CompilerParams(
            collective_id=1, has_side_effects=True, vmem_limit_bytes=32 * 1024 * 1024),
        cost_estimate=pl.CostEstimate(
            flops=0, transcendentals=0, bytes_accessed=nd * rows * xw * 2 * 64),
    )(wcol)


def on_device(tokens, small_weights, ffn_growth, width_growth):
    n_t = lax.axis_size("tensor")
    n_d = lax.axis_size("dp")
    t = lax.axis_index("tensor")
    rows, ds = width_growth.shape
    xw = ds // n_t
    blk = ds // n_d
    w_cols = lax.dynamic_slice_in_dim(width_growth, t * xw, xw, axis=1)
    w_gath = _wg(w_cols, n_d)
    m, per_dev, fs = small_weights.shape
    tok, rb = tokens.shape
    t_rows = -(-tok * rb // fs)
    t_pad = jnp.pad(tokens.reshape(-1), (0, t_rows * fs - tok * rb)).reshape(t_rows, fs)
    ext = jnp.concatenate([small_weights.reshape(m * per_dev, fs), t_pad], axis=0)
    g = lax.all_gather(ext, "tensor", axis=0, tiled=False)
    s_part = g[:, : m * per_dev, :]
    t_full = g[:, m * per_dev:, :].reshape(n_t, t_rows * fs)[:, : tok * rb].reshape(n_t, tok, rb)
    t_row = t_full.transpose(1, 0, 2).reshape(tok, n_t * rb)
    tw_part = jnp.dot(t_row, w_gath.reshape(n_d * rows, xw), preferred_element_type=jnp.float32)
    tw_own = tw_part.astype(jnp.bfloat16)
    tw_blocks = tw_own[None]
    s = 1
    while s < n_t:
        got = lax.ppermute(tw_blocks, "tensor", perm=[(i, (i + s) % n_t) for i in range(n_t)])
        tw_blocks = jnp.concatenate([tw_blocks, got], axis=0)
        s *= 2
    p_dev = jnp.einsum(
        "kjf,cf->kjc", s_part, ffn_growth, preferred_element_type=jnp.float32
    ).astype(jnp.bfloat16)
    cols = p_dev.shape[2]
    panels = p_dev.reshape(n_t, m, per_dev, cols).transpose(1, 0, 2, 3).reshape(m, blk, cols)
    hb = blk // 2
    w3h = width_growth.reshape(rows, n_d, 2, hb).transpose(1, 2, 0, 3)
    quarters = panels.reshape(4, hb, cols)
    grown_weights, hidden = _dp_ring(quarters, w3h, tw_blocks)
    return (grown_weights, hidden)


def solution(mesh):
    placed = (P("dp", "tensor"), P(None, ("dp", "tensor"), None), P("tensor", None), P("dp", None))
    return jax.shard_map(
        on_device,
        mesh=mesh,
        in_specs=placed,
        out_specs=(P(None, "dp", "tensor"), P("dp", "tensor")),
        check_vma=False,
    )
```

```python
import functools

import jax
import jax.numpy as jnp
from jax import lax
from jax.experimental import pallas as pl
from jax.experimental.pallas import tpu as pltpu
from jax.sharding import PartitionSpec as P

MESH = pl.DeviceIdType.MESH


def _ring_pos(d):
    h = d // 4
    return h * 7 + (1 - 2 * h) * (d % 4)


def _ring_dev(p):
    h = p // 4
    return h * 4 + h * 3 + (1 - 2 * h) * (p % 4)


def _cross_pos(d):
    z = d % 4
    return 2 * z + (d // 4 + z) % 2


def _cross_dev(p):
    i = p // 2
    return ((i + p % 2) % 2) * 4 + i


def _flip_z(d, c):
    z = d % 4
    return d + c * (1 - 2 * (z % 2))


def _flip_y(d, c):
    y = d // 4
    return d + c * (1 - 2 * y) * 4


def _dp_ring_kernel(n, p_ref, w3_ref, tw_ref, grown_ref, hid_ref, recv, acc, pre, ssem, rsem, osem):
    t = lax.axis_index("tensor")
    d = lax.axis_index("dp")
    c = t % 2
    pos_a = _ring_pos(_flip_z(d, c))
    pos_b = _cross_pos(_flip_y(d, c))

    def dev_a(p):
        return _flip_z(_ring_dev(p % n), c)

    def dev_b(p):
        return _flip_y(_cross_dev(p % n), c)

    flows = [
        (dev_a, pos_a, 1),
        (dev_a, pos_a, -1),
        (dev_b, pos_b, 1),
        (dev_b, pos_b, -1),
    ]
    xw = tw_ref.shape[2]

    barrier = pltpu.get_barrier_semaphore()
    for dev, pos, sgn in flows:
        pl.semaphore_signal(barrier, inc=1, device_id=(dev(pos + sgn + n), t), device_id_type=MESH)
    pl.semaphore_wait(barrier, 4)

    own = []
    for q in range(4):
        cp = pltpu.make_async_copy(p_ref.at[q], recv.at[q, d], osem.at[q])
        cp.start()
        own.append(cp)
    for cp in own:
        cp.wait()

    def origin(q, k):
        dev, pos, sgn = flows[q]
        return dev(pos - sgn * k + n)

    def contrib(q, o):
        g = jnp.dot(w3_ref[o, q % 2], recv[q, o], preferred_element_type=jnp.float32)
        h = jnp.dot(tw_ref[(t - 2 * o - q % 2 + 2 * n) % tw_ref.shape[0]], recv[q, o],
                    preferred_element_type=jnp.float32)
        return g, h

    def step(k, carry):
        copies = []
        origins = []
        for q in range(4):
            dev, pos, sgn = flows[q]
            o = origin(q, k)
            cp = pltpu.make_async_remote_copy(
                src_ref=recv.at[q, o], dst_ref=recv.at[q, o],
                send_sem=ssem.at[q, k], recv_sem=rsem.at[q, k],
                device_id=(dev(pos + sgn + n), t), device_id_type=MESH)
            cp.start()
            copies.append(cp)
            origins.append(o)
        parts = [contrib(q, origins[q]) for q in range(4)]
        g0 = parts[0][0] + parts[1][0]
        g1 = parts[2][0] + parts[3][0]
        h0 = parts[0][1] + parts[1][1]
        h1 = parts[2][1] + parts[3][1]

        @pl.when(k == 0)
        def _():
            acc[0] = g0
            acc[1] = g1
            pre[0] = h0
            pre[1] = h1

        @pl.when(k > 0)
        def _():
            acc[0] += g0
            acc[1] += g1
            pre[0] += h0
            pre[1] += h1

        for cp in copies:
            cp.wait()
        return carry

    lax.fori_loop(0, n - 1, step, 0)
    parts = [contrib(q, origin(q, n - 1)) for q in range(4)]
    acc[0] += parts[0][0] + parts[1][0]
    acc[1] += parts[2][0] + parts[3][0]
    grown_ref[...] = acc[...].astype(grown_ref.dtype)
    gate = pre[0] + parts[0][1] + parts[1][1]
    up = pre[1] + parts[2][1] + parts[3][1]
    hid_ref[...] = (gate / (1.0 + jnp.exp(-gate)) * up).astype(hid_ref.dtype)


def _dp_ring(quarters, w3h, tw_blocks):
    n, _, rows, hb = w3h.shape
    _, _, cols = quarters.shape
    nt, tok, xw = tw_blocks.shape
    flops = 2 * 2 * rows * hb * 2 * cols * n + 2 * 2 * tok * xw * nt * cols
    return pl.pallas_call(
        functools.partial(_dp_ring_kernel, n),
        out_shape=(
            jax.ShapeDtypeStruct((2, rows, cols), jnp.bfloat16),
            jax.ShapeDtypeStruct((tok, cols), jnp.bfloat16),
        ),
        in_specs=[pl.BlockSpec(memory_space=pltpu.VMEM)] * 3,
        out_specs=(pl.BlockSpec(memory_space=pltpu.VMEM), pl.BlockSpec(memory_space=pltpu.VMEM)),
        scratch_shapes=[
            pltpu.VMEM((4, n, hb, cols), jnp.bfloat16),
            pltpu.VMEM((2, rows, cols), jnp.float32),
            pltpu.VMEM((2, tok, cols), jnp.float32),
            pltpu.SemaphoreType.DMA((4, n - 1)),
            pltpu.SemaphoreType.DMA((4, n - 1)),
            pltpu.SemaphoreType.DMA((4,)),
        ],
        compiler_params=pltpu.CompilerParams(
            collective_id=0, has_side_effects=True, vmem_limit_bytes=56 * 1024 * 1024),
        cost_estimate=pl.CostEstimate(
            flops=flops, transcendentals=tok * cols, bytes_accessed=4 * n * hb * cols * 2),
    )(quarters, w3h, tw_blocks)


def _tw_kernel(nt, nd, tok_ref, wcol_ref, out_ref, tbuf, wbuf, xbuf,
               ts_sem, tr_sem, ws_sem, wr_sem, xs_sem, xr_sem, l_sem):
    t = lax.axis_index("tensor")
    d = lax.axis_index("dp")
    rb = tok_ref.shape[1]
    shifts = []
    s = 1
    while s < nt:
        shifts.append(s)
        s *= 2
    peers = sorted({s for s in shifts} | {nt - s for s in shifts})

    barrier = pltpu.get_barrier_semaphore()
    for s in peers:
        pl.semaphore_signal(barrier, inc=1, device_id=(d, (t + s) % nt), device_id_type=MESH)

    def greet_d(j, c):
        pl.semaphore_signal(barrier, inc=1, device_id=((d + j) % nd, t), device_id_type=MESH)
        return c

    lax.fori_loop(1, nd, greet_d, 0)
    pl.semaphore_wait(barrier, len(peers) + nd - 1)

    c0 = pltpu.make_async_copy(tok_ref, tbuf.at[0], l_sem.at[0])
    c1 = pltpu.make_async_copy(wcol_ref, wbuf.at[d], l_sem.at[1])
    c0.start()
    c1.start()

    def w_copy(p):
        return pltpu.make_async_remote_copy(
            src_ref=wcol_ref, dst_ref=wbuf.at[d], send_sem=ws_sem.at[p], recv_sem=wr_sem.at[d],
            device_id=(p, t), device_id_type=MESH)

    def w_recv(p):
        return pltpu.make_async_remote_copy(
            src_ref=wcol_ref, dst_ref=wbuf.at[p], send_sem=ws_sem.at[p], recv_sem=wr_sem.at[p],
            device_id=(p, t), device_id_type=MESH)

    def send_d(j, c):
        w_copy((d + j) % nd).start()
        return c

    lax.fori_loop(1, nd, send_d, 0)
    c0.wait()

    def doubling(buf, s_sem, r_sem):
        for r, s in enumerate(shifts):
            cp = pltpu.make_async_remote_copy(
                src_ref=buf.at[pl.ds(0, s)], dst_ref=buf.at[pl.ds(s, s)],
                send_sem=s_sem.at[r], recv_sem=r_sem.at[r],
                device_id=(d, (t + s) % nt), device_id_type=MESH)
            cp.start()
            cp.wait()

    doubling(tbuf, ts_sem, tr_sem)

    def wait_d(j, c):
        p = (d + j) % nd
        w_copy(p).wait_send()
        w_recv(p).wait_recv()
        return c

    lax.fori_loop(1, nd, wait_d, 0)
    c1.wait()

    per = nt // nd
    acc = None
    for j in range(nt):
        q = (t - j + nt) % nt
        off = pl.multiple_of((q % per) * rb, rb)
        part = jnp.dot(tbuf[j], wbuf[q // per, pl.ds(off, rb), :],
                       preferred_element_type=jnp.float32)
        acc = part if acc is None else acc + part
    xbuf[0] = acc.astype(xbuf.dtype)
    doubling(xbuf, xs_sem, xr_sem)
    out_ref[...] = xbuf[...]


def _tw(tokens, wcol, nt, nd):
    tok, rb = tokens.shape
    rounds = max(1, (nt - 1).bit_length())
    rows, xw = wcol.shape
    return pl.pallas_call(
        functools.partial(_tw_kernel, nt, nd),
        out_shape=jax.ShapeDtypeStruct((nt, tok, xw), jnp.bfloat16),
        in_specs=[pl.BlockSpec(memory_space=pltpu.VMEM)] * 2,
        out_specs=pl.BlockSpec(memory_space=pltpu.VMEM),
        scratch_shapes=[
            pltpu.VMEM((nt, tok, rb), jnp.bfloat16),
            pltpu.VMEM((nd, rows, xw), jnp.bfloat16),
            pltpu.VMEM((nt, tok, xw), jnp.bfloat16),
            pltpu.SemaphoreType.DMA((rounds,)),
            pltpu.SemaphoreType.DMA((rounds,)),
            pltpu.SemaphoreType.DMA((nd,)),
            pltpu.SemaphoreType.DMA((nd,)),
            pltpu.SemaphoreType.DMA((rounds,)),
            pltpu.SemaphoreType.DMA((rounds,)),
            pltpu.SemaphoreType.DMA((2,)),
        ],
        compiler_params=pltpu.CompilerParams(
            collective_id=1, has_side_effects=True, vmem_limit_bytes=32 * 1024 * 1024),
        cost_estimate=pl.CostEstimate(
            flops=2 * tok * rb * nt * xw, transcendentals=0,
            bytes_accessed=(nt * tok * rb + nd * rows * xw + 2 * nt * tok * xw) * 2),
    )(tokens, wcol)


def on_device(tokens, small_weights, ffn_growth, width_growth):
    n_t = lax.axis_size("tensor")
    n_d = lax.axis_size("dp")
    t = lax.axis_index("tensor")
    rows, ds = width_growth.shape
    xw = ds // n_t
    blk = ds // n_d
    w_cols = lax.dynamic_slice_in_dim(width_growth, t * xw, xw, axis=1)
    tw_blocks = _tw(tokens, w_cols, n_t, n_d)
    panels = jnp.einsum(
        "msf,cf->msc",
        lax.all_gather(small_weights, "tensor", axis=1, tiled=True),
        ffn_growth,
        preferred_element_type=jnp.float32,
    ).astype(jnp.bfloat16)
    hb = blk // 2
    w3h = width_growth.reshape(rows, n_d, 2, hb).transpose(1, 2, 0, 3)
    quarters = panels.reshape(4, hb, panels.shape[2])
    grown_weights, hidden = _dp_ring(quarters, w3h, tw_blocks)
    return (grown_weights, hidden)


def solution(mesh):
    placed = (P("dp", "tensor"), P(None, ("dp", "tensor"), None), P("tensor", None), P("dp", None))
    return jax.shard_map(
        on_device,
        mesh=mesh,
        in_specs=placed,
        out_specs=(P(None, "dp", "tensor"), P("dp", "tensor")),
        check_vma=False,
    )
```

```python
import functools

import jax
import jax.numpy as jnp
from jax import lax
from jax.experimental import pallas as pl
from jax.experimental.pallas import tpu as pltpu
from jax.sharding import PartitionSpec as P

MESH = pl.DeviceIdType.MESH


def _ring_pos(d):
    h = d // 4
    return h * 7 + (1 - 2 * h) * (d % 4)


def _ring_dev(p):
    h = p // 4
    return h * 4 + h * 3 + (1 - 2 * h) * (p % 4)


def _cross_pos(d):
    z = d % 4
    return 2 * z + (d // 4 + z) % 2


def _cross_dev(p):
    i = p // 2
    return ((i + p % 2) % 2) * 4 + i


def _flip_z(d, c):
    z = d % 4
    return d + c * (1 - 2 * (z % 2))


def _flip_y(d, c):
    y = d // 4
    return d + c * (1 - 2 * y) * 4


def _dp_ring_kernel(n, p_ref, w3_ref, tw_ref, grown_ref, hid_ref, recv, acc, pre, ssem, rsem, osem):
    t = lax.axis_index("tensor")
    d = lax.axis_index("dp")
    c = t % 2
    pos_a = _ring_pos(_flip_z(d, c))
    pos_b = _cross_pos(_flip_y(d, c))

    def dev_a(p):
        return _flip_z(_ring_dev(p % n), c)

    def dev_b(p):
        return _flip_y(_cross_dev(p % n), c)

    flows = [
        (dev_a, pos_a, 1),
        (dev_a, pos_a, -1),
        (dev_b, pos_b, 1),
        (dev_b, pos_b, -1),
    ]
    xw = tw_ref.shape[2]

    barrier = pltpu.get_barrier_semaphore()
    for dev, pos, sgn in flows:
        pl.semaphore_signal(barrier, inc=1, device_id=(dev(pos + sgn + n), t), device_id_type=MESH)
    pl.semaphore_wait(barrier, 4)

    own = []
    for q in range(4):
        cp = pltpu.make_async_copy(p_ref.at[q], recv.at[q, d], osem.at[q])
        cp.start()
        own.append(cp)
    for cp in own:
        cp.wait()

    def origin(q, k):
        dev, pos, sgn = flows[q]
        return dev(pos - sgn * k + n)

    def contrib(q, o):
        g = jnp.dot(w3_ref[o, q % 2], recv[q, o], preferred_element_type=jnp.float32)
        h = jnp.dot(tw_ref[2 * o + q % 2], recv[q, o], preferred_element_type=jnp.float32)
        return g, h

    def step(k, carry):
        copies = []
        origins = []
        for q in range(4):
            dev, pos, sgn = flows[q]
            o = origin(q, k)
            cp = pltpu.make_async_remote_copy(
                src_ref=recv.at[q, o], dst_ref=recv.at[q, o],
                send_sem=ssem.at[q, k], recv_sem=rsem.at[q, k],
                device_id=(dev(pos + sgn + n), t), device_id_type=MESH)
            cp.start()
            copies.append(cp)
            origins.append(o)
        parts = [contrib(q, origins[q]) for q in range(4)]
        g0 = parts[0][0] + parts[1][0]
        g1 = parts[2][0] + parts[3][0]
        h0 = parts[0][1] + parts[1][1]
        h1 = parts[2][1] + parts[3][1]

        @pl.when(k == 0)
        def _():
            acc[0] = g0
            acc[1] = g1
            pre[0] = h0
            pre[1] = h1

        @pl.when(k > 0)
        def _():
            acc[0] += g0
            acc[1] += g1
            pre[0] += h0
            pre[1] += h1

        for cp in copies:
            cp.wait()
        return carry

    lax.fori_loop(0, n - 1, step, 0)
    parts = [contrib(q, origin(q, n - 1)) for q in range(4)]
    acc[0] += parts[0][0] + parts[1][0]
    acc[1] += parts[2][0] + parts[3][0]
    grown_ref[...] = acc[...].astype(grown_ref.dtype)
    gate = pre[0] + parts[0][1] + parts[1][1]
    up = pre[1] + parts[2][1] + parts[3][1]
    hid_ref[...] = (gate / (1.0 + jnp.exp(-gate)) * up).astype(hid_ref.dtype)


def _dp_ring(quarters, w3h, tw_blocks):
    n, _, rows, hb = w3h.shape
    _, _, cols = quarters.shape
    nt, tok, xw = tw_blocks.shape
    flops = 2 * 2 * rows * hb * 2 * cols * n + 2 * 2 * tok * xw * nt * cols
    return pl.pallas_call(
        functools.partial(_dp_ring_kernel, n),
        out_shape=(
            jax.ShapeDtypeStruct((2, rows, cols), jnp.bfloat16),
            jax.ShapeDtypeStruct((tok, cols), jnp.bfloat16),
        ),
        in_specs=[pl.BlockSpec(memory_space=pltpu.VMEM)] * 3,
        out_specs=(pl.BlockSpec(memory_space=pltpu.VMEM), pl.BlockSpec(memory_space=pltpu.VMEM)),
        scratch_shapes=[
            pltpu.VMEM((4, n, hb, cols), jnp.bfloat16),
            pltpu.VMEM((2, rows, cols), jnp.float32),
            pltpu.VMEM((2, tok, cols), jnp.float32),
            pltpu.SemaphoreType.DMA((4, n - 1)),
            pltpu.SemaphoreType.DMA((4, n - 1)),
            pltpu.SemaphoreType.DMA((4,)),
        ],
        compiler_params=pltpu.CompilerParams(
            collective_id=0, has_side_effects=True, vmem_limit_bytes=56 * 1024 * 1024),
        cost_estimate=pl.CostEstimate(
            flops=flops, transcendentals=tok * cols, bytes_accessed=4 * n * hb * cols * 2),
    )(quarters, w3h, tw_blocks)


def _tw_kernel(nt, nd, tok_ref, wcol_ref, out_ref, tbuf, wbuf, xbuf,
               ts_sem, tr_sem, ws_sem, wr_sem, xs_sem, xr_sem, l_sem):
    t = lax.axis_index("tensor")
    d = lax.axis_index("dp")
    rb = tok_ref.shape[1]

    barrier = pltpu.get_barrier_semaphore()

    def greet_t(j, c):
        pl.semaphore_signal(barrier, inc=1, device_id=(d, (t + j) % nt), device_id_type=MESH)
        return c

    def greet_d(j, c):
        pl.semaphore_signal(barrier, inc=1, device_id=((d + j) % nd, t), device_id_type=MESH)
        return c

    lax.fori_loop(1, nt, greet_t, 0)
    lax.fori_loop(1, nd, greet_d, 0)
    pl.semaphore_wait(barrier, nt - 1 + nd - 1)

    c0 = pltpu.make_async_copy(tok_ref, tbuf.at[t], l_sem.at[0])
    c1 = pltpu.make_async_copy(wcol_ref, wbuf.at[d], l_sem.at[1])
    c0.start()
    c1.start()

    def t_copy(p):
        return pltpu.make_async_remote_copy(
            src_ref=tok_ref, dst_ref=tbuf.at[t], send_sem=ts_sem.at[p], recv_sem=tr_sem.at[t],
            device_id=(d, p), device_id_type=MESH)

    def t_recv(p):
        return pltpu.make_async_remote_copy(
            src_ref=tok_ref, dst_ref=tbuf.at[p], send_sem=ts_sem.at[p], recv_sem=tr_sem.at[p],
            device_id=(d, p), device_id_type=MESH)

    def w_copy(p):
        return pltpu.make_async_remote_copy(
            src_ref=wcol_ref, dst_ref=wbuf.at[d], send_sem=ws_sem.at[p], recv_sem=wr_sem.at[d],
            device_id=(p, t), device_id_type=MESH)

    def w_recv(p):
        return pltpu.make_async_remote_copy(
            src_ref=wcol_ref, dst_ref=wbuf.at[p], send_sem=ws_sem.at[p], recv_sem=wr_sem.at[p],
            device_id=(p, t), device_id_type=MESH)

    def send_t(j, c):
        t_copy((t + j) % nt).start()
        return c

    def send_d(j, c):
        w_copy((d + j) % nd).start()
        return c

    lax.fori_loop(1, nt, send_t, 0)
    lax.fori_loop(1, nd, send_d, 0)

    def wait_t(j, c):
        p = (t + j) % nt
        t_copy(p).wait_send()
        t_recv(p).wait_recv()
        return c

    def wait_d(j, c):
        p = (d + j) % nd
        w_copy(p).wait_send()
        w_recv(p).wait_recv()
        return c

    lax.fori_loop(1, nt, wait_t, 0)
    lax.fori_loop(1, nd, wait_d, 0)
    c0.wait()
    c1.wait()

    per = nt // nd
    acc = None
    for q in range(nt):
        part = jnp.dot(tbuf[q], wbuf[q // per, pl.ds((q % per) * rb, rb), :],
                       preferred_element_type=jnp.float32)
        acc = part if acc is None else acc + part
    xbuf[t] = acc.astype(xbuf.dtype)

    def x_copy(p):
        return pltpu.make_async_remote_copy(
            src_ref=xbuf.at[t], dst_ref=xbuf.at[t], send_sem=xs_sem.at[p], recv_sem=xr_sem.at[t],
            device_id=(d, p), device_id_type=MESH)

    def x_recv(p):
        return pltpu.make_async_remote_copy(
            src_ref=xbuf.at[p], dst_ref=xbuf.at[p], send_sem=xs_sem.at[p], recv_sem=xr_sem.at[p],
            device_id=(d, p), device_id_type=MESH)

    def send_x(j, c):
        x_copy((t + j) % nt).start()
        return c

    def wait_x(j, c):
        p = (t + j) % nt
        x_copy(p).wait_send()
        x_recv(p).wait_recv()
        return c

    lax.fori_loop(1, nt, send_x, 0)
    lax.fori_loop(1, nt, wait_x, 0)
    out_ref[...] = xbuf[...]


def _tw(tokens, wcol, nt, nd):
    tok, rb = tokens.shape
    rows, xw = wcol.shape
    return pl.pallas_call(
        functools.partial(_tw_kernel, nt, nd),
        out_shape=jax.ShapeDtypeStruct((nt, tok, xw), jnp.bfloat16),
        in_specs=[pl.BlockSpec(memory_space=pltpu.VMEM)] * 2,
        out_specs=pl.BlockSpec(memory_space=pltpu.VMEM),
        scratch_shapes=[
            pltpu.VMEM((nt, tok, rb), jnp.bfloat16),
            pltpu.VMEM((nd, rows, xw), jnp.bfloat16),
            pltpu.VMEM((nt, tok, xw), jnp.bfloat16),
            pltpu.SemaphoreType.DMA((nt,)),
            pltpu.SemaphoreType.DMA((nt,)),
            pltpu.SemaphoreType.DMA((nd,)),
            pltpu.SemaphoreType.DMA((nd,)),
            pltpu.SemaphoreType.DMA((nt,)),
            pltpu.SemaphoreType.DMA((nt,)),
            pltpu.SemaphoreType.DMA((2,)),
        ],
        compiler_params=pltpu.CompilerParams(
            collective_id=1, has_side_effects=True, vmem_limit_bytes=32 * 1024 * 1024),
        cost_estimate=pl.CostEstimate(
            flops=2 * tok * rb * nt * xw, transcendentals=0,
            bytes_accessed=(nt * tok * rb + nd * rows * xw + 2 * nt * tok * xw) * 2),
    )(tokens, wcol)


def on_device(tokens, small_weights, ffn_growth, width_growth):
    n_t = lax.axis_size("tensor")
    n_d = lax.axis_size("dp")
    t = lax.axis_index("tensor")
    rows, ds = width_growth.shape
    xw = ds // n_t
    blk = ds // n_d
    w_cols = lax.dynamic_slice_in_dim(width_growth, t * xw, xw, axis=1)
    tw_blocks = _tw(tokens, w_cols, n_t, n_d)
    m, per_dev, fs = small_weights.shape
    s_dev = lax.all_gather(small_weights.reshape(m * per_dev, fs), "tensor", axis=0, tiled=False)
    p_dev = jnp.einsum(
        "kjf,cf->kjc", s_dev, ffn_growth, preferred_element_type=jnp.float32
    ).astype(jnp.bfloat16)
    cols_p = p_dev.shape[2]
    panels = p_dev.reshape(n_t, m, per_dev, cols_p).transpose(1, 0, 2, 3).reshape(m, blk, cols_p)
    hb = blk // 2
    w3h = width_growth.reshape(rows, n_d, 2, hb).transpose(1, 2, 0, 3)
    quarters = panels.reshape(4, hb, panels.shape[2])
    grown_weights, hidden = _dp_ring(quarters, w3h, tw_blocks)
    return (grown_weights, hidden)


def solution(mesh):
    placed = (P("dp", "tensor"), P(None, ("dp", "tensor"), None), P("tensor", None), P("dp", None))
    return jax.shard_map(
        on_device,
        mesh=mesh,
        in_specs=placed,
        out_specs=(P(None, "dp", "tensor"), P("dp", "tensor")),
        check_vma=False,
    )
```

```python
import functools

import jax
import jax.numpy as jnp
from jax import lax
from jax.experimental import pallas as pl
from jax.experimental.pallas import tpu as pltpu
from jax.sharding import PartitionSpec as P

MESH = pl.DeviceIdType.MESH


def _ring_pos(d):
    h = d // 4
    return h * 7 + (1 - 2 * h) * (d % 4)


def _ring_dev(p):
    h = p // 4
    return h * 4 + h * 3 + (1 - 2 * h) * (p % 4)


def _cross_pos(d):
    z = d % 4
    return 2 * z + (d // 4 + z) % 2


def _cross_dev(p):
    i = p // 2
    return ((i + p % 2) % 2) * 4 + i


def _flip_z(d, c):
    z = d % 4
    return d + c * (1 - 2 * (z % 2))


def _flip_y(d, c):
    y = d // 4
    return d + c * (1 - 2 * y) * 4


def _dp_ring_kernel(n, p_ref, w3_ref, tw_ref, grown_ref, hid_ref, recv, acc, pre, ssem, rsem, osem):
    t = lax.axis_index("tensor")
    d = lax.axis_index("dp")
    c = t % 2
    pos_a = _ring_pos(_flip_z(d, c))
    pos_b = _cross_pos(_flip_y(d, c))

    def dev_a(p):
        return _flip_z(_ring_dev(p % n), c)

    def dev_b(p):
        return _flip_y(_cross_dev(p % n), c)

    flows = [
        (dev_a, pos_a, 1),
        (dev_a, pos_a, -1),
        (dev_b, pos_b, 1),
        (dev_b, pos_b, -1),
    ]
    xw = tw_ref.shape[2]

    barrier = pltpu.get_barrier_semaphore()
    for dev, pos, sgn in flows:
        pl.semaphore_signal(barrier, inc=1, device_id=(dev(pos + sgn + n), t), device_id_type=MESH)
    pl.semaphore_wait(barrier, 4)

    own = []
    for q in range(4):
        cp = pltpu.make_async_copy(p_ref.at[q], recv.at[q, d], osem.at[q])
        cp.start()
        own.append(cp)
    for cp in own:
        cp.wait()

    def origin(q, k):
        dev, pos, sgn = flows[q]
        return dev(pos - sgn * k + n)

    def contrib(q, o):
        g = jnp.dot(w3_ref[o, q % 2], recv[q, o], preferred_element_type=jnp.float32)
        h = jnp.dot(tw_ref[2 * o + q % 2], recv[q, o], preferred_element_type=jnp.float32)
        return g, h

    def step(k, carry):
        copies = []
        origins = []
        for q in range(4):
            dev, pos, sgn = flows[q]
            o = origin(q, k)
            cp = pltpu.make_async_remote_copy(
                src_ref=recv.at[q, o], dst_ref=recv.at[q, o],
                send_sem=ssem.at[q, k], recv_sem=rsem.at[q, k],
                device_id=(dev(pos + sgn + n), t), device_id_type=MESH)
            cp.start()
            copies.append(cp)
            origins.append(o)
        parts = [contrib(q, origins[q]) for q in range(4)]
        g0 = parts[0][0] + parts[1][0]
        g1 = parts[2][0] + parts[3][0]
        h0 = parts[0][1] + parts[1][1]
        h1 = parts[2][1] + parts[3][1]

        @pl.when(k == 0)
        def _():
            acc[0] = g0
            acc[1] = g1
            pre[0] = h0
            pre[1] = h1

        @pl.when(k > 0)
        def _():
            acc[0] += g0
            acc[1] += g1
            pre[0] += h0
            pre[1] += h1

        for cp in copies:
            cp.wait()
        return carry

    lax.fori_loop(0, n - 1, step, 0)
    parts = [contrib(q, origin(q, n - 1)) for q in range(4)]
    acc[0] += parts[0][0] + parts[1][0]
    acc[1] += parts[2][0] + parts[3][0]
    grown_ref[...] = acc[...].astype(grown_ref.dtype)
    gate = pre[0] + parts[0][1] + parts[1][1]
    up = pre[1] + parts[2][1] + parts[3][1]
    hid_ref[...] = (gate / (1.0 + jnp.exp(-gate)) * up).astype(hid_ref.dtype)


def _dp_ring(quarters, w3h, tw_blocks):
    n, _, rows, hb = w3h.shape
    _, _, cols = quarters.shape
    nt, tok, xw = tw_blocks.shape
    flops = 2 * 2 * rows * hb * 2 * cols * n + 2 * 2 * tok * xw * nt * cols
    return pl.pallas_call(
        functools.partial(_dp_ring_kernel, n),
        out_shape=(
            jax.ShapeDtypeStruct((2, rows, cols), jnp.bfloat16),
            jax.ShapeDtypeStruct((tok, cols), jnp.bfloat16),
        ),
        in_specs=[pl.BlockSpec(memory_space=pltpu.VMEM)] * 3,
        out_specs=(pl.BlockSpec(memory_space=pltpu.VMEM), pl.BlockSpec(memory_space=pltpu.VMEM)),
        scratch_shapes=[
            pltpu.VMEM((4, n, hb, cols), jnp.bfloat16),
            pltpu.VMEM((2, rows, cols), jnp.float32),
            pltpu.VMEM((2, tok, cols), jnp.float32),
            pltpu.SemaphoreType.DMA((4, n - 1)),
            pltpu.SemaphoreType.DMA((4, n - 1)),
            pltpu.SemaphoreType.DMA((4,)),
        ],
        compiler_params=pltpu.CompilerParams(
            collective_id=0, has_side_effects=True, vmem_limit_bytes=56 * 1024 * 1024),
        cost_estimate=pl.CostEstimate(
            flops=flops, transcendentals=tok * cols, bytes_accessed=4 * n * hb * cols * 2),
    )(quarters, w3h, tw_blocks)


def _tw_kernel(nt, nd, tok_ref, wcol_ref, out_ref, tbuf, wbuf, xbuf,
               ts_sem, tr_sem, ws_sem, wr_sem, xs_sem, xr_sem, l_sem):
    t = lax.axis_index("tensor")
    d = lax.axis_index("dp")
    rb = tok_ref.shape[1]

    barrier = pltpu.get_barrier_semaphore()

    def greet_t(j, c):
        pl.semaphore_signal(barrier, inc=1, device_id=(d, (t + j) % nt), device_id_type=MESH)
        return c

    def greet_d(j, c):
        pl.semaphore_signal(barrier, inc=1, device_id=((d + j) % nd, t), device_id_type=MESH)
        return c

    lax.fori_loop(1, nt, greet_t, 0)
    lax.fori_loop(1, nd, greet_d, 0)
    pl.semaphore_wait(barrier, nt - 1 + nd - 1)

    c0 = pltpu.make_async_copy(tok_ref, tbuf.at[t], l_sem.at[0])
    c1 = pltpu.make_async_copy(wcol_ref, wbuf.at[d], l_sem.at[1])
    c0.start()
    c1.start()

    def t_copy(p):
        return pltpu.make_async_remote_copy(
            src_ref=tok_ref, dst_ref=tbuf.at[t], send_sem=ts_sem.at[p], recv_sem=tr_sem.at[t],
            device_id=(d, p), device_id_type=MESH)

    def t_recv(p):
        return pltpu.make_async_remote_copy(
            src_ref=tok_ref, dst_ref=tbuf.at[p], send_sem=ts_sem.at[p], recv_sem=tr_sem.at[p],
            device_id=(d, p), device_id_type=MESH)

    def w_copy(p):
        return pltpu.make_async_remote_copy(
            src_ref=wcol_ref, dst_ref=wbuf.at[d], send_sem=ws_sem.at[p], recv_sem=wr_sem.at[d],
            device_id=(p, t), device_id_type=MESH)

    def w_recv(p):
        return pltpu.make_async_remote_copy(
            src_ref=wcol_ref, dst_ref=wbuf.at[p], send_sem=ws_sem.at[p], recv_sem=wr_sem.at[p],
            device_id=(p, t), device_id_type=MESH)

    def send_t(j, c):
        t_copy((t + j) % nt).start()
        return c

    def send_d(j, c):
        w_copy((d + j) % nd).start()
        return c

    lax.fori_loop(1, nt, send_t, 0)
    lax.fori_loop(1, nd, send_d, 0)

    def wait_t(j, c):
        p = (t + j) % nt
        t_copy(p).wait_send()
        t_recv(p).wait_recv()
        return c

    def wait_d(j, c):
        p = (d + j) % nd
        w_copy(p).wait_send()
        w_recv(p).wait_recv()
        return c

    lax.fori_loop(1, nt, wait_t, 0)
    lax.fori_loop(1, nd, wait_d, 0)
    c0.wait()
    c1.wait()

    per = nt // nd
    acc = None
    for q in range(nt):
        part = jnp.dot(tbuf[q], wbuf[q // per, pl.ds((q % per) * rb, rb), :],
                       preferred_element_type=jnp.float32)
        acc = part if acc is None else acc + part
    xbuf[t] = acc.astype(xbuf.dtype)

    def x_copy(p):
        return pltpu.make_async_remote_copy(
            src_ref=xbuf.at[t], dst_ref=xbuf.at[t], send_sem=xs_sem.at[p], recv_sem=xr_sem.at[t],
            device_id=(d, p), device_id_type=MESH)

    def x_recv(p):
        return pltpu.make_async_remote_copy(
            src_ref=xbuf.at[p], dst_ref=xbuf.at[p], send_sem=xs_sem.at[p], recv_sem=xr_sem.at[p],
            device_id=(d, p), device_id_type=MESH)

    def send_x(j, c):
        x_copy((t + j) % nt).start()
        return c

    def wait_x(j, c):
        p = (t + j) % nt
        x_copy(p).wait_send()
        x_recv(p).wait_recv()
        return c

    lax.fori_loop(1, nt, send_x, 0)
    lax.fori_loop(1, nt, wait_x, 0)
    out_ref[...] = xbuf[...]


def _tw(tokens, wcol, nt, nd):
    tok, rb = tokens.shape
    rows, xw = wcol.shape
    return pl.pallas_call(
        functools.partial(_tw_kernel, nt, nd),
        out_shape=jax.ShapeDtypeStruct((nt, tok, xw), jnp.bfloat16),
        in_specs=[pl.BlockSpec(memory_space=pltpu.VMEM)] * 2,
        out_specs=pl.BlockSpec(memory_space=pltpu.VMEM),
        scratch_shapes=[
            pltpu.VMEM((nt, tok, rb), jnp.bfloat16),
            pltpu.VMEM((nd, rows, xw), jnp.bfloat16),
            pltpu.VMEM((nt, tok, xw), jnp.bfloat16),
            pltpu.SemaphoreType.DMA((nt,)),
            pltpu.SemaphoreType.DMA((nt,)),
            pltpu.SemaphoreType.DMA((nd,)),
            pltpu.SemaphoreType.DMA((nd,)),
            pltpu.SemaphoreType.DMA((nt,)),
            pltpu.SemaphoreType.DMA((nt,)),
            pltpu.SemaphoreType.DMA((2,)),
        ],
        compiler_params=pltpu.CompilerParams(
            collective_id=1, has_side_effects=True, vmem_limit_bytes=32 * 1024 * 1024),
        cost_estimate=pl.CostEstimate(
            flops=2 * tok * rb * nt * xw, transcendentals=0,
            bytes_accessed=(nt * tok * rb + nd * rows * xw + 2 * nt * tok * xw) * 2),
    )(tokens, wcol)


def on_device(tokens, small_weights, ffn_growth, width_growth):
    n_t = lax.axis_size("tensor")
    n_d = lax.axis_size("dp")
    t = lax.axis_index("tensor")
    rows, ds = width_growth.shape
    xw = ds // n_t
    blk = ds // n_d
    w_cols = lax.dynamic_slice_in_dim(width_growth, t * xw, xw, axis=1)
    tw_blocks = _tw(tokens, w_cols, n_t, n_d)
    s_rows = lax.all_gather(small_weights.transpose(1, 0, 2), "tensor", axis=0, tiled=True)
    panels = jnp.einsum(
        "smf,cf->msc", s_rows, ffn_growth, preferred_element_type=jnp.float32
    ).astype(jnp.bfloat16)
    hb = blk // 2
    w3h = width_growth.reshape(rows, n_d, 2, hb).transpose(1, 2, 0, 3)
    quarters = panels.reshape(4, hb, panels.shape[2])
    grown_weights, hidden = _dp_ring(quarters, w3h, tw_blocks)
    return (grown_weights, hidden)


def solution(mesh):
    placed = (P("dp", "tensor"), P(None, ("dp", "tensor"), None), P("tensor", None), P("dp", None))
    return jax.shard_map(
        on_device,
        mesh=mesh,
        in_specs=placed,
        out_specs=(P(None, "dp", "tensor"), P("dp", "tensor")),
        check_vma=False,
    )
```

```python
import functools

import jax
import jax.numpy as jnp
from jax import lax
from jax.experimental import pallas as pl
from jax.experimental.pallas import tpu as pltpu
from jax.sharding import PartitionSpec as P

MESH = pl.DeviceIdType.MESH


def _ring_pos(d):
    h = d // 4
    return h * 7 + (1 - 2 * h) * (d % 4)


def _ring_dev(p):
    h = p // 4
    return h * 4 + h * 3 + (1 - 2 * h) * (p % 4)


def _cross_pos(d):
    z = d % 4
    return 2 * z + (d // 4 + z) % 2


def _cross_dev(p):
    i = p // 2
    return ((i + p % 2) % 2) * 4 + i


def _flip_z(d, c):
    z = d % 4
    return d + c * (1 - 2 * (z % 2))


def _flip_y(d, c):
    y = d // 4
    return d + c * (1 - 2 * y) * 4


def _dp_ring_kernel(n, p_ref, w3_ref, tw_ref, grown_ref, hid_ref, recv, acc, pre, ssem, rsem, osem):
    t = lax.axis_index("tensor")
    d = lax.axis_index("dp")
    c = t % 2
    pos_a = _ring_pos(_flip_z(d, c))
    pos_b = _cross_pos(_flip_y(d, c))

    def dev_a(p):
        return _flip_z(_ring_dev(p % n), c)

    def dev_b(p):
        return _flip_y(_cross_dev(p % n), c)

    flows = [
        (dev_a, pos_a, 1),
        (dev_a, pos_a, -1),
        (dev_b, pos_b, 1),
        (dev_b, pos_b, -1),
    ]
    xw = tw_ref.shape[2]

    barrier = pltpu.get_barrier_semaphore()
    for dev, pos, sgn in flows:
        pl.semaphore_signal(barrier, inc=1, device_id=(dev(pos + sgn + n), t), device_id_type=MESH)
    pl.semaphore_wait(barrier, 4)

    own = []
    for q in range(4):
        cp = pltpu.make_async_copy(p_ref.at[q], recv.at[q, d], osem.at[q])
        cp.start()
        own.append(cp)
    for cp in own:
        cp.wait()

    def origin(q, k):
        dev, pos, sgn = flows[q]
        return dev(pos - sgn * k + n)

    def contrib(q, o):
        g = jnp.dot(w3_ref[o, q % 2], recv[q, o], preferred_element_type=jnp.float32)
        h = jnp.dot(tw_ref[2 * o + q % 2], recv[q, o], preferred_element_type=jnp.float32)
        return g, h

    def step(k, carry):
        copies = []
        origins = []
        for q in range(4):
            dev, pos, sgn = flows[q]
            o = origin(q, k)
            cp = pltpu.make_async_remote_copy(
                src_ref=recv.at[q, o], dst_ref=recv.at[q, o],
                send_sem=ssem.at[q, k], recv_sem=rsem.at[q, k],
                device_id=(dev(pos + sgn + n), t), device_id_type=MESH)
            cp.start()
            copies.append(cp)
            origins.append(o)
        parts = [contrib(q, origins[q]) for q in range(4)]
        g0 = parts[0][0] + parts[1][0]
        g1 = parts[2][0] + parts[3][0]
        h0 = parts[0][1] + parts[1][1]
        h1 = parts[2][1] + parts[3][1]

        @pl.when(k == 0)
        def _():
            acc[0] = g0
            acc[1] = g1
            pre[0] = h0
            pre[1] = h1

        @pl.when(k > 0)
        def _():
            acc[0] += g0
            acc[1] += g1
            pre[0] += h0
            pre[1] += h1

        for cp in copies:
            cp.wait()
        return carry

    lax.fori_loop(0, n - 1, step, 0)
    parts = [contrib(q, origin(q, n - 1)) for q in range(4)]
    acc[0] += parts[0][0] + parts[1][0]
    acc[1] += parts[2][0] + parts[3][0]
    for mm in range(2):
        grown_ref[mm] = acc[mm].T.astype(grown_ref.dtype)
    gate = pre[0] + parts[0][1] + parts[1][1]
    up = pre[1] + parts[2][1] + parts[3][1]
    hid_ref[...] = (gate / (1.0 + jnp.exp(-gate)) * up).T.astype(hid_ref.dtype)


def _dp_ring(quarters, w3h, tw_blocks):
    n, _, rows, hb = w3h.shape
    _, _, cols = quarters.shape
    nt, tok, xw = tw_blocks.shape
    flops = 2 * 2 * rows * hb * 2 * cols * n + 2 * 2 * tok * xw * nt * cols
    return pl.pallas_call(
        functools.partial(_dp_ring_kernel, n),
        out_shape=(
            jax.ShapeDtypeStruct((2, cols, rows), jnp.bfloat16),
            jax.ShapeDtypeStruct((cols, tok), jnp.bfloat16),
        ),
        in_specs=[pl.BlockSpec(memory_space=pltpu.VMEM)] * 3,
        out_specs=(pl.BlockSpec(memory_space=pltpu.VMEM), pl.BlockSpec(memory_space=pltpu.VMEM)),
        scratch_shapes=[
            pltpu.VMEM((4, n, hb, cols), jnp.bfloat16),
            pltpu.VMEM((2, rows, cols), jnp.float32),
            pltpu.VMEM((2, tok, cols), jnp.float32),
            pltpu.SemaphoreType.DMA((4, n - 1)),
            pltpu.SemaphoreType.DMA((4, n - 1)),
            pltpu.SemaphoreType.DMA((4,)),
        ],
        compiler_params=pltpu.CompilerParams(
            collective_id=0, has_side_effects=True, vmem_limit_bytes=56 * 1024 * 1024),
        cost_estimate=pl.CostEstimate(
            flops=flops, transcendentals=tok * cols, bytes_accessed=4 * n * hb * cols * 2),
    )(quarters, w3h, tw_blocks)


def _tw_kernel(nt, nd, tok_ref, wcol_ref, out_ref, tbuf, wbuf, xbuf,
               ts_sem, tr_sem, ws_sem, wr_sem, xs_sem, xr_sem, l_sem):
    t = lax.axis_index("tensor")
    d = lax.axis_index("dp")
    rb = tok_ref.shape[1]

    barrier = pltpu.get_barrier_semaphore()

    def greet_t(j, c):
        pl.semaphore_signal(barrier, inc=1, device_id=(d, (t + j) % nt), device_id_type=MESH)
        return c

    def greet_d(j, c):
        pl.semaphore_signal(barrier, inc=1, device_id=((d + j) % nd, t), device_id_type=MESH)
        return c

    lax.fori_loop(1, nt, greet_t, 0)
    lax.fori_loop(1, nd, greet_d, 0)
    pl.semaphore_wait(barrier, nt - 1 + nd - 1)

    c0 = pltpu.make_async_copy(tok_ref, tbuf.at[t], l_sem.at[0])
    c1 = pltpu.make_async_copy(wcol_ref, wbuf.at[d], l_sem.at[1])
    c0.start()
    c1.start()

    def t_copy(p):
        return pltpu.make_async_remote_copy(
            src_ref=tok_ref, dst_ref=tbuf.at[t], send_sem=ts_sem.at[p], recv_sem=tr_sem.at[t],
            device_id=(d, p), device_id_type=MESH)

    def t_recv(p):
        return pltpu.make_async_remote_copy(
            src_ref=tok_ref, dst_ref=tbuf.at[p], send_sem=ts_sem.at[p], recv_sem=tr_sem.at[p],
            device_id=(d, p), device_id_type=MESH)

    def w_copy(p):
        return pltpu.make_async_remote_copy(
            src_ref=wcol_ref, dst_ref=wbuf.at[d], send_sem=ws_sem.at[p], recv_sem=wr_sem.at[d],
            device_id=(p, t), device_id_type=MESH)

    def w_recv(p):
        return pltpu.make_async_remote_copy(
            src_ref=wcol_ref, dst_ref=wbuf.at[p], send_sem=ws_sem.at[p], recv_sem=wr_sem.at[p],
            device_id=(p, t), device_id_type=MESH)

    def send_t(j, c):
        t_copy((t + j) % nt).start()
        return c

    def send_d(j, c):
        w_copy((d + j) % nd).start()
        return c

    lax.fori_loop(1, nt, send_t, 0)
    lax.fori_loop(1, nd, send_d, 0)

    def wait_t(j, c):
        p = (t + j) % nt
        t_copy(p).wait_send()
        t_recv(p).wait_recv()
        return c

    def wait_d(j, c):
        p = (d + j) % nd
        w_copy(p).wait_send()
        w_recv(p).wait_recv()
        return c

    lax.fori_loop(1, nt, wait_t, 0)
    lax.fori_loop(1, nd, wait_d, 0)
    c0.wait()
    c1.wait()

    per = nt // nd
    acc = None
    for q in range(nt):
        part = jnp.dot(tbuf[q], wbuf[q // per, pl.ds((q % per) * rb, rb), :],
                       preferred_element_type=jnp.float32)
        acc = part if acc is None else acc + part
    xbuf[t] = acc.astype(xbuf.dtype)

    def x_copy(p):
        return pltpu.make_async_remote_copy(
            src_ref=xbuf.at[t], dst_ref=xbuf.at[t], send_sem=xs_sem.at[p], recv_sem=xr_sem.at[t],
            device_id=(d, p), device_id_type=MESH)

    def x_recv(p):
        return pltpu.make_async_remote_copy(
            src_ref=xbuf.at[p], dst_ref=xbuf.at[p], send_sem=xs_sem.at[p], recv_sem=xr_sem.at[p],
            device_id=(d, p), device_id_type=MESH)

    def send_x(j, c):
        x_copy((t + j) % nt).start()
        return c

    def wait_x(j, c):
        p = (t + j) % nt
        x_copy(p).wait_send()
        x_recv(p).wait_recv()
        return c

    lax.fori_loop(1, nt, send_x, 0)
    lax.fori_loop(1, nt, wait_x, 0)
    out_ref[...] = xbuf[...]


def _tw(tokens, wcol, nt, nd):
    tok, rb = tokens.shape
    rows, xw = wcol.shape
    return pl.pallas_call(
        functools.partial(_tw_kernel, nt, nd),
        out_shape=jax.ShapeDtypeStruct((nt, tok, xw), jnp.bfloat16),
        in_specs=[pl.BlockSpec(memory_space=pltpu.VMEM)] * 2,
        out_specs=pl.BlockSpec(memory_space=pltpu.VMEM),
        scratch_shapes=[
            pltpu.VMEM((nt, tok, rb), jnp.bfloat16),
            pltpu.VMEM((nd, rows, xw), jnp.bfloat16),
            pltpu.VMEM((nt, tok, xw), jnp.bfloat16),
            pltpu.SemaphoreType.DMA((nt,)),
            pltpu.SemaphoreType.DMA((nt,)),
            pltpu.SemaphoreType.DMA((nd,)),
            pltpu.SemaphoreType.DMA((nd,)),
            pltpu.SemaphoreType.DMA((nt,)),
            pltpu.SemaphoreType.DMA((nt,)),
            pltpu.SemaphoreType.DMA((2,)),
        ],
        compiler_params=pltpu.CompilerParams(
            collective_id=1, has_side_effects=True, vmem_limit_bytes=32 * 1024 * 1024),
        cost_estimate=pl.CostEstimate(
            flops=2 * tok * rb * nt * xw, transcendentals=0,
            bytes_accessed=(nt * tok * rb + nd * rows * xw + 2 * nt * tok * xw) * 2),
    )(tokens, wcol)


def on_device(tokens, small_weights, ffn_growth, width_growth):
    n_t = lax.axis_size("tensor")
    n_d = lax.axis_size("dp")
    t = lax.axis_index("tensor")
    rows, ds = width_growth.shape
    xw = ds // n_t
    blk = ds // n_d
    w_cols = lax.dynamic_slice_in_dim(width_growth, t * xw, xw, axis=1)
    tw_blocks = _tw(tokens, w_cols, n_t, n_d)
    s_rows = lax.all_gather(small_weights.transpose(1, 0, 2), "tensor", axis=0, tiled=True)
    panels = jnp.einsum(
        "smf,cf->msc", s_rows, ffn_growth, preferred_element_type=jnp.float32
    ).astype(jnp.bfloat16)
    hb = blk // 2
    w3h = width_growth.reshape(rows, n_d, 2, hb).transpose(1, 2, 0, 3)
    quarters = panels.reshape(4, hb, panels.shape[2])
    grown_t, hidden_t = _dp_ring(quarters, w3h, tw_blocks)
    grown_weights = grown_t.transpose(0, 2, 1)
    hidden = hidden_t.T
    return (grown_weights, hidden)


def solution(mesh):
    placed = (P("dp", "tensor"), P(None, ("dp", "tensor"), None), P("tensor", None), P("dp", None))
    return jax.shard_map(
        on_device,
        mesh=mesh,
        in_specs=placed,
        out_specs=(P(None, "dp", "tensor"), P("dp", "tensor")),
        check_vma=False,
    )
```

```python
import functools

import jax
import jax.numpy as jnp
from jax import lax
from jax.experimental import pallas as pl
from jax.experimental.pallas import tpu as pltpu
from jax.sharding import PartitionSpec as P

MESH = pl.DeviceIdType.MESH


def _ring_pos(d):
    h = d // 4
    return h * 7 + (1 - 2 * h) * (d % 4)


def _ring_dev(p):
    h = p // 4
    return h * 4 + h * 3 + (1 - 2 * h) * (p % 4)


def _cross_pos(d):
    z = d % 4
    return 2 * z + (d // 4 + z) % 2


def _cross_dev(p):
    i = p // 2
    return ((i + p % 2) % 2) * 4 + i


def _flip_z(d, c):
    z = d % 4
    return d + c * (1 - 2 * (z % 2))


def _flip_y(d, c):
    y = d // 4
    return d + c * (1 - 2 * y) * 4


def _dp_ring_kernel(n, p_ref, w3_ref, tw_ref, grown_ref, hid_ref, recv, acc, pre, ssem, rsem, osem):
    t = lax.axis_index("tensor")
    d = lax.axis_index("dp")
    c = t % 2
    pos_a = _ring_pos(_flip_z(d, c))
    pos_b = _cross_pos(_flip_y(d, c))

    def dev_a(p):
        return _flip_z(_ring_dev(p % n), c)

    def dev_b(p):
        return _flip_y(_cross_dev(p % n), c)

    flows = [
        (dev_a, pos_a, 1),
        (dev_a, pos_a, -1),
        (dev_b, pos_b, 1),
        (dev_b, pos_b, -1),
    ]
    xw = tw_ref.shape[2]

    barrier = pltpu.get_barrier_semaphore()
    for dev, pos, sgn in flows:
        pl.semaphore_signal(barrier, inc=1, device_id=(dev(pos + sgn + n), t), device_id_type=MESH)
    pl.semaphore_wait(barrier, 4)

    own = []
    for q in range(4):
        cp = pltpu.make_async_copy(p_ref.at[q], recv.at[q, d], osem.at[q])
        cp.start()
        own.append(cp)
    for cp in own:
        cp.wait()

    def origin(q, k):
        dev, pos, sgn = flows[q]
        return dev(pos - sgn * k + n)

    def contrib(q, o):
        g = jnp.dot(w3_ref[o, q % 2], recv[q, o], preferred_element_type=jnp.float32)
        h = jnp.dot(tw_ref[2 * o + q % 2], recv[q, o], preferred_element_type=jnp.float32)
        return g, h

    hb = recv.shape[2]
    cut = (hb // 2) // 16 * 16
    subs = ((0, cut), (cut, hb - cut))

    def send(q, sub, k):
        dev, pos, sgn = flows[q]
        o = origin(q, k)
        lo, ln = subs[sub]
        return pltpu.make_async_remote_copy(
            src_ref=recv.at[q, o, pl.ds(lo, ln)], dst_ref=recv.at[q, o, pl.ds(lo, ln)],
            send_sem=ssem.at[q, sub, k], recv_sem=rsem.at[q, sub, k],
            device_id=(dev(pos + sgn + n), t), device_id_type=MESH)

    for q in range(4):
        for sub in range(2):
            send(q, sub, 0).start()

    def step(k, carry):
        parts = [contrib(q, origin(q, k)) for q in range(4)]
        g0 = parts[0][0] + parts[1][0]
        g1 = parts[2][0] + parts[3][0]
        h0 = parts[0][1] + parts[1][1]
        h1 = parts[2][1] + parts[3][1]

        @pl.when(k == 0)
        def _():
            acc[0] = g0
            acc[1] = g1
            pre[0] = h0
            pre[1] = h1

        @pl.when(k > 0)
        def _():
            acc[0] += g0
            acc[1] += g1
            pre[0] += h0
            pre[1] += h1

        for sub in range(2):
            for q in range(4):
                send(q, sub, k).wait()

                @pl.when(k + 1 < n - 1)
                def _():
                    send(q, sub, k + 1).start()
        return carry

    lax.fori_loop(0, n - 1, step, 0)
    parts = [contrib(q, origin(q, n - 1)) for q in range(4)]
    acc[0] += parts[0][0] + parts[1][0]
    acc[1] += parts[2][0] + parts[3][0]
    grown_ref[...] = acc[...].astype(grown_ref.dtype)
    gate = pre[0] + parts[0][1] + parts[1][1]
    up = pre[1] + parts[2][1] + parts[3][1]
    hid_ref[...] = (gate / (1.0 + jnp.exp(-gate)) * up).astype(hid_ref.dtype)


def _dp_ring(quarters, w3h, tw_blocks):
    n, _, rows, hb = w3h.shape
    _, _, cols = quarters.shape
    nt, tok, xw = tw_blocks.shape
    flops = 2 * 2 * rows * hb * 2 * cols * n + 2 * 2 * tok * xw * nt * cols
    return pl.pallas_call(
        functools.partial(_dp_ring_kernel, n),
        out_shape=(
            jax.ShapeDtypeStruct((2, rows, cols), jnp.bfloat16),
            jax.ShapeDtypeStruct((tok, cols), jnp.bfloat16),
        ),
        in_specs=[pl.BlockSpec(memory_space=pltpu.VMEM)] * 3,
        out_specs=(pl.BlockSpec(memory_space=pltpu.VMEM), pl.BlockSpec(memory_space=pltpu.VMEM)),
        scratch_shapes=[
            pltpu.VMEM((4, n, hb, cols), jnp.bfloat16),
            pltpu.VMEM((2, rows, cols), jnp.float32),
            pltpu.VMEM((2, tok, cols), jnp.float32),
            pltpu.SemaphoreType.DMA((4, 2, n - 1)),
            pltpu.SemaphoreType.DMA((4, 2, n - 1)),
            pltpu.SemaphoreType.DMA((4,)),
        ],
        compiler_params=pltpu.CompilerParams(
            collective_id=0, has_side_effects=True, vmem_limit_bytes=56 * 1024 * 1024),
        cost_estimate=pl.CostEstimate(
            flops=flops, transcendentals=tok * cols, bytes_accessed=4 * n * hb * cols * 2),
    )(quarters, w3h, tw_blocks)


def _tw_kernel(nt, nd, tok_ref, wcol_ref, out_ref, tbuf, wbuf, xbuf,
               ts_sem, tr_sem, ws_sem, wr_sem, xs_sem, xr_sem, l_sem):
    t = lax.axis_index("tensor")
    d = lax.axis_index("dp")
    rb = tok_ref.shape[1]

    barrier = pltpu.get_barrier_semaphore()

    def greet_t(j, c):
        pl.semaphore_signal(barrier, inc=1, device_id=(d, (t + j) % nt), device_id_type=MESH)
        return c

    def greet_d(j, c):
        pl.semaphore_signal(barrier, inc=1, device_id=((d + j) % nd, t), device_id_type=MESH)
        return c

    lax.fori_loop(1, nt, greet_t, 0)
    lax.fori_loop(1, nd, greet_d, 0)
    pl.semaphore_wait(barrier, nt - 1 + nd - 1)

    c0 = pltpu.make_async_copy(tok_ref, tbuf.at[t], l_sem.at[0])
    c1 = pltpu.make_async_copy(wcol_ref, wbuf.at[d], l_sem.at[1])
    c0.start()
    c1.start()

    def t_copy(p):
        return pltpu.make_async_remote_copy(
            src_ref=tok_ref, dst_ref=tbuf.at[t], send_sem=ts_sem.at[p], recv_sem=tr_sem.at[t],
            device_id=(d, p), device_id_type=MESH)

    def t_recv(p):
        return pltpu.make_async_remote_copy(
            src_ref=tok_ref, dst_ref=tbuf.at[p], send_sem=ts_sem.at[p], recv_sem=tr_sem.at[p],
            device_id=(d, p), device_id_type=MESH)

    def w_copy(p):
        return pltpu.make_async_remote_copy(
            src_ref=wcol_ref, dst_ref=wbuf.at[d], send_sem=ws_sem.at[p], recv_sem=wr_sem.at[d],
            device_id=(p, t), device_id_type=MESH)

    def w_recv(p):
        return pltpu.make_async_remote_copy(
            src_ref=wcol_ref, dst_ref=wbuf.at[p], send_sem=ws_sem.at[p], recv_sem=wr_sem.at[p],
            device_id=(p, t), device_id_type=MESH)

    def send_t(j, c):
        t_copy((t + j) % nt).start()
        return c

    def send_d(j, c):
        w_copy((d + j) % nd).start()
        return c

    lax.fori_loop(1, nt, send_t, 0)
    lax.fori_loop(1, nd, send_d, 0)

    def wait_t(j, c):
        p = (t + j) % nt
        t_copy(p).wait_send()
        t_recv(p).wait_recv()
        return c

    def wait_d(j, c):
        p = (d + j) % nd
        w_copy(p).wait_send()
        w_recv(p).wait_recv()
        return c

    lax.fori_loop(1, nt, wait_t, 0)
    lax.fori_loop(1, nd, wait_d, 0)
    c0.wait()
    c1.wait()

    per = nt // nd
    acc = None
    for q in range(nt):
        part = jnp.dot(tbuf[q], wbuf[q // per, pl.ds((q % per) * rb, rb), :],
                       preferred_element_type=jnp.float32)
        acc = part if acc is None else acc + part
    xbuf[t] = acc.astype(xbuf.dtype)

    def x_copy(p):
        return pltpu.make_async_remote_copy(
            src_ref=xbuf.at[t], dst_ref=xbuf.at[t], send_sem=xs_sem.at[p], recv_sem=xr_sem.at[t],
            device_id=(d, p), device_id_type=MESH)

    def x_recv(p):
        return pltpu.make_async_remote_copy(
            src_ref=xbuf.at[p], dst_ref=xbuf.at[p], send_sem=xs_sem.at[p], recv_sem=xr_sem.at[p],
            device_id=(d, p), device_id_type=MESH)

    def send_x(j, c):
        x_copy((t + j) % nt).start()
        return c

    def wait_x(j, c):
        p = (t + j) % nt
        x_copy(p).wait_send()
        x_recv(p).wait_recv()
        return c

    lax.fori_loop(1, nt, send_x, 0)
    lax.fori_loop(1, nt, wait_x, 0)
    out_ref[...] = xbuf[...]


def _tw(tokens, wcol, nt, nd):
    tok, rb = tokens.shape
    rows, xw = wcol.shape
    return pl.pallas_call(
        functools.partial(_tw_kernel, nt, nd),
        out_shape=jax.ShapeDtypeStruct((nt, tok, xw), jnp.bfloat16),
        in_specs=[pl.BlockSpec(memory_space=pltpu.VMEM)] * 2,
        out_specs=pl.BlockSpec(memory_space=pltpu.VMEM),
        scratch_shapes=[
            pltpu.VMEM((nt, tok, rb), jnp.bfloat16),
            pltpu.VMEM((nd, rows, xw), jnp.bfloat16),
            pltpu.VMEM((nt, tok, xw), jnp.bfloat16),
            pltpu.SemaphoreType.DMA((nt,)),
            pltpu.SemaphoreType.DMA((nt,)),
            pltpu.SemaphoreType.DMA((nd,)),
            pltpu.SemaphoreType.DMA((nd,)),
            pltpu.SemaphoreType.DMA((nt,)),
            pltpu.SemaphoreType.DMA((nt,)),
            pltpu.SemaphoreType.DMA((2,)),
        ],
        compiler_params=pltpu.CompilerParams(
            collective_id=1, has_side_effects=True, vmem_limit_bytes=32 * 1024 * 1024),
        cost_estimate=pl.CostEstimate(
            flops=2 * tok * rb * nt * xw, transcendentals=0,
            bytes_accessed=(nt * tok * rb + nd * rows * xw + 2 * nt * tok * xw) * 2),
    )(tokens, wcol)


def on_device(tokens, small_weights, ffn_growth, width_growth):
    n_t = lax.axis_size("tensor")
    n_d = lax.axis_size("dp")
    t = lax.axis_index("tensor")
    rows, ds = width_growth.shape
    xw = ds // n_t
    blk = ds // n_d
    w_cols = lax.dynamic_slice_in_dim(width_growth, t * xw, xw, axis=1)
    tw_blocks = _tw(tokens, w_cols, n_t, n_d)
    s_rows = lax.all_gather(small_weights.transpose(1, 0, 2), "tensor", axis=0, tiled=True)
    panels = jnp.einsum(
        "smf,cf->msc", s_rows, ffn_growth, preferred_element_type=jnp.float32
    ).astype(jnp.bfloat16)
    hb = blk // 2
    w3h = width_growth.reshape(rows, n_d, 2, hb).transpose(1, 2, 0, 3)
    quarters = panels.reshape(4, hb, panels.shape[2])
    grown_weights, hidden = _dp_ring(quarters, w3h, tw_blocks)
    return (grown_weights, hidden)


def solution(mesh):
    placed = (P("dp", "tensor"), P(None, ("dp", "tensor"), None), P("tensor", None), P("dp", None))
    return jax.shard_map(
        on_device,
        mesh=mesh,
        in_specs=placed,
        out_specs=(P(None, "dp", "tensor"), P("dp", "tensor")),
        check_vma=False,
    )
```

```python
import functools

import jax
import jax.numpy as jnp
from jax import lax
from jax.experimental import pallas as pl
from jax.experimental.pallas import tpu as pltpu
from jax.sharding import PartitionSpec as P

MESH = pl.DeviceIdType.MESH


def _ring_pos(d):
    h = d // 4
    return h * 7 + (1 - 2 * h) * (d % 4)


def _ring_dev(p):
    h = p // 4
    return h * 4 + h * 3 + (1 - 2 * h) * (p % 4)


def _cross_pos(d):
    z = d % 4
    return 2 * z + (d // 4 + z) % 2


def _cross_dev(p):
    i = p // 2
    return ((i + p % 2) % 2) * 4 + i


def _flip_z(d, c):
    z = d % 4
    return d + c * (1 - 2 * (z % 2))


def _flip_y(d, c):
    y = d // 4
    return d + c * (1 - 2 * y) * 4


def _dp_ring_kernel(n, p_ref, w3_ref, tw_ref, grown_ref, hid_ref, recv, acc, pre, ssem, rsem, osem):
    t = lax.axis_index("tensor")
    d = lax.axis_index("dp")
    c = t % 2
    pos_a = _ring_pos(_flip_z(d, c))
    pos_b = _cross_pos(_flip_y(d, c))

    def dev_a(p):
        return _flip_z(_ring_dev(p % n), c)

    def dev_b(p):
        return _flip_y(_cross_dev(p % n), c)

    flows = [
        (dev_a, pos_a, 1),
        (dev_a, pos_a, -1),
        (dev_b, pos_b, 1),
        (dev_b, pos_b, -1),
    ]
    xw = tw_ref.shape[2]

    barrier = pltpu.get_barrier_semaphore()
    for dev, pos, sgn in flows:
        pl.semaphore_signal(barrier, inc=1, device_id=(dev(pos + sgn + n), t), device_id_type=MESH)
    pl.semaphore_wait(barrier, 4)

    own = []
    for q in range(4):
        cp = pltpu.make_async_copy(p_ref.at[q], recv.at[q, d], osem.at[q])
        cp.start()
        own.append(cp)
    for cp in own:
        cp.wait()

    def origin(q, k):
        dev, pos, sgn = flows[q]
        return dev(pos - sgn * k + n)

    def contrib(q, o):
        g = jnp.dot(w3_ref[o, q % 2], recv[q, o], preferred_element_type=jnp.float32)
        h = jnp.dot(tw_ref[2 * o + q % 2], recv[q, o], preferred_element_type=jnp.float32)
        return g, h

    hb = recv.shape[2]
    cut = (hb // 3) // 16 * 16
    subs = ((0, cut), (cut, cut), (2 * cut, hb - 2 * cut))

    def send(q, sub, k):
        dev, pos, sgn = flows[q]
        o = origin(q, k)
        lo, ln = subs[sub]
        return pltpu.make_async_remote_copy(
            src_ref=recv.at[q, o, pl.ds(lo, ln)], dst_ref=recv.at[q, o, pl.ds(lo, ln)],
            send_sem=ssem.at[q, sub, k], recv_sem=rsem.at[q, sub, k],
            device_id=(dev(pos + sgn + n), t), device_id_type=MESH)

    for q in range(4):
        for sub in range(len(subs)):
            send(q, sub, 0).start()

    def step(k, carry):
        parts = [contrib(q, origin(q, k)) for q in range(4)]
        g0 = parts[0][0] + parts[1][0]
        g1 = parts[2][0] + parts[3][0]
        h0 = parts[0][1] + parts[1][1]
        h1 = parts[2][1] + parts[3][1]

        @pl.when(k == 0)
        def _():
            acc[0] = g0
            acc[1] = g1
            pre[0] = h0
            pre[1] = h1

        @pl.when(k > 0)
        def _():
            acc[0] += g0
            acc[1] += g1
            pre[0] += h0
            pre[1] += h1

        for sub in range(len(subs)):
            for q in range(4):
                send(q, sub, k).wait()

                @pl.when(k + 1 < n - 1)
                def _():
                    send(q, sub, k + 1).start()
        return carry

    lax.fori_loop(0, n - 1, step, 0)
    parts = [contrib(q, origin(q, n - 1)) for q in range(4)]
    acc[0] += parts[0][0] + parts[1][0]
    acc[1] += parts[2][0] + parts[3][0]
    grown_ref[...] = acc[...].astype(grown_ref.dtype)
    gate = pre[0] + parts[0][1] + parts[1][1]
    up = pre[1] + parts[2][1] + parts[3][1]
    hid_ref[...] = (gate / (1.0 + jnp.exp(-gate)) * up).astype(hid_ref.dtype)


def _dp_ring(quarters, w3h, tw_blocks):
    n, _, rows, hb = w3h.shape
    _, _, cols = quarters.shape
    nt, tok, xw = tw_blocks.shape
    flops = 2 * 2 * rows * hb * 2 * cols * n + 2 * 2 * tok * xw * nt * cols
    return pl.pallas_call(
        functools.partial(_dp_ring_kernel, n),
        out_shape=(
            jax.ShapeDtypeStruct((2, rows, cols), jnp.bfloat16),
            jax.ShapeDtypeStruct((tok, cols), jnp.bfloat16),
        ),
        in_specs=[pl.BlockSpec(memory_space=pltpu.VMEM)] * 3,
        out_specs=(pl.BlockSpec(memory_space=pltpu.VMEM), pl.BlockSpec(memory_space=pltpu.VMEM)),
        scratch_shapes=[
            pltpu.VMEM((4, n, hb, cols), jnp.bfloat16),
            pltpu.VMEM((2, rows, cols), jnp.float32),
            pltpu.VMEM((2, tok, cols), jnp.float32),
            pltpu.SemaphoreType.DMA((4, 3, n - 1)),
            pltpu.SemaphoreType.DMA((4, 3, n - 1)),
            pltpu.SemaphoreType.DMA((4,)),
        ],
        compiler_params=pltpu.CompilerParams(
            collective_id=0, has_side_effects=True, vmem_limit_bytes=56 * 1024 * 1024),
        cost_estimate=pl.CostEstimate(
            flops=flops, transcendentals=tok * cols, bytes_accessed=4 * n * hb * cols * 2),
    )(quarters, w3h, tw_blocks)


def _tw_kernel(nt, nd, tok_ref, wcol_ref, out_ref, tbuf, wbuf, xbuf,
               ts_sem, tr_sem, ws_sem, wr_sem, xs_sem, xr_sem, l_sem):
    t = lax.axis_index("tensor")
    d = lax.axis_index("dp")
    rb = tok_ref.shape[1]

    barrier = pltpu.get_barrier_semaphore()

    def greet_t(j, c):
        pl.semaphore_signal(barrier, inc=1, device_id=(d, (t + j) % nt), device_id_type=MESH)
        return c

    def greet_d(j, c):
        pl.semaphore_signal(barrier, inc=1, device_id=((d + j) % nd, t), device_id_type=MESH)
        return c

    lax.fori_loop(1, nt, greet_t, 0)
    lax.fori_loop(1, nd, greet_d, 0)
    pl.semaphore_wait(barrier, nt - 1 + nd - 1)

    c0 = pltpu.make_async_copy(tok_ref, tbuf.at[t], l_sem.at[0])
    c1 = pltpu.make_async_copy(wcol_ref, wbuf.at[d], l_sem.at[1])
    c0.start()
    c1.start()

    def t_copy(p):
        return pltpu.make_async_remote_copy(
            src_ref=tok_ref, dst_ref=tbuf.at[t], send_sem=ts_sem.at[p], recv_sem=tr_sem.at[t],
            device_id=(d, p), device_id_type=MESH)

    def t_recv(p):
        return pltpu.make_async_remote_copy(
            src_ref=tok_ref, dst_ref=tbuf.at[p], send_sem=ts_sem.at[p], recv_sem=tr_sem.at[p],
            device_id=(d, p), device_id_type=MESH)

    def w_copy(p):
        return pltpu.make_async_remote_copy(
            src_ref=wcol_ref, dst_ref=wbuf.at[d], send_sem=ws_sem.at[p], recv_sem=wr_sem.at[d],
            device_id=(p, t), device_id_type=MESH)

    def w_recv(p):
        return pltpu.make_async_remote_copy(
            src_ref=wcol_ref, dst_ref=wbuf.at[p], send_sem=ws_sem.at[p], recv_sem=wr_sem.at[p],
            device_id=(p, t), device_id_type=MESH)

    def send_t(j, c):
        t_copy((t + j) % nt).start()
        return c

    def send_d(j, c):
        w_copy((d + j) % nd).start()
        return c

    lax.fori_loop(1, nt, send_t, 0)
    lax.fori_loop(1, nd, send_d, 0)

    def wait_t(j, c):
        p = (t + j) % nt
        t_copy(p).wait_send()
        t_recv(p).wait_recv()
        return c

    def wait_d(j, c):
        p = (d + j) % nd
        w_copy(p).wait_send()
        w_recv(p).wait_recv()
        return c

    lax.fori_loop(1, nt, wait_t, 0)
    lax.fori_loop(1, nd, wait_d, 0)
    c0.wait()
    c1.wait()

    per = nt // nd
    acc = None
    for q in range(nt):
        part = jnp.dot(tbuf[q], wbuf[q // per, pl.ds((q % per) * rb, rb), :],
                       preferred_element_type=jnp.float32)
        acc = part if acc is None else acc + part
    xbuf[t] = acc.astype(xbuf.dtype)

    def x_copy(p):
        return pltpu.make_async_remote_copy(
            src_ref=xbuf.at[t], dst_ref=xbuf.at[t], send_sem=xs_sem.at[p], recv_sem=xr_sem.at[t],
            device_id=(d, p), device_id_type=MESH)

    def x_recv(p):
        return pltpu.make_async_remote_copy(
            src_ref=xbuf.at[p], dst_ref=xbuf.at[p], send_sem=xs_sem.at[p], recv_sem=xr_sem.at[p],
            device_id=(d, p), device_id_type=MESH)

    def send_x(j, c):
        x_copy((t + j) % nt).start()
        return c

    def wait_x(j, c):
        p = (t + j) % nt
        x_copy(p).wait_send()
        x_recv(p).wait_recv()
        return c

    lax.fori_loop(1, nt, send_x, 0)
    lax.fori_loop(1, nt, wait_x, 0)
    out_ref[...] = xbuf[...]


def _tw(tokens, wcol, nt, nd):
    tok, rb = tokens.shape
    rows, xw = wcol.shape
    return pl.pallas_call(
        functools.partial(_tw_kernel, nt, nd),
        out_shape=jax.ShapeDtypeStruct((nt, tok, xw), jnp.bfloat16),
        in_specs=[pl.BlockSpec(memory_space=pltpu.VMEM)] * 2,
        out_specs=pl.BlockSpec(memory_space=pltpu.VMEM),
        scratch_shapes=[
            pltpu.VMEM((nt, tok, rb), jnp.bfloat16),
            pltpu.VMEM((nd, rows, xw), jnp.bfloat16),
            pltpu.VMEM((nt, tok, xw), jnp.bfloat16),
            pltpu.SemaphoreType.DMA((nt,)),
            pltpu.SemaphoreType.DMA((nt,)),
            pltpu.SemaphoreType.DMA((nd,)),
            pltpu.SemaphoreType.DMA((nd,)),
            pltpu.SemaphoreType.DMA((nt,)),
            pltpu.SemaphoreType.DMA((nt,)),
            pltpu.SemaphoreType.DMA((2,)),
        ],
        compiler_params=pltpu.CompilerParams(
            collective_id=1, has_side_effects=True, vmem_limit_bytes=32 * 1024 * 1024),
        cost_estimate=pl.CostEstimate(
            flops=2 * tok * rb * nt * xw, transcendentals=0,
            bytes_accessed=(nt * tok * rb + nd * rows * xw + 2 * nt * tok * xw) * 2),
    )(tokens, wcol)


def on_device(tokens, small_weights, ffn_growth, width_growth):
    n_t = lax.axis_size("tensor")
    n_d = lax.axis_size("dp")
    t = lax.axis_index("tensor")
    rows, ds = width_growth.shape
    xw = ds // n_t
    blk = ds // n_d
    w_cols = lax.dynamic_slice_in_dim(width_growth, t * xw, xw, axis=1)
    tw_blocks = _tw(tokens, w_cols, n_t, n_d)
    s_rows = lax.all_gather(small_weights.transpose(1, 0, 2), "tensor", axis=0, tiled=True)
    panels = jnp.einsum(
        "smf,cf->msc", s_rows, ffn_growth, preferred_element_type=jnp.float32
    ).astype(jnp.bfloat16)
    hb = blk // 2
    w3h = width_growth.reshape(rows, n_d, 2, hb).transpose(1, 2, 0, 3)
    quarters = panels.reshape(4, hb, panels.shape[2])
    grown_weights, hidden = _dp_ring(quarters, w3h, tw_blocks)
    return (grown_weights, hidden)


def solution(mesh):
    placed = (P("dp", "tensor"), P(None, ("dp", "tensor"), None), P("tensor", None), P("dp", None))
    return jax.shard_map(
        on_device,
        mesh=mesh,
        in_specs=placed,
        out_specs=(P(None, "dp", "tensor"), P("dp", "tensor")),
        check_vma=False,
    )
```

```python
import functools

import jax
import jax.numpy as jnp
from jax import lax
from jax.experimental import pallas as pl
from jax.experimental.pallas import tpu as pltpu
from jax.sharding import PartitionSpec as P

MESH = pl.DeviceIdType.MESH


def _ring_pos(d):
    h = d // 4
    return h * 7 + (1 - 2 * h) * (d % 4)


def _ring_dev(p):
    h = p // 4
    return h * 4 + h * 3 + (1 - 2 * h) * (p % 4)


def _cross_pos(d):
    z = d % 4
    return 2 * z + (d // 4 + z) % 2


def _cross_dev(p):
    i = p // 2
    return ((i + p % 2) % 2) * 4 + i


def _flip_z(d, c):
    z = d % 4
    return d + c * (1 - 2 * (z % 2))


def _flip_y(d, c):
    y = d // 4
    return d + c * (1 - 2 * y) * 4


def _dp_ring_kernel(n, p_ref, w3_ref, tw_ref, grown_ref, hid_ref, recv, acc, pre, ssem, rsem, osem):
    t = lax.axis_index("tensor")
    d = lax.axis_index("dp")
    c = t % 2
    pos_a = _ring_pos(_flip_z(d, c))
    pos_b = _cross_pos(_flip_y(d, c))

    def dev_a(p):
        return _flip_z(_ring_dev(p % n), c)

    def dev_b(p):
        return _flip_y(_cross_dev(p % n), c)

    flows = [
        (dev_a, pos_a, 1),
        (dev_a, pos_a, -1),
        (dev_b, pos_b, 1),
        (dev_b, pos_b, -1),
    ]
    xw = tw_ref.shape[2]

    barrier = pltpu.get_barrier_semaphore()
    for dev, pos, sgn in flows:
        pl.semaphore_signal(barrier, inc=1, device_id=(dev(pos + sgn + n), t), device_id_type=MESH)
    pl.semaphore_wait(barrier, 4)

    own = []
    for q in range(4):
        cp = pltpu.make_async_copy(p_ref.at[q], recv.at[q, d], osem.at[q])
        cp.start()
        own.append(cp)
    for cp in own:
        cp.wait()

    def origin(q, k):
        dev, pos, sgn = flows[q]
        return dev(pos - sgn * k + n)

    def contrib(q, o):
        g = jnp.dot(w3_ref[o, q % 2], recv[q, o], preferred_element_type=jnp.float32)
        h = jnp.dot(tw_ref[2 * o + q % 2], recv[q, o], preferred_element_type=jnp.float32)
        return g, h

    hb = recv.shape[2]
    cut = (hb // 3) // 16 * 16
    subs = ((0, cut), (cut, hb - cut))

    def send(q, sub, k):
        dev, pos, sgn = flows[q]
        o = origin(q, k)
        lo, ln = subs[sub]
        return pltpu.make_async_remote_copy(
            src_ref=recv.at[q, o, pl.ds(lo, ln)], dst_ref=recv.at[q, o, pl.ds(lo, ln)],
            send_sem=ssem.at[q, sub, k], recv_sem=rsem.at[q, sub, k],
            device_id=(dev(pos + sgn + n), t), device_id_type=MESH)

    for q in range(4):
        for sub in range(2):
            send(q, sub, 0).start()

    def step(k, carry):
        parts = [contrib(q, origin(q, k)) for q in range(4)]
        g0 = parts[0][0] + parts[1][0]
        g1 = parts[2][0] + parts[3][0]
        h0 = parts[0][1] + parts[1][1]
        h1 = parts[2][1] + parts[3][1]

        @pl.when(k == 0)
        def _():
            acc[0] = g0
            acc[1] = g1
            pre[0] = h0
            pre[1] = h1

        @pl.when(k > 0)
        def _():
            acc[0] += g0
            acc[1] += g1
            pre[0] += h0
            pre[1] += h1

        for sub in range(2):
            for q in range(4):
                send(q, sub, k).wait()

                @pl.when(k + 1 < n - 1)
                def _():
                    send(q, sub, k + 1).start()
        return carry

    lax.fori_loop(0, n - 1, step, 0)
    parts = [contrib(q, origin(q, n - 1)) for q in range(4)]
    acc[0] += parts[0][0] + parts[1][0]
    acc[1] += parts[2][0] + parts[3][0]
    grown_ref[...] = acc[...].astype(grown_ref.dtype)
    gate = pre[0] + parts[0][1] + parts[1][1]
    up = pre[1] + parts[2][1] + parts[3][1]
    hid_ref[...] = (gate / (1.0 + jnp.exp(-gate)) * up).astype(hid_ref.dtype)


def _dp_ring(quarters, w3h, tw_blocks):
    n, _, rows, hb = w3h.shape
    _, _, cols = quarters.shape
    nt, tok, xw = tw_blocks.shape
    flops = 2 * 2 * rows * hb * 2 * cols * n + 2 * 2 * tok * xw * nt * cols
    return pl.pallas_call(
        functools.partial(_dp_ring_kernel, n),
        out_shape=(
            jax.ShapeDtypeStruct((2, rows, cols), jnp.bfloat16),
            jax.ShapeDtypeStruct((tok, cols), jnp.bfloat16),
        ),
        in_specs=[pl.BlockSpec(memory_space=pltpu.VMEM)] * 3,
        out_specs=(pl.BlockSpec(memory_space=pltpu.VMEM), pl.BlockSpec(memory_space=pltpu.VMEM)),
        scratch_shapes=[
            pltpu.VMEM((4, n, hb, cols), jnp.bfloat16),
            pltpu.VMEM((2, rows, cols), jnp.float32),
            pltpu.VMEM((2, tok, cols), jnp.float32),
            pltpu.SemaphoreType.DMA((4, 2, n - 1)),
            pltpu.SemaphoreType.DMA((4, 2, n - 1)),
            pltpu.SemaphoreType.DMA((4,)),
        ],
        compiler_params=pltpu.CompilerParams(
            collective_id=0, has_side_effects=True, vmem_limit_bytes=56 * 1024 * 1024),
        cost_estimate=pl.CostEstimate(
            flops=flops, transcendentals=tok * cols, bytes_accessed=4 * n * hb * cols * 2),
    )(quarters, w3h, tw_blocks)


def _tw_kernel(nt, nd, tok_ref, wcol_ref, out_ref, tbuf, wbuf, xbuf,
               ts_sem, tr_sem, ws_sem, wr_sem, xs_sem, xr_sem, l_sem):
    t = lax.axis_index("tensor")
    d = lax.axis_index("dp")
    rb = tok_ref.shape[1]

    barrier = pltpu.get_barrier_semaphore()

    def greet_t(j, c):
        pl.semaphore_signal(barrier, inc=1, device_id=(d, (t + j) % nt), device_id_type=MESH)
        return c

    def greet_d(j, c):
        pl.semaphore_signal(barrier, inc=1, device_id=((d + j) % nd, t), device_id_type=MESH)
        return c

    lax.fori_loop(1, nt, greet_t, 0)
    lax.fori_loop(1, nd, greet_d, 0)
    pl.semaphore_wait(barrier, nt - 1 + nd - 1)

    c0 = pltpu.make_async_copy(tok_ref, tbuf.at[t], l_sem.at[0])
    c1 = pltpu.make_async_copy(wcol_ref, wbuf.at[d], l_sem.at[1])
    c0.start()
    c1.start()

    def t_copy(p):
        return pltpu.make_async_remote_copy(
            src_ref=tok_ref, dst_ref=tbuf.at[t], send_sem=ts_sem.at[p], recv_sem=tr_sem.at[t],
            device_id=(d, p), device_id_type=MESH)

    def t_recv(p):
        return pltpu.make_async_remote_copy(
            src_ref=tok_ref, dst_ref=tbuf.at[p], send_sem=ts_sem.at[p], recv_sem=tr_sem.at[p],
            device_id=(d, p), device_id_type=MESH)

    def w_copy(p):
        return pltpu.make_async_remote_copy(
            src_ref=wcol_ref, dst_ref=wbuf.at[d], send_sem=ws_sem.at[p], recv_sem=wr_sem.at[d],
            device_id=(p, t), device_id_type=MESH)

    def w_recv(p):
        return pltpu.make_async_remote_copy(
            src_ref=wcol_ref, dst_ref=wbuf.at[p], send_sem=ws_sem.at[p], recv_sem=wr_sem.at[p],
            device_id=(p, t), device_id_type=MESH)

    def send_t(j, c):
        t_copy((t + j) % nt).start()
        return c

    def send_d(j, c):
        w_copy((d + j) % nd).start()
        return c

    lax.fori_loop(1, nt, send_t, 0)
    lax.fori_loop(1, nd, send_d, 0)

    def wait_t(j, c):
        p = (t + j) % nt
        t_copy(p).wait_send()
        t_recv(p).wait_recv()
        return c

    def wait_d(j, c):
        p = (d + j) % nd
        w_copy(p).wait_send()
        w_recv(p).wait_recv()
        return c

    lax.fori_loop(1, nt, wait_t, 0)
    lax.fori_loop(1, nd, wait_d, 0)
    c0.wait()
    c1.wait()

    per = nt // nd
    acc = None
    for q in range(nt):
        part = jnp.dot(tbuf[q], wbuf[q // per, pl.ds((q % per) * rb, rb), :],
                       preferred_element_type=jnp.float32)
        acc = part if acc is None else acc + part
    xbuf[t] = acc.astype(xbuf.dtype)

    def x_copy(p):
        return pltpu.make_async_remote_copy(
            src_ref=xbuf.at[t], dst_ref=xbuf.at[t], send_sem=xs_sem.at[p], recv_sem=xr_sem.at[t],
            device_id=(d, p), device_id_type=MESH)

    def x_recv(p):
        return pltpu.make_async_remote_copy(
            src_ref=xbuf.at[p], dst_ref=xbuf.at[p], send_sem=xs_sem.at[p], recv_sem=xr_sem.at[p],
            device_id=(d, p), device_id_type=MESH)

    def send_x(j, c):
        x_copy((t + j) % nt).start()
        return c

    def wait_x(j, c):
        p = (t + j) % nt
        x_copy(p).wait_send()
        x_recv(p).wait_recv()
        return c

    lax.fori_loop(1, nt, send_x, 0)
    lax.fori_loop(1, nt, wait_x, 0)
    out_ref[...] = xbuf[...]


def _tw(tokens, wcol, nt, nd):
    tok, rb = tokens.shape
    rows, xw = wcol.shape
    return pl.pallas_call(
        functools.partial(_tw_kernel, nt, nd),
        out_shape=jax.ShapeDtypeStruct((nt, tok, xw), jnp.bfloat16),
        in_specs=[pl.BlockSpec(memory_space=pltpu.VMEM)] * 2,
        out_specs=pl.BlockSpec(memory_space=pltpu.VMEM),
        scratch_shapes=[
            pltpu.VMEM((nt, tok, rb), jnp.bfloat16),
            pltpu.VMEM((nd, rows, xw), jnp.bfloat16),
            pltpu.VMEM((nt, tok, xw), jnp.bfloat16),
            pltpu.SemaphoreType.DMA((nt,)),
            pltpu.SemaphoreType.DMA((nt,)),
            pltpu.SemaphoreType.DMA((nd,)),
            pltpu.SemaphoreType.DMA((nd,)),
            pltpu.SemaphoreType.DMA((nt,)),
            pltpu.SemaphoreType.DMA((nt,)),
            pltpu.SemaphoreType.DMA((2,)),
        ],
        compiler_params=pltpu.CompilerParams(
            collective_id=1, has_side_effects=True, vmem_limit_bytes=32 * 1024 * 1024),
        cost_estimate=pl.CostEstimate(
            flops=2 * tok * rb * nt * xw, transcendentals=0,
            bytes_accessed=(nt * tok * rb + nd * rows * xw + 2 * nt * tok * xw) * 2),
    )(tokens, wcol)


def on_device(tokens, small_weights, ffn_growth, width_growth):
    n_t = lax.axis_size("tensor")
    n_d = lax.axis_size("dp")
    t = lax.axis_index("tensor")
    rows, ds = width_growth.shape
    xw = ds // n_t
    blk = ds // n_d
    w_cols = lax.dynamic_slice_in_dim(width_growth, t * xw, xw, axis=1)
    tw_blocks = _tw(tokens, w_cols, n_t, n_d)
    s_rows = lax.all_gather(small_weights.transpose(1, 0, 2), "tensor", axis=0, tiled=True)
    panels = jnp.einsum(
        "smf,cf->msc", s_rows, ffn_growth, preferred_element_type=jnp.float32
    ).astype(jnp.bfloat16)
    hb = blk // 2
    w3h = width_growth.reshape(rows, n_d, 2, hb).transpose(1, 2, 0, 3)
    quarters = panels.reshape(4, hb, panels.shape[2])
    grown_weights, hidden = _dp_ring(quarters, w3h, tw_blocks)
    return (grown_weights, hidden)


def solution(mesh):
    placed = (P("dp", "tensor"), P(None, ("dp", "tensor"), None), P("tensor", None), P("dp", None))
    return jax.shard_map(
        on_device,
        mesh=mesh,
        in_specs=placed,
        out_specs=(P(None, "dp", "tensor"), P("dp", "tensor")),
        check_vma=False,
    )
```

```python
import functools

import jax
import jax.numpy as jnp
from jax import lax
from jax.experimental import pallas as pl
from jax.experimental.pallas import tpu as pltpu
from jax.sharding import PartitionSpec as P

MESH = pl.DeviceIdType.MESH


def _ring_pos(d):
    h = d // 4
    return h * 7 + (1 - 2 * h) * (d % 4)


def _ring_dev(p):
    h = p // 4
    return h * 4 + h * 3 + (1 - 2 * h) * (p % 4)


def _cross_pos(d):
    z = d % 4
    return 2 * z + (d // 4 + z) % 2


def _cross_dev(p):
    i = p // 2
    return ((i + p % 2) % 2) * 4 + i


def _flip_z(d, c):
    z = d % 4
    return d + c * (1 - 2 * (z % 2))


def _flip_y(d, c):
    y = d // 4
    return d + c * (1 - 2 * y) * 4


def _dp_ring_kernel(n, p_ref, w3_ref, tw_ref, grown_ref, hid_ref, recv, acc, pre, ssem, rsem, osem):
    t = lax.axis_index("tensor")
    d = lax.axis_index("dp")
    c = t % 2
    pos_a = _ring_pos(_flip_z(d, c))
    pos_b = _cross_pos(_flip_y(d, c))

    def dev_a(p):
        return _flip_z(_ring_dev(p % n), c)

    def dev_b(p):
        return _flip_y(_cross_dev(p % n), c)

    flows = [
        (dev_a, pos_a, 1),
        (dev_a, pos_a, -1),
        (dev_b, pos_b, 1),
        (dev_b, pos_b, -1),
    ]
    xw = tw_ref.shape[2]

    barrier = pltpu.get_barrier_semaphore()
    for dev, pos, sgn in flows:
        pl.semaphore_signal(barrier, inc=1, device_id=(dev(pos + sgn + n), t), device_id_type=MESH)
    pl.semaphore_wait(barrier, 4)

    own = []
    for q in range(4):
        cp = pltpu.make_async_copy(p_ref.at[q], recv.at[q, d], osem.at[q])
        cp.start()
        own.append(cp)
    for cp in own:
        cp.wait()

    def origin(q, k):
        dev, pos, sgn = flows[q]
        return dev(pos - sgn * k + n)

    def contrib(q, o):
        g = jnp.dot(w3_ref[o, q % 2], recv[q, o], preferred_element_type=jnp.float32)
        h = jnp.dot(tw_ref[2 * o + q % 2], recv[q, o], preferred_element_type=jnp.float32)
        return g, h

    hb = recv.shape[2]
    cut = (hb // 4) // 16 * 16
    subs = ((0, cut), (cut, hb - cut))

    def send(q, sub, k):
        dev, pos, sgn = flows[q]
        o = origin(q, k)
        lo, ln = subs[sub]
        return pltpu.make_async_remote_copy(
            src_ref=recv.at[q, o, pl.ds(lo, ln)], dst_ref=recv.at[q, o, pl.ds(lo, ln)],
            send_sem=ssem.at[q, sub, k], recv_sem=rsem.at[q, sub, k],
            device_id=(dev(pos + sgn + n), t), device_id_type=MESH)

    for q in range(4):
        for sub in range(2):
            send(q, sub, 0).start()

    def step(k, carry):
        parts = [contrib(q, origin(q, k)) for q in range(4)]
        g0 = parts[0][0] + parts[1][0]
        g1 = parts[2][0] + parts[3][0]
        h0 = parts[0][1] + parts[1][1]
        h1 = parts[2][1] + parts[3][1]

        @pl.when(k == 0)
        def _():
            acc[0] = g0
            acc[1] = g1
            pre[0] = h0
            pre[1] = h1

        @pl.when(k > 0)
        def _():
            acc[0] += g0
            acc[1] += g1
            pre[0] += h0
            pre[1] += h1

        for sub in range(2):
            for q in range(4):
                send(q, sub, k).wait()

                @pl.when(k + 1 < n - 1)
                def _():
                    send(q, sub, k + 1).start()
        return carry

    lax.fori_loop(0, n - 1, step, 0)
    parts = [contrib(q, origin(q, n - 1)) for q in range(4)]
    acc[0] += parts[0][0] + parts[1][0]
    acc[1] += parts[2][0] + parts[3][0]
    grown_ref[...] = acc[...].astype(grown_ref.dtype)
    gate = pre[0] + parts[0][1] + parts[1][1]
    up = pre[1] + parts[2][1] + parts[3][1]
    hid_ref[...] = (gate / (1.0 + jnp.exp(-gate)) * up).astype(hid_ref.dtype)


def _dp_ring(quarters, w3h, tw_blocks):
    n, _, rows, hb = w3h.shape
    _, _, cols = quarters.shape
    nt, tok, xw = tw_blocks.shape
    flops = 2 * 2 * rows * hb * 2 * cols * n + 2 * 2 * tok * xw * nt * cols
    return pl.pallas_call(
        functools.partial(_dp_ring_kernel, n),
        out_shape=(
            jax.ShapeDtypeStruct((2, rows, cols), jnp.bfloat16),
            jax.ShapeDtypeStruct((tok, cols), jnp.bfloat16),
        ),
        in_specs=[pl.BlockSpec(memory_space=pltpu.VMEM)] * 3,
        out_specs=(pl.BlockSpec(memory_space=pltpu.VMEM), pl.BlockSpec(memory_space=pltpu.VMEM)),
        scratch_shapes=[
            pltpu.VMEM((4, n, hb, cols), jnp.bfloat16),
            pltpu.VMEM((2, rows, cols), jnp.float32),
            pltpu.VMEM((2, tok, cols), jnp.float32),
            pltpu.SemaphoreType.DMA((4, 2, n - 1)),
            pltpu.SemaphoreType.DMA((4, 2, n - 1)),
            pltpu.SemaphoreType.DMA((4,)),
        ],
        compiler_params=pltpu.CompilerParams(
            collective_id=0, has_side_effects=True, vmem_limit_bytes=56 * 1024 * 1024),
        cost_estimate=pl.CostEstimate(
            flops=flops, transcendentals=tok * cols, bytes_accessed=4 * n * hb * cols * 2),
    )(quarters, w3h, tw_blocks)


def _tw_kernel(nt, nd, tok_ref, wcol_ref, out_ref, tbuf, wbuf, xbuf,
               ts_sem, tr_sem, ws_sem, wr_sem, xs_sem, xr_sem, l_sem):
    t = lax.axis_index("tensor")
    d = lax.axis_index("dp")
    rb = tok_ref.shape[1]

    barrier = pltpu.get_barrier_semaphore()

    def greet_t(j, c):
        pl.semaphore_signal(barrier, inc=1, device_id=(d, (t + j) % nt), device_id_type=MESH)
        return c

    def greet_d(j, c):
        pl.semaphore_signal(barrier, inc=1, device_id=((d + j) % nd, t), device_id_type=MESH)
        return c

    lax.fori_loop(1, nt, greet_t, 0)
    lax.fori_loop(1, nd, greet_d, 0)
    pl.semaphore_wait(barrier, nt - 1 + nd - 1)

    c0 = pltpu.make_async_copy(tok_ref, tbuf.at[t], l_sem.at[0])
    c1 = pltpu.make_async_copy(wcol_ref, wbuf.at[d], l_sem.at[1])
    c0.start()
    c1.start()

    def t_copy(p):
        return pltpu.make_async_remote_copy(
            src_ref=tok_ref, dst_ref=tbuf.at[t], send_sem=ts_sem.at[p], recv_sem=tr_sem.at[t],
            device_id=(d, p), device_id_type=MESH)

    def t_recv(p):
        return pltpu.make_async_remote_copy(
            src_ref=tok_ref, dst_ref=tbuf.at[p], send_sem=ts_sem.at[p], recv_sem=tr_sem.at[p],
            device_id=(d, p), device_id_type=MESH)

    def w_copy(p):
        return pltpu.make_async_remote_copy(
            src_ref=wcol_ref, dst_ref=wbuf.at[d], send_sem=ws_sem.at[p], recv_sem=wr_sem.at[d],
            device_id=(p, t), device_id_type=MESH)

    def w_recv(p):
        return pltpu.make_async_remote_copy(
            src_ref=wcol_ref, dst_ref=wbuf.at[p], send_sem=ws_sem.at[p], recv_sem=wr_sem.at[p],
            device_id=(p, t), device_id_type=MESH)

    def send_t(j, c):
        t_copy((t + j) % nt).start()
        return c

    def send_d(j, c):
        w_copy((d + j) % nd).start()
        return c

    lax.fori_loop(1, nt, send_t, 0)
    lax.fori_loop(1, nd, send_d, 0)

    def wait_t(j, c):
        p = (t + j) % nt
        t_copy(p).wait_send()
        t_recv(p).wait_recv()
        return c

    def wait_d(j, c):
        p = (d + j) % nd
        w_copy(p).wait_send()
        w_recv(p).wait_recv()
        return c

    lax.fori_loop(1, nt, wait_t, 0)
    lax.fori_loop(1, nd, wait_d, 0)
    c0.wait()
    c1.wait()

    per = nt // nd
    acc = None
    for q in range(nt):
        part = jnp.dot(tbuf[q], wbuf[q // per, pl.ds((q % per) * rb, rb), :],
                       preferred_element_type=jnp.float32)
        acc = part if acc is None else acc + part
    xbuf[t] = acc.astype(xbuf.dtype)

    def x_copy(p):
        return pltpu.make_async_remote_copy(
            src_ref=xbuf.at[t], dst_ref=xbuf.at[t], send_sem=xs_sem.at[p], recv_sem=xr_sem.at[t],
            device_id=(d, p), device_id_type=MESH)

    def x_recv(p):
        return pltpu.make_async_remote_copy(
            src_ref=xbuf.at[p], dst_ref=xbuf.at[p], send_sem=xs_sem.at[p], recv_sem=xr_sem.at[p],
            device_id=(d, p), device_id_type=MESH)

    def send_x(j, c):
        x_copy((t + j) % nt).start()
        return c

    def wait_x(j, c):
        p = (t + j) % nt
        x_copy(p).wait_send()
        x_recv(p).wait_recv()
        return c

    lax.fori_loop(1, nt, send_x, 0)
    lax.fori_loop(1, nt, wait_x, 0)
    out_ref[...] = xbuf[...]


def _tw(tokens, wcol, nt, nd):
    tok, rb = tokens.shape
    rows, xw = wcol.shape
    return pl.pallas_call(
        functools.partial(_tw_kernel, nt, nd),
        out_shape=jax.ShapeDtypeStruct((nt, tok, xw), jnp.bfloat16),
        in_specs=[pl.BlockSpec(memory_space=pltpu.VMEM)] * 2,
        out_specs=pl.BlockSpec(memory_space=pltpu.VMEM),
        scratch_shapes=[
            pltpu.VMEM((nt, tok, rb), jnp.bfloat16),
            pltpu.VMEM((nd, rows, xw), jnp.bfloat16),
            pltpu.VMEM((nt, tok, xw), jnp.bfloat16),
            pltpu.SemaphoreType.DMA((nt,)),
            pltpu.SemaphoreType.DMA((nt,)),
            pltpu.SemaphoreType.DMA((nd,)),
            pltpu.SemaphoreType.DMA((nd,)),
            pltpu.SemaphoreType.DMA((nt,)),
            pltpu.SemaphoreType.DMA((nt,)),
            pltpu.SemaphoreType.DMA((2,)),
        ],
        compiler_params=pltpu.CompilerParams(
            collective_id=1, has_side_effects=True, vmem_limit_bytes=32 * 1024 * 1024),
        cost_estimate=pl.CostEstimate(
            flops=2 * tok * rb * nt * xw, transcendentals=0,
            bytes_accessed=(nt * tok * rb + nd * rows * xw + 2 * nt * tok * xw) * 2),
    )(tokens, wcol)


def on_device(tokens, small_weights, ffn_growth, width_growth):
    n_t = lax.axis_size("tensor")
    n_d = lax.axis_size("dp")
    t = lax.axis_index("tensor")
    rows, ds = width_growth.shape
    xw = ds // n_t
    blk = ds // n_d
    w_cols = lax.dynamic_slice_in_dim(width_growth, t * xw, xw, axis=1)
    tw_blocks = _tw(tokens, w_cols, n_t, n_d)
    s_rows = lax.all_gather(small_weights.transpose(1, 0, 2), "tensor", axis=0, tiled=True)
    panels = jnp.einsum(
        "smf,cf->msc", s_rows, ffn_growth, preferred_element_type=jnp.float32
    ).astype(jnp.bfloat16)
    hb = blk // 2
    w3h = width_growth.reshape(rows, n_d, 2, hb).transpose(1, 2, 0, 3)
    quarters = panels.reshape(4, hb, panels.shape[2])
    grown_weights, hidden = _dp_ring(quarters, w3h, tw_blocks)
    return (grown_weights, hidden)


def solution(mesh):
    placed = (P("dp", "tensor"), P(None, ("dp", "tensor"), None), P("tensor", None), P("dp", None))
    return jax.shard_map(
        on_device,
        mesh=mesh,
        in_specs=placed,
        out_specs=(P(None, "dp", "tensor"), P("dp", "tensor")),
        check_vma=False,
    )
```
